32 devices in a mesh: gx: 4 (over y, x), gy: 8 (over z, core).
Axes of the slice: x: 2, y: 2, z: 4, core: 2. Of those that a mesh axis runs over, the one named last changes fastest.
Arguments:
- node_shift: float32 [2, 256, 4096], P(None, 'gx', 'gy'), may hold values from -1.5 to 1.5
- node_speed: float32 [2, 256, 4096], P(None, 'gx', 'gy'), may hold values from -4 to 4
- damage_initial: int32 [2, 256, 4096], P(None, 'gx', 'gy'), may hold values from 0 to 7
- cohesive_markers: int32 [32, 8], P('gx', 'gy'), may hold values from 0 to 1, as said below
- cell_warmth: float32 [128, 2048], P(('gx', 'gy')), may hold values from 0 to 1
- heat_storage: float32 [128, 2048], P(('gx', 'gy')), may hold values from 0.5 to 2
- surface_transfer: float32 [128, 2048], P(('gx', 'gy')), may hold values from 0.1 to 1
- quench_liquid_heat: float32 [128, 2048], P(('gx', 'gy')), may hold values from 0 to 0.3
Outputs:
- displace_new: float32 [2, 256, 4096], P(None, 'gx', 'gy')
- velocity_new: float32 [2, 256, 4096], P(None, 'gx', 'gy')
- damage: bfloat16 [2, 256, 4096], P(None, 'gx', 'gy')
- warmth_after_solve: float32 [128, 2048], P(('gx', 'gy'))
The draws below stay inside these ranges and needn't reach their ends.
Inputs may be any that keep to these rules, and one draw needn't show every extreme that they name: `cohesive_markers`: within each column, every block of 8 consecutive tile rows starting at a multiple of 8 holds between 1 and 4 ones, and in every draw some block holds exactly 4.
All inputs are finite; a program needn't handle non-finite values.
Results may differ from the reference program's by a relative error of at most 0.001.
Values sent between devices are 32-bit elements; how exact they have to be, the bound alone decides.
A program may use at most 64 MiB of HBM per device.

```python
import math
import jax
import jax.numpy as jnp
from jax import lax

FX = 64
FY = 512
SR = 8
SEG = 128
SUBSTEPS = 8
ITERS = 4
NXF = 256
NYF = 4096
CELL_HEIGHT_NUM = 128
CELL_WIDTH_NUM = 2048
STRIPS = 8
MOST = 4
N_GX = 4
N_GY = 8


def marker_grid(key):
    block_total = NXF // FX * N_GY
    key_count, key_force, key_order = jax.random.split(jax.random.fold_in(key, 11), 3)
    counts = jax.random.randint(key_count, (block_total,), 1, MOST + 1)
    forced = jax.random.randint(key_force, (), 0, block_total)
    counts = jnp.where(jnp.arange(block_total) == forced, MOST, counts)
    orders = jax.vmap(lambda subkey: jax.random.permutation(subkey, STRIPS))(jax.random.split(key_order, block_total))
    marking = (orders < counts[:, None]).astype(jnp.int32)
    grid_marks = marking.reshape(NXF // FX, N_GY, STRIPS)
    return jnp.transpose(grid_marks, (0, 2, 1)).reshape(NXF // SR, N_GY)


def draw_cohesive_markers(key, part):
    return marker_grid(key)


def draw_damage_initial(key, part):
    key_level, key_keep = jax.random.split(jax.random.fold_in(key, 23))
    levels = jax.random.randint(key_level, (2, NXF, NYF), 0, 8)
    keeping = jax.random.randint(key_keep, (2, NXF, NYF), 0, 4)
    return jnp.where(keeping == 0, levels, 0).astype(jnp.int32)


def draw_node_speed(key, part):
    key_phase, key_rough = jax.random.split(jax.random.fold_in(key, 31))
    phases = jax.random.uniform(key_phase, (4,), jnp.float32)
    rows = jnp.arange(NXF, dtype=jnp.float32)[:, None]
    cols = jnp.arange(NYF, dtype=jnp.float32)[None, :]
    two_pi = 2.0 * math.pi
    amplitude = 1.6
    rough = jnp.clip(0.25 * jax.random.normal(key_rough, (2, NXF, NYF), jnp.float32), -1.0, 1.0)
    along_rows = amplitude * jnp.sin(two_pi * (rows / 32.0 + phases[0])) * (1.0 + 0.5 * jnp.sin(two_pi * (cols / 64.0 + phases[1])))
    along_cols = amplitude * jnp.sin(two_pi * (cols / 32.0 + phases[2])) * (1.0 + 0.5 * jnp.sin(two_pi * (rows / 64.0 + phases[3])))
    return (jnp.stack([along_rows, along_cols]) + rough).astype(jnp.float32)


def draw_heat_storage(key, part):
    marks = marker_grid(key)
    row_tile = 2 * jnp.arange(CELL_HEIGHT_NUM, dtype=jnp.int32) // SR
    col_tile = 2 * jnp.arange(CELL_WIDTH_NUM, dtype=jnp.int32) // FY
    coarse_marks = marks[row_tile][:, col_tile]
    fraction = jax.random.uniform(jax.random.fold_in(key, 41), (CELL_HEIGHT_NUM, CELL_WIDTH_NUM), jnp.float32)
    lower = jnp.where(coarse_marks == 1, math.log(0.5), math.log(1.25))
    upper = jnp.where(coarse_marks == 1, math.log(1.0), math.log(2.0))
    return jnp.exp(lower + (upper - lower) * fraction).astype(jnp.float32)


def shard_levels(stream_key, shape, cuts, smallest, largest):
    gain = 1.0
    for dim, blocks in cuts:
        steps = jax.random.uniform(jax.random.fold_in(jax.random.fold_in(stream_key, 6), dim), (blocks,), jnp.float32, smallest / len(cuts), largest / len(cuts))
        gain = gain * jnp.repeat(jnp.exp(steps), shape[dim] // blocks).reshape((-1,) + (1,) * (len(shape) - 1 - dim))
    return gain


def bell_draw(own_key, extent, width, most, cuts=(), held_as=jnp.bfloat16):
    result = width * jax.random.normal(own_key, extent, jnp.float32)
    if cuts:
        result = result * shard_levels(own_key, extent, cuts, -0.22, 0.18)
    return jnp.clip(result, -most, most).astype(held_as)


def setup_inputs(seed: int = 0) -> dict:
    key_of = jax.random.split(jax.random.key(seed), 9)
    node_shift = bell_draw(key_of[0], (2, NXF, NYF), 0.1, 1.5, ((1, 4), (2, 8)), jnp.float32)
    node_speed = draw_node_speed(jax.random.fold_in(key_of[8], 71), 0)
    damage_initial = draw_damage_initial(jax.random.fold_in(key_of[8], 71), 0)
    cohesive_markers = draw_cohesive_markers(jax.random.fold_in(key_of[8], 71), 0)
    cell_warmth = jnp.clip(1.0 * jax.random.uniform(key_of[4], (CELL_HEIGHT_NUM, CELL_WIDTH_NUM), jnp.float32) ** shard_levels(key_of[4], (CELL_HEIGHT_NUM, CELL_WIDTH_NUM), ((0, 32),), -0.2, 0.2), 0.0, 1.0)
    heat_storage = draw_heat_storage(jax.random.fold_in(key_of[8], 71), 0)
    surface_transfer = jnp.clip(0.1 + 0.9 * jax.random.uniform(key_of[6], (CELL_HEIGHT_NUM, CELL_WIDTH_NUM), jnp.float32) ** shard_levels(key_of[6], (CELL_HEIGHT_NUM, CELL_WIDTH_NUM), ((0, 32),), -0.2, 0.2), 0.1, 1.0)
    quench_liquid_heat = jnp.clip(0.3 * jax.random.uniform(key_of[7], (CELL_HEIGHT_NUM, CELL_WIDTH_NUM), jnp.float32) ** shard_levels(key_of[7], (CELL_HEIGHT_NUM, CELL_WIDTH_NUM), ((0, 32),), -0.2, 0.2), 0.0, 0.3)
    return dict(node_shift=node_shift, node_speed=node_speed, damage_initial=damage_initial, cohesive_markers=cohesive_markers, cell_warmth=cell_warmth, heat_storage=heat_storage, surface_transfer=surface_transfer, quench_liquid_heat=quench_liquid_heat)


STIFFNESS = 1.0
EXPANSION = 0.6
SOFTENING_SCALE = 0.25
TIME_STEP = 0.4
DAMPING = 0.05
HEAT_INCREMENT = 1.0
GAP_GAIN = 0.5


def softening(opening):
    stretch = jnp.maximum(opening, 0.0)
    return 1.0 - jnp.exp(-stretch * stretch / SOFTENING_SCALE)


def edge_masks(row_first, col_first, height_number_all, width_number, total_rows, total_cols):
    row_index = row_first + jnp.arange(height_number_all, dtype=jnp.int32)
    col_index = col_first + jnp.arange(width_number, dtype=jnp.int32)
    in_rows = (row_index >= 0) & (row_index < total_rows)
    in_cols = (col_index >= 0) & (col_index < total_cols)
    present_horizontal = ((row_index >= 1) & (row_index < total_rows))[:, None] & in_cols[None, :]
    present_vertical = in_rows[:, None] & ((col_index >= 1) & (col_index < total_cols))[None, :]
    return present_horizontal.astype(jnp.float32), present_vertical.astype(jnp.float32)


def march_forward(state_tensors, dense_mesh_heat, present_horizontal, present_vertical):
    disp_x, disp_y, vel_x, vel_y, dam_x, dam_y, weight = [state_tensors[number] for number in range(7)]
    average_horizontal = 0.5 * (dense_mesh_heat[1:, :] + dense_mesh_heat[:-1, :])
    open_x = disp_x[1:, :] - disp_x[:-1, :] - EXPANSION * average_horizontal
    shear_x = disp_y[1:, :] - disp_y[:-1, :]
    new_dx = jnp.maximum(dam_x[1:, :], softening(open_x) * weight[1:, :] * present_horizontal[1:, :])
    spring_x = STIFFNESS * (1.0 - new_dx) * present_horizontal[1:, :]
    normal_x = spring_x * open_x
    along_x = spring_x * shear_x
    average_vertical = 0.5 * (dense_mesh_heat[:, 1:] + dense_mesh_heat[:, :-1])
    open_y = disp_y[:, 1:] - disp_y[:, :-1] - EXPANSION * average_vertical
    shear_y = disp_x[:, 1:] - disp_x[:, :-1]
    new_dy = jnp.maximum(dam_y[:, 1:], softening(open_y) * weight[:, 1:] * present_vertical[:, 1:])
    spring_y = STIFFNESS * (1.0 - new_dy) * present_vertical[:, 1:]
    normal_y = spring_y * open_y
    along_y = spring_y * shear_y
    force_x = (normal_x[1:, 1:-1] - normal_x[:-1, 1:-1]) + (along_y[1:-1, 1:] - along_y[1:-1, :-1])
    force_y = (along_x[1:, 1:-1] - along_x[:-1, 1:-1]) + (normal_y[1:-1, 1:] - normal_y[1:-1, :-1])
    inner_vx = vel_x[1:-1, 1:-1]
    inner_vy = vel_y[1:-1, 1:-1]
    next_vx = inner_vx + TIME_STEP * (force_x - DAMPING * inner_vx)
    next_vy = inner_vy + TIME_STEP * (force_y - DAMPING * inner_vy)
    next_ux = disp_x[1:-1, 1:-1] + TIME_STEP * next_vx
    next_uy = disp_y[1:-1, 1:-1] + TIME_STEP * next_vy
    return jnp.stack([next_ux, next_uy, next_vx, next_vy, new_dx[:-1, 1:-1], new_dy[1:-1, :-1], weight[1:-1, 1:-1]])


def widen_upward(padded):
    middle = padded[1:-1]
    even_rows = 0.75 * middle + 0.25 * padded[:-2]
    odd_rows = 0.75 * middle + 0.25 * padded[2:]
    return jnp.stack([even_rows, odd_rows], axis=1).reshape(2 * middle.shape[0], padded.shape[1])


def widen_sideways(padded):
    middle = padded[:, 1:-1]
    even_cols = 0.75 * middle + 0.25 * padded[:, :-2]
    odd_cols = 0.75 * middle + 0.25 * padded[:, 2:]
    return jnp.stack([even_cols, odd_cols], axis=2).reshape(padded.shape[0], 2 * middle.shape[1])


def kernel_table():
    position = jnp.arange(SEG, dtype=jnp.float32)
    return jnp.exp(-4.0 * jnp.abs(position[:, None] - position[None, :]) / SEG) * (2.0 / SEG)


def radiate(values):
    flattened = values.reshape(-1, SEG)
    product = jnp.dot(flattened, kernel_table(), precision=lax.Precision.HIGHEST, preferred_element_type=jnp.float32)
    return product.reshape(values.shape)


def sweep_plate(state_tensors, dense_margin, mask_x, mask_y):
    padded = jnp.pad(state_tensors, ((0, 0), (1, 1), (1, 1)))

    def one_block(block_index):
        first_row = (block_index * FX).astype(jnp.int32)
        piece_rows = lax.dynamic_slice_in_dim(padded, first_row, FX + 2, 1)
        warmth_lines = lax.dynamic_slice_in_dim(dense_margin, first_row, FX + 2, 0)
        rows_x = lax.dynamic_slice_in_dim(mask_x, first_row, FX + 2, 0)
        rows_y = lax.dynamic_slice_in_dim(mask_y, first_row, FX + 2, 0)
        return march_forward(piece_rows, warmth_lines, rows_x, rows_y)

    blocks = lax.map(one_block, jnp.arange(N_GX, dtype=jnp.int32))
    return jnp.moveaxis(blocks, 0, 1).reshape(7, NXF, NYF)


def heat_baseline_check(cell_warmth, heat_storage, surface_transfer, quench_liquid_heat, thermal_impedance):
    heat_conductance = (1.0 + 0.5 * cell_warmth) / (1.0 + thermal_impedance)
    padded_cond = jnp.pad(heat_conductance, 1)
    row_index = jnp.arange(CELL_HEIGHT_NUM, dtype=jnp.int32)[:, None]
    col_index = jnp.arange(CELL_WIDTH_NUM, dtype=jnp.int32)[None, :]
    cond_down = 0.5 * (heat_conductance + padded_cond[:-2, 1:-1]) * (row_index >= 1).astype(jnp.float32)
    cond_up = 0.5 * (heat_conductance + padded_cond[2:, 1:-1]) * (row_index <= CELL_HEIGHT_NUM - 2).astype(jnp.float32)
    cond_left = 0.5 * (heat_conductance + padded_cond[1:-1, :-2]) * (col_index >= 1).astype(jnp.float32)
    cond_right = 0.5 * (heat_conductance + padded_cond[1:-1, 2:]) * (col_index <= CELL_WIDTH_NUM - 2).astype(jnp.float32)
    offsum = cond_down + cond_up + cond_left + cond_right
    diagonal = (heat_storage / HEAT_INCREMENT + surface_transfer) + offsum
    off_ratio = offsum / diagonal
    bound_low = jnp.min(1.0 - off_ratio)
    bound_high = jnp.max(1.0 + off_ratio)

    def laplace_action(field):
        padded = jnp.pad(field, 1)
        return diagonal * field - (cond_down * padded[:-2, 1:-1] + cond_up * padded[2:, 1:-1]
                                   + cond_left * padded[1:-1, :-2] + cond_right * padded[1:-1, 2:])

    center = 0.5 * (bound_high + bound_low)
    spread = 0.5 * (bound_high - bound_low)
    sigma_ratio = center / spread
    rho_now = 1.0 / sigma_ratio
    forcing_entries = heat_storage / HEAT_INCREMENT * cell_warmth + surface_transfer * quench_liquid_heat
    misfit_norm = forcing_entries - laplace_action(cell_warmth)
    direction = misfit_norm / diagonal / center
    answer_state = cell_warmth
    for iteration in range(ITERS):
        answer_state = answer_state + direction
        if iteration + 1 < ITERS:
            misfit_norm = misfit_norm - laplace_action(direction)
            rho_next = 1.0 / (2.0 * sigma_ratio - rho_now)
            direction = rho_next * rho_now * direction + (2.0 * rho_next / spread) * (misfit_norm / diagonal)
            rho_now = rho_next
    return answer_state


def reference(node_shift, node_speed, damage_initial, cohesive_markers, cell_warmth, heat_storage, surface_transfer, quench_liquid_heat):
    weight = jnp.repeat(jnp.repeat(cohesive_markers, SR, axis=0), FY, axis=1).astype(jnp.float32)
    present_horizontal, present_vertical = edge_masks(0, 0, NXF, NYF, NXF, NYF)
    start_damage = damage_initial.astype(jnp.float32) * 0.125 * weight[None]
    state_tensors = jnp.stack([node_shift[0], node_shift[1], node_speed[0], node_speed[1],
                        start_damage[0] * present_horizontal, start_damage[1] * present_vertical, weight])
    dense_mesh_heat = widen_sideways(widen_upward(jnp.pad(cell_warmth, 1, mode="edge")))
    dense_margin = jnp.pad(dense_mesh_heat, 1)
    mask_x, mask_y = edge_masks(-1, -1, NXF + 2, NYF + 2, NXF, NYF)
    for substep in range(SUBSTEPS):
        state_tensors = sweep_plate(state_tensors, dense_margin, mask_x, mask_y)
    gap_sum = state_tensors[4] + state_tensors[5]
    glowing = radiate(gap_sum)
    thermal_impedance = GAP_GAIN * glowing.reshape(CELL_HEIGHT_NUM, 2, CELL_WIDTH_NUM, 2).sum(axis=(1, 3))
    warmth_after_solve = heat_baseline_check(cell_warmth, heat_storage, surface_transfer, quench_liquid_heat, thermal_impedance)
    return state_tensors[0:2], state_tensors[2:4], state_tensors[4:6].astype(jnp.bfloat16), warmth_after_solve
```

```python
import functools

import jax
import jax.numpy as jnp
from jax import lax
from jax.experimental import pallas as pl
from jax.experimental.pallas import tpu as pltpu
from jax.sharding import PartitionSpec as P

SR = 8
SEG = 128
SUBSTEPS = 8
HALO = 8
MESH = pl.DeviceIdType.MESH
F32 = jnp.float32


def lane_iota(shape):
    return lax.broadcasted_iota(jnp.int32, shape, 1)


def row_iota(shape):
    return lax.broadcasted_iota(jnp.int32, shape, 0)


def full_dot(a, b):
    return jnp.dot(a, b, precision=lax.Precision.HIGHEST, preferred_element_type=F32)


def kernel(
    n_gx,
    n_gy,
    shift,
    speed,
    level_h,
    mark_h,
    warm_h,
    store_h,
    film_h,
    bath_h,
    o_shift,
    o_speed,
    o_dam,
    o_warm,
    tsend,
    trecv,
    asend,
    arecv,
    pk_l,
    pk_r,
    rk_l,
    rk_r,
    wsend,
    wrecv,
    rowsend,
    rowrecv,
    keep,
    hist,
    level,
    warm,
    store,
    film,
    bath,
    state,
    wt,
    tx,
    ty,
    tc,
    acf,
    widebuf,
    gap,
    cbuf,
    crow,
    ccl,
    ccr,
    zsend,
    zrecv,
    msend,
    mrecv,
    nb_send,
    nb_recv,
    t_sem,
    a_sem,
    c_send,
    c_recv,
    z_sem,
    m_sem,
    in_sem,
    mark,
):
    ndev = n_gx * n_gy
    gx = lax.axis_index("gx")
    gy = lax.axis_index("gy")
    me = gx * n_gy + gy
    _, hh, ww = shift.shape
    rpd, _ = warm_h.shape
    cw = ww // 2
    ch = hh // 2
    hb = HALO // rpd
    nsl = n_gy + 2 * hb
    up = lax.rem(gx + n_gx - 1, n_gx)
    down = lax.rem(gx + 1, n_gx)
    left = lax.rem(gy + n_gy - 1, n_gy)
    right = lax.rem(gy + 1, n_gy)

    barrier = pltpu.get_barrier_semaphore()

    def greet(k, c):
        t = lax.rem(me + k, ndev)
        pl.semaphore_signal(barrier, inc=1, device_id=(t // n_gy, t % n_gy), device_id_type=MESH)
        return c

    lax.fori_loop(1, ndev, greet, 0)

    own_r = slice(HALO, HALO + hh)
    loads = [
        pltpu.make_async_copy(src, dst, in_sem.at[i])
        for i, (src, dst) in enumerate(
            (
                (warm_h, warm),
                (level_h, level),
                (shift, state.at[0:2, own_r, 0:ww]),
                (speed, state.at[2:4, own_r, 0:ww]),
                (store_h, store),
                (film_h, film),
                (bath_h, bath),
                (mark_h, mark),
            )
        )
    ]
    for copy in loads:
        copy.start()

    lane = lane_iota((hh, 128))
    loads[7].wait()
    for s in range(hh // SR):
        wt[HALO + SR * s : HALO + SR * s + SR, 0:ww] = jnp.full((SR, ww), mark[0, s], jnp.int32).astype(F32)
    w_own = wt[own_r, 0:ww]
    grow = gx * hh + row_iota((hh, ww))
    gcol = gy * ww + lane_iota((hh, ww))
    loads[1].wait()
    state[4, own_r, 0:ww] = jnp.where(grow >= 1, level[0].astype(F32) * 0.125 * w_own, 1.0)
    state[5, own_r, 0:ww] = jnp.where(gcol >= 1, level[1].astype(F32) * 0.125 * w_own, 1.0)
    wsend[0] = wt[HALO : HALO + 8, 0:128]
    wsend[1] = wt[HALO + hh - 8 : HALO + hh, 0:128]
    loads[2].wait()
    loads[3].wait()
    acc_l = jnp.zeros((hh, 128), F32)
    acc_r = jnp.zeros((hh, 128), F32)
    for f in range(7):
        field = state.at[f] if f < 6 else wt
        first, last = field[own_r, 0:128], field[own_r, ww - 128 : ww]
        here = (lane >= 8 * f) & (lane < 8 * f + 8)
        first = pltpu.roll(first, 8 * f, 1) if f else first
        acc_l = jnp.where(here, first, acc_l)
        acc_r = jnp.where(here, pltpu.roll(last, 8 * f + 8, 1), acc_r)
        if f < 6:
            rowsend[0, f] = field[HALO : HALO + 8, 0:ww]
            rowsend[1, f] = field[HALO + hh - 8 : HALO + hh, 0:ww]
    pk_l[...] = acc_l
    pk_r[...] = acc_r

    lane_c = lane_iota((rpd, 128))

    def chunk(value, k):
        after = value[:, (cw * (k + 1)) % (cw * n_gy) :][:, 0:128]
        before = value[:, (cw * k - 128) % (cw * n_gy) :][:, 0:128]
        return value[:, cw * k : cw * k + cw], jnp.where(lane_c < 64, after, before)

    for i in (0, 4, 5, 6):
        loads[i].wait()
    t_own = warm[...]
    base = store[...] + film[...]
    force_own = store[...] * t_own + film[...] * bath[...]
    for k in range(n_gy):
        main, edge = chunk(t_own, k)
        tsend[k, :, 0:cw] = main
        tsend[k, :, cw : cw + 128] = edge
        for q, val in enumerate((base, force_own)):
            main, edge = chunk(val, k)
            asend[k, q, :, 0:cw] = main
            asend[k, q, :, cw : cw + 128] = edge

    pl.semaphore_wait(barrier, ndev - 1)

    def remote(src, dst, ssem, rsem, where):
        return pltpu.make_async_remote_copy(
            src_ref=src, dst_ref=dst, send_sem=ssem, recv_sem=rsem, device_id=where,
            device_id_type=MESH,
        )

    def neighbours(send_l, send_r, row_u, row_d, recv_l, recv_r, got_u, got_d, rows, ssem, rsem):
        top, end = slice(0, 8), slice(rows - 8, rows)
        lo, mid, hi = slice(0, 8), slice(8, rows + 8), slice(rows + 8, rows + 16)
        return [
            remote(row_u, got_d, ssem.at[0], rsem.at[0], (up, gy)),
            remote(row_d, got_u, ssem.at[1], rsem.at[1], (down, gy)),
            remote(send_l, recv_r.at[mid], ssem.at[2], rsem.at[2], (gx, left)),
            remote(send_r, recv_l.at[mid], ssem.at[3], rsem.at[3], (gx, right)),
            remote(send_l.at[top], recv_r.at[hi], ssem.at[4], rsem.at[4], (up, left)),
            remote(send_r.at[top], recv_l.at[hi], ssem.at[5], rsem.at[5], (up, right)),
            remote(send_l.at[end], recv_r.at[lo], ssem.at[6], rsem.at[6], (down, left)),
            remote(send_r.at[end], recv_l.at[lo], ssem.at[7], rsem.at[7], (down, right)),
        ]

    first = neighbours(
        pk_l,
        pk_r,
        rowsend.at[0],
        rowsend.at[1],
        rk_l,
        rk_r,
        rowrecv.at[0],
        rowrecv.at[1],
        hh,
        nb_send,
        nb_recv,
    ) + [
        remote(wsend.at[0], wrecv.at[1], nb_send.at[8], nb_recv.at[8], (up, gy)),
        remote(wsend.at[1], wrecv.at[0], nb_send.at[9], nb_recv.at[9], (down, gy)),
    ]

    def spread_out(send, recv, sem):
        def along(k, c):
            t = lax.rem(gy + k, n_gy)
            remote(send.at[t], recv.at[gy + hb], sem.at[1], sem.at[0], (gx, t)).start()
            return c

        lax.fori_loop(1, n_gy, along, 0)
        pltpu.make_async_copy(send.at[gy], recv.at[gy + hb], sem.at[0]).start()

        @pl.when(gy < hb)
        def _():
            def go(k, c):
                remote(
                    send.at[k], recv.at[gy + hb + n_gy], sem.at[2], sem.at[0], (up, k)
                ).start()
                return c

            lax.fori_loop(0, n_gy, go, 0)

        @pl.when(gy >= n_gy - hb)
        def _():
            def go(k, c):
                remote(
                    send.at[k], recv.at[gy - (n_gy - hb)], sem.at[3], sem.at[0], (down, k)
                ).start()
                return c

            lax.fori_loop(0, n_gy, go, 0)

    def spread_sent(send, recv, sem):
        part = pl.ds(0, n_gy - 1)
        remote(send.at[part], recv.at[part], sem.at[1], sem.at[0], (gx, right)).wait_send()
        whole = pl.ds(0, n_gy)

        @pl.when(gy < hb)
        def _():
            remote(send, recv.at[whole], sem.at[2], sem.at[0], (up, gy)).wait_send()

        @pl.when(gy >= n_gy - hb)
        def _():
            remote(send, recv.at[whole], sem.at[3], sem.at[0], (down, gy)).wait_send()

    spread_out(tsend, trecv, t_sem)
    for copy in first[2:8] + first[8:10] + first[0:2]:
        copy.start()

    pltpu.make_async_copy(trecv, trecv, t_sem.at[0]).wait()

    def late(k, c):
        t = lax.rem(gy + k, n_gy)
        remote(asend.at[t], arecv.at[gy], a_sem.at[1], a_sem.at[0], (gx, t)).start()
        return c

    lax.fori_loop(1, n_gy, late, 0)
    pltpu.make_async_copy(asend.at[gy], arecv.at[gy], a_sem.at[0]).start()
    crows = ch + 16
    for k in range(nsl):
        tc[rpd * k : rpd * k + rpd, :] = trecv[k]
    cshape = (crows, cw + 128)
    crow_i, clane_i = row_iota(cshape), lane_iota(cshape)
    t_all = tc[...]
    p = t_all
    p = jnp.where((gx == 0) & (crow_i < 8), t_all[8:9, :], p)
    p = jnp.where((gx == n_gx - 1) & (crow_i >= ch + 8), t_all[ch + 7 : ch + 8, :], p)
    wide = cw + 128
    q = jnp.where((gy == 0) & (clane_i == wide - 1), pltpu.roll(p, wide - 1, 1), p)
    q = jnp.where((gy == n_gy - 1) & (clane_i == cw), pltpu.roll(p, 1, 1), q)
    even = 0.75 * q + 0.25 * pltpu.roll(q, 1, 0)
    odd = 0.75 * q + 0.25 * pltpu.roll(q, crows - 1, 0)
    frows = hh + 2 * HALO
    need = frows // 2
    ntile = wide // 128
    for t in range(ntile):
        cols = slice(128 * t, 128 * t + 128)
        widebuf[t, pl.ds(0, need, stride=2), :] = even[4 : 4 + need, cols]
        widebuf[t, pl.ds(1, need, stride=2), :] = odd[4 : 4 + need, cols]
    r = jnp.concatenate([widebuf[t] for t in range(ntile)], axis=1)
    ecol = 0.75 * r + 0.25 * pltpu.roll(r, 1, 1)
    ocol = 0.75 * r + 0.25 * pltpu.roll(r, wide - 1, 1)
    k_i, n_i = row_iota((256, 256)), lane_iota((256, 256))
    weave = (n_i == jnp.where(k_i < 128, 2 * k_i, 2 * k_i - 255)).astype(F32)
    stack = jnp.concatenate(
        [
            jnp.concatenate([ecol[:, 128 * t : 128 * t + 128], ocol[:, 128 * t : 128 * t + 128]], 1)
            for t in range(ntile)
        ],
        axis=0,
    )
    woven = full_dot(stack, weave)
    lane_f = lane_iota((frows, 128))
    pieces = [woven[frows * t : frows * t + frows] for t in range(ntile)]
    edge = jnp.where(lane_f < 64, pieces[-1][:, 0:128], pieces[-1][:, 128:256])
    fine = jnp.concatenate(pieces[:-1] + [edge], axis=1)
    fwide = ww + 128
    tx[...] = 0.6 * (0.5 * (fine + pltpu.roll(fine, 1, 0)))
    ty[...] = 0.6 * (0.5 * (fine + pltpu.roll(fine, 1, 1)))

    for copy in first[2:8]:
        copy.wait_recv()
    got_l, got_r = rk_l[...], rk_r[...]
    for f in range(7):
        from_r = pltpu.roll(got_r, 128 - 8 * f, 1) if f else got_r
        from_l = pltpu.roll(got_l, 120 - 8 * f, 1)
        side = jnp.where(lane_f < 8, from_r, jnp.where(lane_f >= 120, from_l, 0.0))
        if f == 5:
            off_l = (gy == 0) & (lane_f >= 64)
            off_r = (gy == n_gy - 1) & (lane_f < 64)
            side = jnp.where(off_l | off_r, 1.0, side)
        target = state.at[f] if f < 6 else wt
        target[:, ww:fwide] = side
    sub = row_iota((8, fwide))
    last_strip = frows // 8 - 1

    def edges(s, old):
        rows = slice(8 * s, 8 * s + 8)
        u0, u1 = state[0, rows, :], state[1, rows, :]
        w = wt[rows, :]
        r0, r1 = pltpu.roll(u0, 1, 0), pltpu.roll(u1, 1, 0)
        p0 = jnp.where(sub == 0, old["r0"], r0) if old else r0
        p1 = jnp.where(sub == 0, old["r1"], r1) if old else r1
        open_x = u0 - p0 - tx[rows, :]
        st = jnp.maximum(open_x, 0.0)
        dx = jnp.maximum(state[4, rows, :], (1.0 - jnp.exp(st * st * -4.0)) * w)
        state[4, rows, :] = dx
        sp = 1.0 - dx
        nx = sp * open_x
        ax = sp * (u1 - p1)
        open_y = u1 - pltpu.roll(u1, 1, 1) - ty[rows, :]
        st = jnp.maximum(open_y, 0.0)
        dy = jnp.maximum(state[5, rows, :], (1.0 - jnp.exp(st * st * -4.0)) * w)
        state[5, rows, :] = dy
        sp = 1.0 - dy
        ny = sp * open_y
        ay = sp * (u0 - pltpu.roll(u0, 1, 1))
        return dict(
            r0=r0, r1=r1, nx=nx, ax=ax, u0=u0, u1=u1,
            sx=pltpu.roll(nx, 7, 0), sa=pltpu.roll(ax, 7, 0),
            fy0=pltpu.roll(ay, fwide - 1, 1) - ay,
            fy1=pltpu.roll(ny, fwide - 1, 1) - ny,
        )

    def advance(s, old, new):
        rows = slice(8 * s, 8 * s + 8)
        nn = jnp.where(sub == 7, new["sx"], old["sx"])
        na = jnp.where(sub == 7, new["sa"], old["sa"])
        f0 = (nn - old["nx"]) + old["fy0"]
        f1 = (na - old["ax"]) + old["fy1"]
        v0, v1 = state[2, rows, :], state[3, rows, :]
        v0 = v0 + 0.4 * (f0 - 0.05 * v0)
        v1 = v1 + 0.4 * (f1 - 0.05 * v1)
        state[2, rows, :] = v0
        state[3, rows, :] = v1
        state[0, rows, :] = old["u0"] + 0.4 * v0
        state[1, rows, :] = old["u1"] + 0.4 * v1

    redo = (slice(8, 16), slice(8 * last_strip - 8, 8 * last_strip))
    for i, rows in enumerate(redo):
        keep[i] = state[:, rows, :]

    def interior(t, c):
        old = None
        for s in range(1, last_strip):
            new = edges(s, old)
            if s == 2:
                hist[t, 0] = new["sx"]
                hist[t, 1] = new["sa"]
            if s == last_strip - 2:
                hist[t, 2] = new["r0"]
                hist[t, 3] = new["r1"]
            if old:
                advance(s - 1, old, new)
            old = new
        advance(last_strip - 1, old, old)
        return c

    lax.fori_loop(0, SUBSTEPS, interior, 0)

    pltpu.make_async_copy(arecv, arecv, a_sem.at[0]).wait()
    for k in range(n_gy):
        for q in range(2):
            acf[q, 8 + rpd * k : 8 + rpd * k + rpd, :] = arecv[k, q]
    coarse_rows = [
        remote(
            acf.at[:, 8:16], acf.at[:, ch + 8 : ch + 16], a_sem.at[2], a_sem.at[4], (up, gy)
        ),
        remote(acf.at[:, ch : ch + 8], acf.at[:, 0:8], a_sem.at[3], a_sem.at[5], (down, gy)),
    ]
    for copy in coarse_rows:
        copy.start()

    for copy in first[0:2] + first[8:10]:
        copy.wait_recv()
    for i, rows in enumerate(redo):
        state[:, rows, :] = keep[i]
    for side_row, at in ((0, 0), (1, hh + HALO)):
        state[:, at : at + 8, 0:ww] = rowrecv[side_row]
        for t in range(ww // 128):
            wt[at : at + 8, 128 * t : 128 * t + 128] = wrecv[side_row]

    @pl.when(gx == 0)
    def _():
        state[4, 0:8, :] = jnp.ones((8, fwide), F32)

    @pl.when(gx == n_gx - 1)
    def _():
        state[4, hh + HALO : hh + HALO + 8, :] = jnp.ones((8, fwide), F32)

    def border(t, c):
        e0 = edges(0, None)
        e1 = edges(1, e0)
        advance(0, e0, e1)
        advance(1, e1, dict(sx=hist[t, 0], sa=hist[t, 1]))
        e8 = edges(last_strip - 1, dict(r0=hist[t, 2], r1=hist[t, 3]))
        e9 = edges(last_strip, e8)
        advance(last_strip - 1, e8, e9)
        advance(last_strip, e9, e9)
        return c

    lax.fori_loop(0, SUBSTEPS, border, 0)

    dam_x = jnp.where(grow >= 1, state[4, own_r, 0:ww], 0.0)
    dam_y = jnp.where(gcol >= 1, state[5, own_r, 0:ww], 0.0)
    both = dam_x + dam_y
    for t in range(ww // 128):
        gap[t] = both[:, 128 * t : 128 * t + 128]
    rows2 = jnp.concatenate(
        [
            gap[t, pl.ds(0, ch, stride=2), :] + gap[t, pl.ds(1, ch, stride=2), :]
            for t in range(ww // 128)
        ],
        axis=1,
    )
    k_i, n_i = row_iota((256, 128)), lane_iota((256, 128))
    pos = (k_i % SEG).astype(F32)
    col = (2 * (n_i % 64)).astype(F32)
    tab = jnp.exp(jnp.abs(pos - col) * (-4.0 / SEG)) + jnp.exp(jnp.abs(pos - col - 1.0) * (-4.0 / SEG))
    tab = jnp.where(k_i // SEG == n_i // 64, tab * (1.0 / SEG), 0.0)
    npair = ww // 256
    glow = full_dot(
        jnp.concatenate([rows2[:, 256 * t : 256 * t + 256] for t in range(npair)], axis=0), tab
    )
    resist = jnp.concatenate([glow[ch * t : ch * t + ch] for t in range(npair)], axis=1)
    cond_own = (1.0 + 0.5 * tc[8 : 8 + ch, 0:cw]) / (1.0 + resist)
    cbuf[...] = cond_own
    second = neighbours(
        cbuf.at[:, 0:128], cbuf.at[:, cw - 128 : cw], cbuf.at[0:8], cbuf.at[ch - 8 : ch],
        ccl, ccr, crow.at[0], crow.at[1], ch, c_send, c_recv,
    )
    for copy in second:
        copy.start()

    o_dam[0] = dam_x.astype(jnp.bfloat16)
    o_dam[1] = dam_y.astype(jnp.bfloat16)
    o_shift[...] = state[0:2, own_r, 0:ww]
    o_speed[...] = state[2:4, own_r, 0:ww]

    for copy in coarse_rows:
        copy.wait_recv()

    for copy in second:
        copy.wait_recv()
    lane_k = lane_iota((crows, 128))
    cond = jnp.concatenate(
        [
            jnp.concatenate([crow[0], cbuf[...], crow[1]], axis=0),
            jnp.where(lane_k < 64, ccr[...], ccl[...]),
        ],
        axis=1,
    )
    crow_g = gx * ch - 8 + crow_i
    ccol_g = gy * cw + jnp.where(clane_i < cw + 64, clane_i, clane_i - wide)

    def four(x):
        return (
            pltpu.roll(x, 1, 0),
            pltpu.roll(x, crows - 1, 0),
            pltpu.roll(x, 1, 1),
            pltpu.roll(x, wide - 1, 1),
        )

    masks = (
        crow_g >= 1,
        crow_g <= ch * n_gx - 2,
        ccol_g >= 1,
        ccol_g <= cw * n_gy - 2,
    )
    faces = [
        jnp.where(m, 0.5 * (cond + nb), 0.0) for m, nb in zip(masks, four(cond))
    ]
    offsum = faces[0] + faces[1] + faces[2] + faces[3]
    diagonal = acf[0] + offsum
    inv = 1.0 / diagonal
    ratio = offsum * inv
    peak = jnp.max(ratio[8 : 8 + ch, 0:cw])
    msend[...] = jnp.full((1, 128), peak, F32)

    def tell(k, c):
        t = lax.rem(me + k, ndev)
        remote(
            msend, mrecv.at[k - 1], m_sem.at[1], m_sem.at[0], (t // n_gy, t % n_gy)
        ).start()
        return c

    lax.fori_loop(1, ndev, tell, 0)

    t_all = tc[...]
    near = sum(f * nb for f, nb in zip(faces, four(t_all)))
    z = (acf[1] - (diagonal * t_all - near)) * inv
    faces = [f * inv for f in faces]
    for j in range(4):
        if j:
            z = z - sum(f * nb for f, nb in zip(faces, four(z)))
        for k in range(n_gy):
            zsend[k, j] = z[8 + rpd * k : 8 + rpd * k + rpd, 0:cw]

    def home(k, c):
        t = lax.rem(gy + k, n_gy)
        remote(zsend.at[t], zrecv.at[gy], z_sem.at[1], z_sem.at[0], (gx, t)).start()
        return c

    lax.fori_loop(1, n_gy, home, 0)
    pltpu.make_async_copy(zsend.at[gy], zrecv.at[gy], z_sem.at[0]).start()

    pltpu.make_async_copy(mrecv, mrecv, m_sem.at[0]).wait()
    peak = jnp.maximum(jnp.max(mrecv[...], axis=0), msend[...])[0:1, :]
    low, high = 1.0 - peak, 1.0 + peak
    center = 0.5 * (high + low)
    spread = 0.5 * (high - low)
    sigma = center / spread
    rho = 1.0 / sigma
    zero = jnp.zeros_like(center)
    e = [zero + 1.0, zero, zero, zero]
    d = [1.0 / center, zero, zero, zero]
    total = list(d)
    for _ in range(3):
        e = [e[0]] + [e[i] - d[i - 1] for i in range(1, 4)]
        rho_next = 1.0 / (2.0 * sigma - rho)
        d = [rho_next * rho * d[i] + (2.0 * rho_next / spread) * e[i] for i in range(4)]
        total = [a + b for a, b in zip(total, d)]
        rho = rho_next
    total = [jnp.concatenate([c] * (cw // 128), axis=1) for c in total]

    pltpu.make_async_copy(zrecv, zrecv, z_sem.at[0]).wait()
    for k in range(n_gy):
        x = warm[:, cw * k : cw * k + cw]
        for j in range(4):
            x = x + total[j] * zrecv[k, j]
        o_warm[:, cw * k : cw * k + cw] = x

    for copy in first + second:
        copy.wait_send()
    spread_sent(tsend, trecv, t_sem)
    remote(
        asend.at[pl.ds(0, n_gy - 1)], arecv.at[pl.ds(0, n_gy - 1)], a_sem.at[1], a_sem.at[0],
        (gx, right),
    ).wait_send()
    for copy in coarse_rows:
        copy.wait_send()
    part = pl.ds(0, n_gy - 1)
    remote(zsend.at[part], zrecv.at[part], z_sem.at[1], z_sem.at[0], (gx, right)).wait_send()
    remote(mrecv, mrecv, m_sem.at[1], m_sem.at[0], (gx, right)).wait_send()


def put_out(*refs):
    src, dst, sem = refs[0:4], refs[4:8], refs[8]
    out = [pltpu.make_async_copy(src[i], dst[i], sem.at[i]) for i in range(4)]
    for copy in out:
        copy.start()
    for copy in out:
        copy.wait()


def per_device(n_gx, n_gy, shift, speed, level, mark, warm, store, film, bath):
    _, hh, ww = shift.shape
    rpd, _ = warm.shape
    cw, ch = ww // 2, hh // 2
    wide, fwide = cw + 128, ww + 128
    crows, frows = ch + 16, hh + 2 * HALO
    nsl = n_gy + 2 * (HALO // rpd)
    vm = lambda *s: pltpu.VMEM(s, F32)
    dma = lambda n: pltpu.SemaphoreType.DMA((n,))
    hbm = pl.BlockSpec(memory_space=pltpu.HBM)
    outs = pl.pallas_call(
        functools.partial(kernel, n_gx, n_gy),
        out_shape=(
            pltpu.VMEM(shift.shape, F32),
            pltpu.VMEM(speed.shape, F32),
            pltpu.VMEM(level.shape, jnp.bfloat16),
            pltpu.VMEM(warm.shape, F32),
        ),
        in_specs=[hbm] * 8,
        out_specs=(pl.BlockSpec(memory_space=pltpu.VMEM),) * 4,
        scratch_shapes=[
            vm(n_gy, rpd, wide),
            vm(nsl, rpd, wide),
            vm(n_gy, 2, rpd, wide),
            vm(n_gy, 2, rpd, wide),
            vm(hh, 128),
            vm(hh, 128),
            vm(frows, 128),
            vm(frows, 128),
            vm(2, 8, 128),
            vm(2, 8, 128),
            vm(2, 6, 8, ww),
            vm(2, 6, 8, ww),
            vm(2, 6, 8, fwide),
            vm(SUBSTEPS, 4, 8, fwide),
            pltpu.VMEM(level.shape, level.dtype),
            vm(*warm.shape),
            vm(*warm.shape),
            vm(*warm.shape),
            vm(*warm.shape),
            vm(6, frows, fwide),
            vm(frows, fwide),
            vm(frows, fwide),
            vm(frows, fwide),
            vm(crows, wide),
            vm(2, crows, wide),
            vm(wide // 128, frows, 128),
            vm(ww // 128, hh, 128),
            vm(ch, cw),
            vm(2, 8, cw),
            vm(crows, 128),
            vm(crows, 128),
            vm(n_gy, 4, rpd, cw),
            vm(n_gy, 4, rpd, cw),
            vm(1, 128),
            vm(n_gx * n_gy - 1, 1, 128),
            dma(10),
            dma(10),
            dma(4),
            dma(6),
            dma(8),
            dma(8),
            dma(2),
            dma(2),
            dma(8),
            pltpu.SMEM((1, hh // SR), mark.dtype),
        ],
        compiler_params=pltpu.CompilerParams(
            collective_id=0, has_side_effects=True
        ),
    )(shift, speed, level, mark.reshape(1, hh // SR), warm, store, film, bath)
    return pl.pallas_call(
        put_out,
        out_shape=tuple(jax.ShapeDtypeStruct(o.shape, o.dtype) for o in outs),
        in_specs=[pl.BlockSpec(memory_space=pltpu.VMEM)] * 4,
        out_specs=(hbm,) * 4,
        scratch_shapes=[dma(4)],
    )(*(pltpu.with_memory_space_constraint(o, pltpu.VMEM) for o in outs))


def solution(mesh):
    rows = P(("gx", "gy"), None)
    plate = P(None, "gx", "gy")
    return jax.shard_map(
        functools.partial(per_device, mesh.shape["gx"], mesh.shape["gy"]),
        mesh=mesh,
        in_specs=(plate, plate, plate, P("gx", "gy"), rows, rows, rows, rows),
        out_specs=(plate, plate, plate, rows),
        check_vma=False,
    )
```

```python
import functools
import math

import jax
import jax.numpy as jnp
from jax import lax
from jax.experimental import pallas as pl
from jax.experimental.pallas import tpu as pltpu
from jax.sharding import PartitionSpec as P

SR = 8
SEG = 128
SUBSTEPS = 8
HALO = 8
FIELDS = 7
MESH = pl.DeviceIdType.MESH
F32 = jnp.float32


def lane_iota(shape):
    return lax.broadcasted_iota(jnp.int32, shape, 1)


def row_iota(shape):
    return lax.broadcasted_iota(jnp.int32, shape, 0)


def full_dot(a, b):
    return jnp.dot(a, b, precision=lax.Precision.HIGHEST, preferred_element_type=F32)


def pick(x, index):
    return jnp.take_along_axis(x, index, axis=1)


def kernel(
    n_gx,
    n_gy,
    shift,
    speed,
    level_h,
    mark_h,
    warm_h,
    store_h,
    film_h,
    bath_h,
    su,
    o_speed,
    o_dam,
    o_warm,
    tsend,
    trecv,
    asend,
    arecv,
    pk,
    rk,
    ck,
    rowsend,
    rowrecv,
    keep,
    hist_n,
    hist_u,
    level,
    warm,
    store,
    film,
    bath,
    sv,
    ss,
    kw,
    kh,
    tx,
    ty,
    fine,
    nx,
    tcx,
    acf,
    widebuf,
    tab_s,
    gap,
    cbuf,
    crow,
    ccl,
    ccr,
    zsend,
    zrecv,
    msend,
    mrecv,
    n_send,
    n_recv,
    t_sem,
    far_sem,
    a_sem,
    c_send,
    c_recv,
    z_sem,
    m_sem,
    in_sem,
    mark,
):
    ndev = n_gx * n_gy
    gx = lax.axis_index("gx")
    gy = lax.axis_index("gy")
    me = gx * n_gy + gy
    _, hh, ww = shift.shape
    rpd, _ = warm_h.shape
    cw = ww // 2
    ch = hh // 2
    hb = HALO // rpd
    nsl = n_gy + 2 * hb
    nt = ww // 128
    ntile = nt + 1
    nct = cw // 128
    frows = hh + 2 * HALO
    nstrip = frows // 8
    up = lax.rem(gx + n_gx - 1, n_gx)
    down = lax.rem(gx + 1, n_gx)
    left = lax.rem(gy + n_gy - 1, n_gy)
    right = lax.rem(gy + 1, n_gy)
    has_u, has_d = gx > 0, gx < n_gx - 1
    has_l, has_r = gy > 0, gy < n_gy - 1
    own_r = slice(HALO, HALO + hh)

    barrier = pltpu.get_barrier_semaphore()
    warm_load = pltpu.make_async_copy(warm_h, warm, in_sem.at[0])
    warm_load.start()

    def greet(a, b):
        pl.semaphore_signal(barrier, inc=1, device_id=(a, b), device_id_type=MESH)

    for k in range(1, n_gy):
        greet(gx, lax.rem(gy + k, n_gy))
    for k in range(1, n_gx):
        greet(lax.rem(gx + k, n_gx), gy)
    for a in (up, down):
        for b in (left, right):
            greet(a, b)

    loads = [
        pltpu.make_async_copy(src, dst, in_sem.at[i])
        for i, (src, dst) in enumerate(
            (
                (mark_h, mark),
                (level_h, level),
                (store_h, store),
                (film_h, film),
                (bath_h, bath),
            ),
            1,
        )
    ]
    loads[0].start()
    loads[1].start()
    for src, dst, i in ((shift, su, 6), (speed, sv, 7)):
        for t in range(nt):
            pltpu.make_async_copy(
                src.at[:, :, 128 * t : 128 * t + 128], dst.at[:, t, own_r, :], in_sem.at[i]
            ).start()
    for copy in loads[2:]:
        copy.start()

    def loaded(dst, i):
        part = dst.at[:, 0:nt, own_r, :]
        pltpu.make_async_copy(part, part, in_sem.at[i]).wait()

    lane_c = lane_iota((rpd, 128))

    def chunk(value, k):
        after = value[:, (cw * (k + 1)) % (cw * n_gy) :][:, 0:128]
        before = value[:, (cw * k - 128) % (cw * n_gy) :][:, 0:128]
        return value[:, cw * k : cw * k + cw], jnp.where(lane_c < 64, after, before)

    def remote(src, dst, ssem, rsem, where):
        return pltpu.make_async_remote_copy(
            src_ref=src, dst_ref=dst, send_sem=ssem, recv_sem=rsem, device_id=where,
            device_id_type=MESH,
        )

    warm_load.wait()
    t_own = warm[...]
    for k in range(n_gy):
        main, edge = chunk(t_own, k)
        tsend[k, :, 0:cw] = main
        tsend[k, :, cw : cw + 128] = edge

    pl.semaphore_wait(barrier, n_gy + n_gx + 2)

    def along(k, c):
        t = lax.rem(gy + k, n_gy)
        remote(tsend.at[t], trecv.at[gy + hb], t_sem.at[1], t_sem.at[0], (gx, t)).start()
        return c

    lax.fori_loop(1, n_gy, along, 0)
    pltpu.make_async_copy(tsend.at[gy], trecv.at[gy + hb], t_sem.at[0]).start()

    sharp = -4.0 * math.log2(math.e)
    lane = lane_iota((hh, 128))
    loads[0].wait()
    for s in range(hh // SR):
        kw[HALO + SR * s : HALO + SR * s + SR, :] = (
            jnp.full((SR, 128), mark[0, s], jnp.int32).astype(F32) * sharp
        )
    w_own = kw[own_r, :] * (0.125 / sharp)
    grow = gx * hh + row_iota((hh, 128))
    loads[1].wait()
    for t in range(nt):
        cols = slice(128 * t, 128 * t + 128)
        gcol = gy * ww + 128 * t + lane
        ss[0, t, own_r, :] = jnp.where(grow >= 1, 1.0 - level[0, :, cols].astype(F32) * w_own, 0.0)
        ss[1, t, own_r, :] = jnp.where(gcol >= 1, 1.0 - level[1, :, cols].astype(F32) * w_own, 0.0)
    loaded(su, 6)
    loaded(sv, 7)
    for c in range(2):
        for t in range(nt):
            sv[c, t, own_r, :] = 0.4 * sv[c, t, own_r, :]
    acc_l = jnp.zeros((hh, 128), F32)
    acc_r = jnp.zeros((hh, 128), F32)
    fields = [(ref, c) for ref in (su, sv, ss) for c in range(2)]
    for f in range(FIELDS):
        if f < 6:
            ref, c = fields[f]
            first, last = ref[c, 0, own_r, :], ref[c, nt - 1, own_r, :]
        else:
            first = last = kw[own_r, :]
        here = (lane >= 8 * f) & (lane < 8 * f + 8)
        first = pltpu.roll(first, 8 * f, 1) if f else first
        acc_l = jnp.where(here, first, acc_l)
        acc_r = jnp.where(here, pltpu.roll(last, 8 * f + 8, 1), acc_r)
    pk[0] = acc_l
    pk[1] = acc_r
    side_l = remote(pk.at[0], rk.at[1], n_send.at[0], n_recv.at[1], (gx, left))
    side_r = remote(pk.at[1], rk.at[0], n_send.at[1], n_recv.at[0], (gx, right))
    top, end = slice(0, 8), slice(hh - 8, hh)
    corners = [
        (has_u & has_l, remote(pk.at[0, top], ck.at[3], n_send.at[2], n_recv.at[5], (up, left)), 2),
        (has_u & has_r, remote(pk.at[1, top], ck.at[2], n_send.at[3], n_recv.at[4], (up, right)), 3),
        (has_d & has_l, remote(pk.at[0, end], ck.at[1], n_send.at[4], n_recv.at[3], (down, left)), 4),
        (has_d & has_r, remote(pk.at[1, end], ck.at[0], n_send.at[5], n_recv.at[2], (down, right)), 5),
    ]
    rows_u = remote(rowsend.at[0], rowrecv.at[1], n_send.at[6], n_recv.at[7], (up, gy))
    rows_d = remote(rowsend.at[1], rowrecv.at[0], n_send.at[7], n_recv.at[6], (down, gy))
    sends = [(has_l, side_l), (has_r, side_r)] + [(a, b) for a, b, _ in corners]
    sends += [(has_u, rows_u), (has_d, rows_d)]

    def start_if(cond, copy):
        @pl.when(cond)
        def _():
            copy.start()

    def sent_if(cond, copy):
        @pl.when(cond)
        def _():
            copy.wait_send()

    def came_if(cond, copy):
        @pl.when(cond)
        def _():
            copy.wait_recv()

    for cond, copy in sends[0:6]:
        start_if(cond, copy)
    for side, at in ((0, HALO), (1, HALO + hh - 8)):
        for f, (ref, c) in enumerate(fields):
            for t in range(nt):
                rowsend[side, nt * f + t] = ref[c, t, at : at + 8, :]
        rowsend[side, 6 * nt] = kw[at : at + 8, :]
    for cond, copy in sends[6:8]:
        start_if(cond, copy)

    k_i, n_i = row_iota((256, 128)), lane_iota((256, 128))
    pos = (k_i % SEG).astype(F32)
    col = (2 * (n_i % 64)).astype(F32)
    tab = jnp.exp(jnp.abs(pos - col) * (-4.0 / SEG)) + jnp.exp(jnp.abs(pos - col - 1.0) * (-4.0 / SEG))
    tab_s[...] = jnp.where(k_i // SEG == n_i // 64, tab * (1.0 / SEG), 0.0)
    for i in (2, 3, 4):
        loads[i].wait()
    base = store[...] + film[...]
    force_own = store[...] * t_own + film[...] * bath[...]
    for k in range(n_gy):
        for q, val in enumerate((base, force_own)):
            main, edge = chunk(val, k)
            asend[k, q, :, 0:cw] = main
            asend[k, q, :, cw : cw + 128] = edge
    for strip in ((nstrip - 2) * 8, nstrip * 8):
        nx[:, :, strip : strip + 8, :] = jnp.zeros((2, ntile, 8, 128), F32)
    keeps = (slice(16, 24), slice(frows - 24, frows - 16))
    for i, rows in enumerate(keeps):
        for f, (ref, c) in enumerate(fields):
            for t in range(nt):
                keep[i, f, t] = ref[c, t, rows, :]

    mid = trecv.at[pl.ds(hb, n_gy)]
    pltpu.make_async_copy(mid, mid, t_sem.at[0]).wait()
    far_u = remote(
        trecv.at[pl.ds(hb, hb)], trecv.at[pl.ds(hb + n_gy, hb)], t_sem.at[2], far_sem.at[1], (up, gy)
    )
    far_d = remote(
        trecv.at[pl.ds(n_gy, hb)], trecv.at[pl.ds(0, hb)], t_sem.at[3], far_sem.at[0], (down, gy)
    )
    start_if(has_u, far_u)
    start_if(has_d, far_d)

    def late(k, c):
        t = lax.rem(gy + k, n_gy)
        remote(asend.at[t], arecv.at[gy], a_sem.at[1], a_sem.at[0], (gx, t)).start()
        return c

    lax.fori_loop(1, n_gy, late, 0)
    pltpu.make_async_copy(asend.at[gy], arecv.at[gy], a_sem.at[0]).start()
    crows = ch + 16
    wide = cw + 128
    lane8 = lane_iota((8, 128))
    first_lane, last_lane = lane8 == 0, lane8 == 127

    def close_edge(rows):
        edge = tcx[nct, rows, :]
        edge = jnp.where(~has_l & last_lane, pltpu.roll(tcx[0, rows, :], 127, 1), edge)
        edge = jnp.where(~has_r & first_lane, pltpu.roll(tcx[nct - 1, rows, :], 1, 1), edge)
        tcx[nct, rows, :] = edge

    for k in range(hb, hb + n_gy):
        for j in range(nct + 1):
            tcx[j, rpd * k : rpd * k + rpd, :] = trecv[k, :, 128 * j : 128 * j + 128]
    for c in range(8, 8 + ch, 8):
        close_edge(slice(c, c + 8))
    half = lane8 // 2
    step = jnp.where(lane8 % 2 == 0, -1, 1)
    lo_g, lo_h = half, jnp.maximum(half + step, 0)
    hi_g, hi_h = half + 64, jnp.minimum(half + 64 + step, 127)
    ed_g = jnp.where(lane8 < 64, half, half + 64)
    ed_h = jnp.minimum(jnp.maximum(ed_g + step, 0), 127)

    def before(tiles):
        turned = [pltpu.roll(x, 1, 1) for x in tiles]
        return [jnp.where(first_lane, turned[t - 1], turned[t]) for t in range(len(tiles))]

    def after(tiles):
        turned = [pltpu.roll(x, 127, 1) for x in tiles]
        n = len(tiles)
        return [jnp.where(last_lane, turned[(t + 1) % n], turned[t]) for t in range(n)]

    def above(ref, s):
        return ref[8 * s - 1 : 8 * s + 7, :] if s else pltpu.roll(ref[0:8, :], 1, 0)

    def heat_x(s):
        rows = slice(8 * s, 8 * s + 8)
        for t in range(ntile):
            tx[t, rows, :] = 0.3 * (fine[t, rows, :] + above(fine.at[t], s))

    def prolong(p):
        c = 8 * p + 4
        for j in range(nct + 1):
            here = 0.75 * tcx[j, c : c + 8, :]
            widebuf[j, pl.ds(16 * p, 8, stride=2), :] = here + 0.25 * tcx[j, c - 1 : c + 7, :]
            widebuf[j, pl.ds(16 * p + 1, 8, stride=2), :] = here + 0.25 * tcx[j, c + 1 : c + 9, :]
        for s in (2 * p, 2 * p + 1):
            rows = slice(8 * s, 8 * s + 8)
            r = [widebuf[j, rows, :] for j in range(nct + 1)]
            fwd = [pltpu.roll(x, 1, 1) for x in r]
            bwd = [pltpu.roll(x, 127, 1) for x in r]
            f = []
            for j in range(nct):
                f.append(
                    0.75 * pick(r[j], lo_g)
                    + 0.25 * jnp.where(first_lane, fwd[j - 1], pick(r[j], lo_h))
                )
                f.append(
                    0.75 * pick(r[j], hi_g)
                    + 0.25 * jnp.where(last_lane, bwd[j + 1], pick(r[j], hi_h))
                )
            e = pick(r[nct], ed_h)
            e = jnp.where(first_lane, fwd[nct - 1], jnp.where(last_lane, bwd[0], e))
            f.append(0.75 * pick(r[nct], ed_g) + 0.25 * e)
            prev = before(f)
            for t in range(ntile):
                fine[t, rows, :] = f[t]
                ty[t, rows, :] = 0.3 * (f[t] + prev[t])

    npair = nstrip // 2
    for p in range(1, npair - 1):
        prolong(p)
    for s in range(2, nstrip - 2):
        heat_x(s)

    came_if(has_l, side_r)
    came_if(has_r, side_l)

    def unpack(got_l, got_r, rows, outside):
        shape = got_l.shape
        lanes = lane_iota(shape)
        gone = outside | (~has_l & (lanes >= 64)) | (~has_r & (lanes < 64))
        for f in range(FIELDS):
            from_r = pltpu.roll(got_r, 128 - 8 * f, 1) if f else got_r
            from_l = pltpu.roll(got_l, 120 - 8 * f, 1)
            side = jnp.where(lanes < 8, from_r, jnp.where(lanes >= 120, from_l, 0.0))
            side = jnp.where(gone, 0.0, side)
            if f < 6:
                ref, c = fields[f]
                ref[c, nt, rows, :] = side
            else:
                kh[rows, :] = side

    unpack(rk[0], rk[1], own_r, False)
    for i, rows in enumerate(keeps):
        for f, (ref, c) in enumerate(fields):
            keep[i, f, nt] = ref[c, nt, rows, :]

    def edges(s):
        rows = slice(8 * s, 8 * s + 8)
        u0 = [su[0, t, rows, :] for t in range(ntile)]
        u1 = [su[1, t, rows, :] for t in range(ntile)]
        k_main, k_side = kw[rows, :], kh[rows, :]
        b0, b1 = before(u0), before(u1)
        ay, ny = [], []
        for t in range(ntile):
            k = k_main if t < nt else k_side
            open_x = u0[t] - above(su.at[0, t], s) - tx[t, rows, :]
            st = jnp.maximum(open_x, 0.0)
            sp = jnp.minimum(ss[0, t, rows, :], jnp.exp2(st * st * k))
            ss[0, t, rows, :] = sp
            nx[0, t, rows, :] = sp * open_x
            nx[1, t, rows, :] = sp * (u1[t] - above(su.at[1, t], s))
            open_y = u1[t] - b1[t] - ty[t, rows, :]
            st = jnp.maximum(open_y, 0.0)
            sp = jnp.minimum(ss[1, t, rows, :], jnp.exp2(st * st * k))
            ss[1, t, rows, :] = sp
            ny.append(sp * open_y)
            ay.append(sp * (u0[t] - b0[t]))
        fy0 = [a - b for a, b in zip(after(ay), ay)]
        fy1 = [a - b for a, b in zip(after(ny), ny)]
        return fy0, fy1

    def advance(s, fy):
        rows = slice(8 * s, 8 * s + 8)
        below = slice(8 * s + 1, 8 * s + 9)
        for c in range(2):
            for t in range(ntile):
                force = (nx[c, t, below, :] - nx[c, t, rows, :]) + fy[c][t]
                v = 0.98 * sv[c, t, rows, :] + 0.16 * force
                sv[c, t, rows, :] = v
                su[c, t, rows, :] = su[c, t, rows, :] + v

    def interior(i, carry):
        old = None
        for s in range(2, nstrip - 2):
            if s == nstrip - 4:
                for c in range(2):
                    for t in range(ntile):
                        hist_u[i, c, t] = su[c, t, 8 * s : 8 * s + 8, :]
            new = edges(s)
            if s == 3:
                for c in range(2):
                    for t in range(ntile):
                        hist_n[i, c, t] = nx[c, t, 8 * s : 8 * s + 8, :]
            if old:
                advance(s - 1, old)
            old = new
        advance(nstrip - 3, old)
        return carry

    lax.fori_loop(0, SUBSTEPS, interior, 0)

    for side, (here, at, slot, line) in enumerate(
        ((has_u, 0, 0, 8), (has_d, ch + 8, hb + n_gy, ch + 7))
    ):
        came_if(here, far_u if side else far_d)

        @pl.when(here)
        def _():
            for k in range(hb):
                for j in range(nct + 1):
                    tcx[j, at + rpd * k : at + rpd * k + rpd, :] = trecv[
                        slot + k, :, 128 * j : 128 * j + 128
                    ]
            close_edge(slice(at, at + 8))

        @pl.when(jnp.logical_not(here))
        def _():
            for j in range(nct + 1):
                tcx[j, at : at + 8, :] = jnp.broadcast_to(tcx[j, line : line + 1, :], (8, 128))

    prolong(0)
    prolong(npair - 1)
    for s in (0, 1, 2, nstrip - 2, nstrip - 1):
        heat_x(s)

    came_if(has_u & has_l, corners[3][1])
    came_if(has_u & has_r, corners[2][1])
    came_if(has_d & has_l, corners[1][1])
    came_if(has_d & has_r, corners[0][1])
    came_if(has_u, rows_d)
    came_if(has_d, rows_u)
    for side, (here, at) in enumerate(((has_u, 0), (has_d, hh + HALO))):
        rows = slice(at, at + 8)
        for f, (ref, c) in enumerate(fields):
            for t in range(nt):
                ref[c, t, rows, :] = jnp.where(here, rowrecv[side, nt * f + t], 0.0)
        kw[rows, :] = jnp.where(here, rowrecv[side, 6 * nt], 0.0)
        unpack(ck[2 * side], ck[2 * side + 1], rows, ~here)
    for i, rows in enumerate(keeps):
        for f, (ref, c) in enumerate(fields):
            for t in range(ntile):
                ref[c, t, rows, :] = keep[i, f, t]
    line = frows - 25
    final = [[su[c, t, line : line + 1, :] for t in range(ntile)] for c in range(2)]
    for c in range(2):
        for t in range(ntile):
            hist_n[SUBSTEPS, c, t, 0:1, :] = final[c][t]

    def border(i, carry):
        for c in range(2):
            for t in range(ntile):
                nx[c, t, 24:32, :] = hist_n[i, c, t]
                su[c, t, line : line + 1, :] = hist_u[i, c, t, 7:8, :]
        for at in (0, nstrip - 3):
            old = None
            for s in range(at, at + 3):
                new = edges(s)
                if old:
                    advance(s - 1, old)
                old = new
            advance(at + 2, old)
        return carry

    lax.fori_loop(0, SUBSTEPS, border, 0)
    for c in range(2):
        for t in range(ntile):
            su[c, t, line : line + 1, :] = hist_n[SUBSTEPS, c, t, 0:1, :]

    pltpu.make_async_copy(arecv, arecv, a_sem.at[0]).wait()
    for k in range(n_gy):
        for q in range(2):
            acf[q, 8 + rpd * k : 8 + rpd * k + rpd, :] = arecv[k, q]
    coarse_rows = [
        remote(
            acf.at[:, 8:16], acf.at[:, ch + 8 : ch + 16], a_sem.at[2], a_sem.at[4], (up, gy)
        ),
        remote(acf.at[:, ch : ch + 8], acf.at[:, 0:8], a_sem.at[3], a_sem.at[5], (down, gy)),
    ]
    for copy in coarse_rows:
        copy.start()

    for t in range(nt):
        gcol = gy * ww + 128 * t + lane
        dam_x = jnp.where(grow >= 1, 1.0 - ss[0, t, own_r, :], 0.0)
        dam_y = jnp.where(gcol >= 1, 1.0 - ss[1, t, own_r, :], 0.0)
        gap[t] = dam_x + dam_y
        o_dam[0, t] = dam_x.astype(jnp.bfloat16)
        o_dam[1, t] = dam_y.astype(jnp.bfloat16)
    rows2 = jnp.concatenate(
        [
            gap[t, pl.ds(0, ch, stride=2), :] + gap[t, pl.ds(1, ch, stride=2), :]
            for t in range(ww // 128)
        ],
        axis=1,
    )
    pairs = ww // 256
    glow = full_dot(
        jnp.concatenate([rows2[:, 256 * t : 256 * t + 256] for t in range(pairs)], axis=0), tab_s[...]
    )
    resist = jnp.concatenate([glow[ch * t : ch * t + ch] for t in range(pairs)], axis=1)
    t_all = jnp.concatenate([tcx[j] for j in range(nct + 1)], axis=1)
    cond_own = (1.0 + 0.5 * t_all[8 : 8 + ch, 0:cw]) / (1.0 + resist)
    cbuf[...] = cond_own
    def neighbours(send_l, send_r, row_u, row_d, recv_l, recv_r, got_u, got_d, rows, ssem, rsem):
        top, end = slice(0, 8), slice(rows - 8, rows)
        lo, mid, hi = slice(0, 8), slice(8, rows + 8), slice(rows + 8, rows + 16)
        return [
            remote(row_u, got_d, ssem.at[0], rsem.at[0], (up, gy)),
            remote(row_d, got_u, ssem.at[1], rsem.at[1], (down, gy)),
            remote(send_l, recv_r.at[mid], ssem.at[2], rsem.at[2], (gx, left)),
            remote(send_r, recv_l.at[mid], ssem.at[3], rsem.at[3], (gx, right)),
            remote(send_l.at[top], recv_r.at[hi], ssem.at[4], rsem.at[4], (up, left)),
            remote(send_r.at[top], recv_l.at[hi], ssem.at[5], rsem.at[5], (up, right)),
            remote(send_l.at[end], recv_r.at[lo], ssem.at[6], rsem.at[6], (down, left)),
            remote(send_r.at[end], recv_l.at[lo], ssem.at[7], rsem.at[7], (down, right)),
        ]

    second = neighbours(
        cbuf.at[:, 0:128], cbuf.at[:, cw - 128 : cw], cbuf.at[0:8], cbuf.at[ch - 8 : ch],
        ccl, ccr, crow.at[0], crow.at[1], ch, c_send, c_recv,
    )
    for copy in second:
        copy.start()

    for c in range(2):
        for t in range(nt):
            o_speed[c, t] = 2.5 * sv[c, t, own_r, :]

    for copy in coarse_rows:
        copy.wait_recv()

    for copy in second:
        copy.wait_recv()
    lane_k = lane_iota((crows, 128))
    cond = jnp.concatenate(
        [
            jnp.concatenate([crow[0], cbuf[...], crow[1]], axis=0),
            jnp.where(lane_k < 64, ccr[...], ccl[...]),
        ],
        axis=1,
    )
    crow_i, clane_i = row_iota((crows, wide)), lane_iota((crows, wide))
    crow_g = gx * ch - 8 + crow_i
    ccol_g = gy * cw + jnp.where(clane_i < cw + 64, clane_i, clane_i - wide)

    def four(x):
        return (
            pltpu.roll(x, 1, 0),
            pltpu.roll(x, crows - 1, 0),
            pltpu.roll(x, 1, 1),
            pltpu.roll(x, wide - 1, 1),
        )

    masks = (
        crow_g >= 1,
        crow_g <= ch * n_gx - 2,
        ccol_g >= 1,
        ccol_g <= cw * n_gy - 2,
    )
    faces = [
        jnp.where(m, 0.5 * (cond + nb), 0.0) for m, nb in zip(masks, four(cond))
    ]
    offsum = faces[0] + faces[1] + faces[2] + faces[3]
    diagonal = acf[0] + offsum
    inv = 1.0 / diagonal
    ratio = offsum * inv
    peak = jnp.max(ratio[8 : 8 + ch, 0:cw])
    msend[...] = jnp.full((1, 128), peak, F32)

    def tell(k, c):
        t = lax.rem(me + k, ndev)
        remote(
            msend, mrecv.at[k - 1], m_sem.at[1], m_sem.at[0], (t // n_gy, t % n_gy)
        ).start()
        return c

    lax.fori_loop(1, ndev, tell, 0)

    near = sum(f * nb for f, nb in zip(faces, four(t_all)))
    z = (acf[1] - (diagonal * t_all - near)) * inv
    faces = [f * inv for f in faces]
    for j in range(4):
        if j:
            z = z - sum(f * nb for f, nb in zip(faces, four(z)))
        for k in range(n_gy):
            zsend[k, j] = z[8 + rpd * k : 8 + rpd * k + rpd, 0:cw]

    def home(k, c):
        t = lax.rem(gy + k, n_gy)
        remote(zsend.at[t], zrecv.at[gy], z_sem.at[1], z_sem.at[0], (gx, t)).start()
        return c

    lax.fori_loop(1, n_gy, home, 0)
    pltpu.make_async_copy(zsend.at[gy], zrecv.at[gy], z_sem.at[0]).start()

    pltpu.make_async_copy(mrecv, mrecv, m_sem.at[0]).wait()
    peak = jnp.maximum(jnp.max(mrecv[...], axis=0), msend[...])[0:1, :]
    low, high = 1.0 - peak, 1.0 + peak
    center = 0.5 * (high + low)
    spread = 0.5 * (high - low)
    sigma = center / spread
    rho = 1.0 / sigma
    zero = jnp.zeros_like(center)
    e = [zero + 1.0, zero, zero, zero]
    d = [1.0 / center, zero, zero, zero]
    total = list(d)
    for _ in range(3):
        e = [e[0]] + [e[i] - d[i - 1] for i in range(1, 4)]
        rho_next = 1.0 / (2.0 * sigma - rho)
        d = [rho_next * rho * d[i] + (2.0 * rho_next / spread) * e[i] for i in range(4)]
        total = [a + b for a, b in zip(total, d)]
        rho = rho_next
    total = [jnp.concatenate([c] * (cw // 128), axis=1) for c in total]

    pltpu.make_async_copy(zrecv, zrecv, z_sem.at[0]).wait()
    for k in range(n_gy):
        x = warm[:, cw * k : cw * k + cw]
        for j in range(4):
            x = x + total[j] * zrecv[k, j]
        o_warm[:, cw * k : cw * k + cw] = x

    for copy in second:
        copy.wait_send()
    for cond, copy in sends:
        sent_if(cond, copy)
    part = pl.ds(0, n_gy - 1)
    remote(tsend.at[part], trecv.at[part], t_sem.at[1], t_sem.at[0], (gx, right)).wait_send()
    sent_if(has_u, far_u)
    sent_if(has_d, far_d)
    remote(
        asend.at[pl.ds(0, n_gy - 1)], arecv.at[pl.ds(0, n_gy - 1)], a_sem.at[1], a_sem.at[0],
        (gx, right),
    ).wait_send()
    for copy in coarse_rows:
        copy.wait_send()
    part = pl.ds(0, n_gy - 1)
    remote(zsend.at[part], zrecv.at[part], z_sem.at[1], z_sem.at[0], (gx, right)).wait_send()
    remote(mrecv, mrecv, m_sem.at[1], m_sem.at[0], (gx, right)).wait_send()


def put_out(su, speed, dam, warm, o_shift, o_speed, o_dam, o_warm, sem):
    nt = dam.shape[1]
    hh = dam.shape[2]
    out = [pltpu.make_async_copy(warm, o_warm, sem.at[3 * nt])]
    for t in range(nt):
        cols = slice(128 * t, 128 * t + 128)
        out += [
            pltpu.make_async_copy(
                su.at[:, t, HALO : HALO + hh, :], o_shift.at[:, :, cols], sem.at[3 * t]
            ),
            pltpu.make_async_copy(speed.at[:, t], o_speed.at[:, :, cols], sem.at[3 * t + 1]),
            pltpu.make_async_copy(dam.at[:, t], o_dam.at[:, :, cols], sem.at[3 * t + 2]),
        ]
    for copy in out:
        copy.start()
    for copy in out:
        copy.wait()


def per_device(n_gx, n_gy, shift, speed, level, mark, warm, store, film, bath):
    _, hh, ww = shift.shape
    rpd, _ = warm.shape
    cw, ch = ww // 2, hh // 2
    wide = cw + 128
    nt, nct = ww // 128, cw // 128
    ntile = nt + 1
    crows, frows = ch + 16, hh + 2 * HALO
    nsl = n_gy + 2 * (HALO // rpd)
    vm = lambda *s: pltpu.VMEM(s, F32)
    dma = lambda n: pltpu.SemaphoreType.DMA((n,))
    hbm = pl.BlockSpec(memory_space=pltpu.HBM)
    vmem = pl.BlockSpec(memory_space=pltpu.VMEM)
    outs = pl.pallas_call(
        functools.partial(kernel, n_gx, n_gy),
        out_shape=(
            vm(2, ntile, frows, 128),
            vm(2, nt, hh, 128),
            pltpu.VMEM((2, nt, hh, 128), jnp.bfloat16),
            vm(*warm.shape),
        ),
        in_specs=[hbm] * 8,
        out_specs=(vmem,) * 4,
        scratch_shapes=[
            vm(n_gy, rpd, wide),
            vm(nsl, rpd, wide),
            vm(n_gy, 2, rpd, wide),
            vm(n_gy, 2, rpd, wide),
            vm(2, hh, 128),
            vm(2, hh, 128),
            vm(4, 8, 128),
            vm(2, 6 * nt + 1, 8, 128),
            vm(2, 6 * nt + 1, 8, 128),
            vm(2, 6, ntile, 8, 128),
            vm(SUBSTEPS + 1, 2, ntile, 8, 128),
            vm(SUBSTEPS, 2, ntile, 8, 128),
            pltpu.VMEM(level.shape, level.dtype),
            vm(*warm.shape),
            vm(*warm.shape),
            vm(*warm.shape),
            vm(*warm.shape),
            vm(2, ntile, frows, 128),
            vm(2, ntile, frows, 128),
            vm(frows, 128),
            vm(frows, 128),
            vm(ntile, frows, 128),
            vm(ntile, frows, 128),
            vm(ntile, frows, 128),
            vm(2, ntile, frows + 8, 128),
            vm(nct + 1, crows, 128),
            vm(2, crows, wide),
            vm(nct + 1, frows, 128),
            vm(256, 128),
            vm(nt, hh, 128),
            vm(ch, cw),
            vm(2, 8, cw),
            vm(crows, 128),
            vm(crows, 128),
            vm(n_gy, 4, rpd, cw),
            vm(n_gy, 4, rpd, cw),
            vm(1, 128),
            vm(n_gx * n_gy - 1, 1, 128),
            dma(8),
            dma(8),
            dma(4),
            dma(2),
            dma(6),
            dma(8),
            dma(8),
            dma(2),
            dma(2),
            dma(8),
            pltpu.SMEM((1, hh // SR), mark.dtype),
        ],
        compiler_params=pltpu.CompilerParams(
            collective_id=0, has_side_effects=True
        ),
    )(shift, speed, level, mark.reshape(1, hh // SR), warm, store, film, bath)
    return pl.pallas_call(
        put_out,
        out_shape=tuple(
            jax.ShapeDtypeStruct(o.shape, d)
            for o, d in ((shift, F32), (speed, F32), (level, jnp.bfloat16), (warm, F32))
        ),
        in_specs=[vmem] * 4,
        out_specs=(hbm,) * 4,
        scratch_shapes=[dma(3 * nt + 1)],
    )(*(pltpu.with_memory_space_constraint(o, pltpu.VMEM) for o in outs))


def solution(mesh):
    rows = P(("gx", "gy"), None)
    plate = P(None, "gx", "gy")
    return jax.shard_map(
        functools.partial(per_device, mesh.shape["gx"], mesh.shape["gy"]),
        mesh=mesh,
        in_specs=(plate, plate, plate, P("gx", "gy"), rows, rows, rows, rows),
        out_specs=(plate, plate, plate, rows),
        check_vma=False,
    )
```

```python
import functools
import math

import jax
import jax.numpy as jnp
from jax import lax
from jax.experimental import pallas as pl
from jax.experimental.pallas import tpu as pltpu
from jax.sharding import PartitionSpec as P

SR = 8
SEG = 128
SUBSTEPS = 8
HALO = 8
FIELDS = 7
MESH = pl.DeviceIdType.MESH
F32 = jnp.float32


def lane_iota(shape):
    return lax.broadcasted_iota(jnp.int32, shape, 1)


def row_iota(shape):
    return lax.broadcasted_iota(jnp.int32, shape, 0)


def full_dot(a, b):
    return jnp.dot(a, b, precision=lax.Precision.HIGHEST, preferred_element_type=F32)


def pick(x, index):
    return jnp.take_along_axis(x, index, axis=1)


def kernel(
    n_gx,
    n_gy,
    shift,
    speed,
    level_h,
    mark_h,
    warm_h,
    store_h,
    film_h,
    bath_h,
    su,
    o_speed,
    o_dam,
    o_warm,
    tsend,
    trecv,
    asend,
    arecv,
    pk,
    rk,
    ck,
    rowsend,
    rowrecv,
    keep,
    hist_n,
    hist_u,
    level,
    warm,
    store,
    film,
    bath,
    sv,
    ss,
    kw,
    kh,
    tx,
    ty,
    fine,
    nx,
    tcx,
    widebuf,
    tab_s,
    gap,
    base_t,
    cpad,
    erow,
    grow_c,
    ecol,
    gcol_c,
    cb4,
    owc,
    own3,
    field,
    zown,
    msend,
    mrecv,
    s_sem,
    r_sem,
    meter,
    mark,
):
    ndev = n_gx * n_gy
    gx = lax.axis_index("gx")
    gy = lax.axis_index("gy")
    me = gx * n_gy + gy
    _, hh, ww = shift.shape
    rpd, _ = warm_h.shape
    cw = ww // 2
    ch = hh // 2
    hb = HALO // rpd
    nsl = n_gy + 2 * hb
    nt = ww // 128
    ntile = nt + 1
    nct = cw // 128
    frows = hh + 2 * HALO
    nstrip = frows // 8
    up = lax.rem(gx + n_gx - 1, n_gx)
    down = lax.rem(gx + 1, n_gx)
    left = lax.rem(gy + n_gy - 1, n_gy)
    right = lax.rem(gy + 1, n_gy)
    has_u, has_d = gx > 0, gx < n_gx - 1
    has_l, has_r = gy > 0, gy < n_gy - 1
    hz = HALO // 2 // rpd
    span = cw * n_gy
    own_r = slice(HALO, HALO + hh)

    n_v = jnp.where(has_u, 1, 0) + jnp.where(has_d, 1, 0)
    n_h = jnp.where(has_l, 1, 0) + jnp.where(has_r, 1, 0)

    def size(ref):
        return math.prod(ref.shape) // 128

    def done(sem, lines):
        part = meter.at[pl.ds(0, lines)]
        pltpu.make_async_copy(part, part, sem).wait()

    def done_if(cond, sem, lines):
        if lines:

            @pl.when(cond)
            def _():
                done(sem, lines)

    barrier = pltpu.get_barrier_semaphore()
    warm_load = pltpu.make_async_copy(warm_h, warm, r_sem.at[9])
    warm_load.start()

    def greet(a, b):
        pl.semaphore_signal(barrier, inc=1, device_id=(a, b), device_id_type=MESH)

    for k in range(1, n_gy):
        greet(gx, lax.rem(gy + k, n_gy))
    for k in range(1, n_gx):
        greet(lax.rem(gx + k, n_gx), gy)
    for a in (up, down):
        for b in (left, right):
            greet(a, b)

    loads = [
        pltpu.make_async_copy(src, dst, r_sem.at[i])
        for src, dst, i in (
            (mark_h, mark, 1),
            (level_h, level, 10),
            (store_h, store, 11),
            (film_h, film, 11),
            (bath_h, bath, 11),
        )
    ]
    loads[0].start()
    loads[1].start()
    for src, dst in ((shift, su), (speed, sv)):
        for t in range(nt):
            pltpu.make_async_copy(
                src.at[:, :, 128 * t : 128 * t + 128], dst.at[:, t, own_r, :], r_sem.at[10]
            ).start()
    for copy in loads[2:]:
        copy.start()

    lane_c = lane_iota((rpd, 128))

    def chunk(value, k):
        after = value[:, (cw * (k + 1)) % (cw * n_gy) :][:, 0:128]
        before = value[:, (cw * k - 128) % (cw * n_gy) :][:, 0:128]
        return value[:, cw * k : cw * k + cw], jnp.where(lane_c < 64, after, before)

    def remote(src, dst, ssem, rsem, where):
        return pltpu.make_async_remote_copy(
            src_ref=src, dst_ref=dst, send_sem=ssem, recv_sem=rsem, device_id=where,
            device_id_type=MESH,
        )

    warm_load.wait()
    t_own = warm[...]
    for k in range(n_gy):
        main, edge = chunk(t_own, k)
        tsend[k, :, 0:cw] = main
        tsend[k, :, cw : cw + 128] = edge

    pl.semaphore_wait(barrier, n_gy + n_gx + 2)

    for k in range(1, n_gy):
        t = lax.rem(gy + k, n_gy)
        remote(tsend.at[t], trecv.at[gy + hb], s_sem.at[0], r_sem.at[3], (gx, t)).start()
    pltpu.make_async_copy(tsend.at[gy], trecv.at[gy + hb], r_sem.at[3]).start()

    sharp = -4.0 * math.log2(math.e)
    lane = lane_iota((hh, 128))
    loads[0].wait()
    done(r_sem.at[10], 3 * size(level))
    for s in range(hh // SR):
        kw[HALO + SR * s : HALO + SR * s + SR, :] = (
            jnp.full((SR, 128), mark[0, s], jnp.int32).astype(F32) * sharp
        )
    w_own = kw[own_r, :] * (0.125 / sharp)
    grow = gx * hh + row_iota((hh, 128))
    for t in range(nt):
        cols = slice(128 * t, 128 * t + 128)
        gcol = gy * ww + 128 * t + lane
        ss[0, t, own_r, :] = jnp.where(grow >= 1, 1.0 - level[0, :, cols].astype(F32) * w_own, 0.0)
        ss[1, t, own_r, :] = jnp.where(gcol >= 1, 1.0 - level[1, :, cols].astype(F32) * w_own, 0.0)
    for c in range(2):
        for t in range(nt):
            sv[c, t, own_r, :] = 0.4 * sv[c, t, own_r, :]
    acc_l = jnp.zeros((hh, 128), F32)
    acc_r = jnp.zeros((hh, 128), F32)
    fields = [(ref, c) for ref in (su, sv, ss) for c in range(2)]
    for f in range(FIELDS):
        if f < 6:
            ref, c = fields[f]
            first, last = ref[c, 0, own_r, :], ref[c, nt - 1, own_r, :]
        else:
            first = last = kw[own_r, :]
        here = (lane >= 8 * f) & (lane < 8 * f + 8)
        first = pltpu.roll(first, 8 * f, 1) if f else first
        acc_l = jnp.where(here, first, acc_l)
        acc_r = jnp.where(here, pltpu.roll(last, 8 * f + 8, 1), acc_r)
    pk[0] = acc_l
    pk[1] = acc_r
    side_l = remote(pk.at[0], rk.at[1], s_sem.at[3], r_sem.at[0], (gx, left))
    side_r = remote(pk.at[1], rk.at[0], s_sem.at[4], r_sem.at[0], (gx, right))
    top, end = slice(0, 8), slice(hh - 8, hh)
    corners = [
        (has_u & has_l, remote(pk.at[0, top], ck.at[3], s_sem.at[1], r_sem.at[2], (up, left)), 2),
        (has_u & has_r, remote(pk.at[1, top], ck.at[2], s_sem.at[1], r_sem.at[2], (up, right)), 3),
        (has_d & has_l, remote(pk.at[0, end], ck.at[1], s_sem.at[2], r_sem.at[2], (down, left)), 4),
        (has_d & has_r, remote(pk.at[1, end], ck.at[0], s_sem.at[2], r_sem.at[2], (down, right)), 5),
    ]
    rows_u = remote(rowsend.at[0], rowrecv.at[1], s_sem.at[1], r_sem.at[2], (up, gy))
    rows_d = remote(rowsend.at[1], rowrecv.at[0], s_sem.at[2], r_sem.at[2], (down, gy))
    sends = [(has_l, side_l), (has_r, side_r)] + [(a, b) for a, b, _ in corners]
    sends += [(has_u, rows_u), (has_d, rows_d)]

    def start_if(cond, copy):
        @pl.when(cond)
        def _():
            copy.start()

    def sent_if(cond, copy):
        @pl.when(cond)
        def _():
            copy.wait_send()

    for cond, copy in sends[0:6]:
        start_if(cond, copy)
    for side, at in ((0, HALO), (1, HALO + hh - 8)):
        for f, (ref, c) in enumerate(fields):
            for t in range(nt):
                rowsend[side, nt * f + t] = ref[c, t, at : at + 8, :]
        rowsend[side, 6 * nt] = kw[at : at + 8, :]
    for cond, copy in sends[6:8]:
        start_if(cond, copy)

    k_i, n_i = row_iota((256, 128)), lane_iota((256, 128))
    pos = (k_i % SEG).astype(F32)
    col = (2 * (n_i % 64)).astype(F32)
    tab = jnp.exp(jnp.abs(pos - col) * (-4.0 / SEG)) + jnp.exp(jnp.abs(pos - col - 1.0) * (-4.0 / SEG))
    tab_s[...] = jnp.where(k_i // SEG == n_i // 64, tab * (1.0 / SEG), 0.0)
    done(r_sem.at[11], 3 * size(store))
    base = store[...] + film[...]
    own3[0, hz] = t_own
    own3[1, hz] = base
    own3[2, hz] = store[...] * t_own + film[...] * bath[...]
    for k in range(n_gy):
        asend[k] = base[:, cw * k : cw * k + cw]
    for strip in ((nstrip - 2) * 8, nstrip * 8):
        nx[:, :, strip : strip + 8, :] = jnp.zeros((2, ntile, 8, 128), F32)
    keeps = (slice(16, 24), slice(frows - 24, frows - 16))
    for i, rows in enumerate(keeps):
        for f, (ref, c) in enumerate(fields):
            for t in range(nt):
                keep[i, f, t] = ref[c, t, rows, :]

    mid = trecv.at[pl.ds(hb, n_gy)]
    pltpu.make_async_copy(mid, mid, r_sem.at[3]).wait()
    far_u = remote(
        trecv.at[pl.ds(hb, hb)], trecv.at[pl.ds(hb + n_gy, hb)], s_sem.at[1], r_sem.at[2], (up, gy)
    )
    far_d = remote(
        trecv.at[pl.ds(n_gy, hb)], trecv.at[pl.ds(0, hb)], s_sem.at[2], r_sem.at[2], (down, gy)
    )
    start_if(has_u, far_u)
    start_if(has_d, far_d)

    def late(k, c):
        t = lax.rem(gy + k, n_gy)
        remote(asend.at[t], arecv.at[gy], s_sem.at[0], r_sem.at[4], (gx, t)).start()
        return c

    lax.fori_loop(1, n_gy, late, 0)
    pltpu.make_async_copy(asend.at[gy], arecv.at[gy], r_sem.at[4]).start()
    mine = own3.at[:, hz]
    swaps = []
    for d in range(1, hz + 1):
        for i, to, ok, came in (
            (d - 1, me + d, me + d < ndev, me >= d),
            (hz + d - 1, me - d, me >= d, me + d < ndev),
        ):
            at = hz - d if i < hz else hz + d
            to = lax.rem(to + ndev, ndev)
            copy = remote(mine, own3.at[:, at], s_sem.at[5 + i], r_sem.at[5], (to // n_gy, to % n_gy))
            swaps.append((ok, came, copy))
    for ok, _, copy in swaps:
        start_if(ok, copy)
    lane8 = lane_iota((8, 128))
    first_lane, last_lane = lane8 == 0, lane8 == 127

    def close_edge(rows):
        edge = tcx[nct, rows, :]
        edge = jnp.where(~has_l & last_lane, pltpu.roll(tcx[0, rows, :], 127, 1), edge)
        edge = jnp.where(~has_r & first_lane, pltpu.roll(tcx[nct - 1, rows, :], 1, 1), edge)
        tcx[nct, rows, :] = edge

    for k in range(hb, hb + n_gy):
        for j in range(nct + 1):
            tcx[j, rpd * k : rpd * k + rpd, :] = trecv[k, :, 128 * j : 128 * j + 128]
    for c in range(8, 8 + ch, 8):
        close_edge(slice(c, c + 8))
    half = lane8 // 2
    step = jnp.where(lane8 % 2 == 0, -1, 1)
    lo_g, lo_h = half, jnp.maximum(half + step, 0)
    hi_g, hi_h = half + 64, jnp.minimum(half + 64 + step, 127)
    ed_g = jnp.where(lane8 < 64, half, half + 64)
    ed_h = jnp.minimum(jnp.maximum(ed_g + step, 0), 127)

    def before(tiles):
        turned = [pltpu.roll(x, 1, 1) for x in tiles]
        return [jnp.where(first_lane, turned[t - 1], turned[t]) for t in range(len(tiles))]

    def after(tiles):
        turned = [pltpu.roll(x, 127, 1) for x in tiles]
        n = len(tiles)
        return [jnp.where(last_lane, turned[(t + 1) % n], turned[t]) for t in range(n)]

    def above(ref, s):
        return ref[8 * s - 1 : 8 * s + 7, :] if s else pltpu.roll(ref[0:8, :], 1, 0)

    def heat_x(s):
        rows = slice(8 * s, 8 * s + 8)
        for t in range(ntile):
            tx[t, rows, :] = 0.3 * (fine[t, rows, :] + above(fine.at[t], s))

    def prolong(p):
        c = 8 * p + 4
        for j in range(nct + 1):
            here = 0.75 * tcx[j, c : c + 8, :]
            widebuf[j, pl.ds(16 * p, 8, stride=2), :] = here + 0.25 * tcx[j, c - 1 : c + 7, :]
            widebuf[j, pl.ds(16 * p + 1, 8, stride=2), :] = here + 0.25 * tcx[j, c + 1 : c + 9, :]
        for s in (2 * p, 2 * p + 1):
            rows = slice(8 * s, 8 * s + 8)
            r = [widebuf[j, rows, :] for j in range(nct + 1)]
            fwd = [pltpu.roll(x, 1, 1) for x in r]
            bwd = [pltpu.roll(x, 127, 1) for x in r]
            f = []
            for j in range(nct):
                f.append(
                    0.75 * pick(r[j], lo_g)
                    + 0.25 * jnp.where(first_lane, fwd[j - 1], pick(r[j], lo_h))
                )
                f.append(
                    0.75 * pick(r[j], hi_g)
                    + 0.25 * jnp.where(last_lane, bwd[j + 1], pick(r[j], hi_h))
                )
            e = pick(r[nct], ed_h)
            e = jnp.where(first_lane, fwd[nct - 1], jnp.where(last_lane, bwd[0], e))
            f.append(0.75 * pick(r[nct], ed_g) + 0.25 * e)
            prev = before(f)
            for t in range(ntile):
                fine[t, rows, :] = f[t]
                ty[t, rows, :] = 0.3 * (f[t] + prev[t])

    npair = nstrip // 2
    for p in range(1, npair - 1):
        prolong(p)
    for s in range(2, nstrip - 2):
        heat_x(s)

    for h in (1, 2):
        done_if(n_h == h, r_sem.at[0], h * size(pk.at[0]))

    def unpack(got_l, got_r, rows, outside):
        shape = got_l.shape
        lanes = lane_iota(shape)
        gone = outside | (~has_l & (lanes >= 64)) | (~has_r & (lanes < 64))
        for f in range(FIELDS):
            from_r = pltpu.roll(got_r, 128 - 8 * f, 1) if f else got_r
            from_l = pltpu.roll(got_l, 120 - 8 * f, 1)
            side = jnp.where(lanes < 8, from_r, jnp.where(lanes >= 120, from_l, 0.0))
            side = jnp.where(gone, 0.0, side)
            if f < 6:
                ref, c = fields[f]
                ref[c, nt, rows, :] = side
            else:
                kh[rows, :] = side

    unpack(rk[0], rk[1], own_r, False)
    for i, rows in enumerate(keeps):
        for f, (ref, c) in enumerate(fields):
            keep[i, f, nt] = ref[c, nt, rows, :]

    def edges(s):
        rows = slice(8 * s, 8 * s + 8)
        u0 = [su[0, t, rows, :] for t in range(ntile)]
        u1 = [su[1, t, rows, :] for t in range(ntile)]
        k_main, k_side = kw[rows, :], kh[rows, :]
        b0, b1 = before(u0), before(u1)
        ay, ny = [], []
        for t in range(ntile):
            k = k_main if t < nt else k_side
            open_x = u0[t] - above(su.at[0, t], s) - tx[t, rows, :]
            st = jnp.maximum(open_x, 0.0)
            sp = jnp.minimum(ss[0, t, rows, :], jnp.exp2(st * st * k))
            ss[0, t, rows, :] = sp
            nx[0, t, rows, :] = sp * open_x
            nx[1, t, rows, :] = sp * (u1[t] - above(su.at[1, t], s))
            open_y = u1[t] - b1[t] - ty[t, rows, :]
            st = jnp.maximum(open_y, 0.0)
            sp = jnp.minimum(ss[1, t, rows, :], jnp.exp2(st * st * k))
            ss[1, t, rows, :] = sp
            ny.append(sp * open_y)
            ay.append(sp * (u0[t] - b0[t]))
        fy0 = [a - b for a, b in zip(after(ay), ay)]
        fy1 = [a - b for a, b in zip(after(ny), ny)]
        return fy0, fy1

    def advance(s, fy):
        rows = slice(8 * s, 8 * s + 8)
        below = slice(8 * s + 1, 8 * s + 9)
        for c in range(2):
            for t in range(ntile):
                force = (nx[c, t, below, :] - nx[c, t, rows, :]) + fy[c][t]
                v = 0.98 * sv[c, t, rows, :] + 0.16 * force
                sv[c, t, rows, :] = v
                su[c, t, rows, :] = su[c, t, rows, :] + v

    def interior(i, carry):
        old = None
        for s in range(2, nstrip - 2):
            if s == nstrip - 4:
                for c in range(2):
                    for t in range(ntile):
                        hist_u[i, c, t] = su[c, t, 8 * s : 8 * s + 8, :]
            new = edges(s)
            if s == 3:
                for c in range(2):
                    for t in range(ntile):
                        hist_n[i, c, t] = nx[c, t, 8 * s : 8 * s + 8, :]
            if old:
                advance(s - 1, old)
            old = new
        advance(nstrip - 3, old)
        return carry

    lax.fori_loop(0, SUBSTEPS, interior, 0)

    far_size = hb * size(trecv.at[0])
    for v in (1, 2):
        for h in (1, 2):
            done_if(
                (n_v == v) & (n_h == h),
                r_sem.at[2],
                v * (size(rowsend.at[0]) + far_size + h * size(ck.at[0])),
            )
    for side, (here, at, slot, line) in enumerate(
        ((has_u, 0, 0, 8), (has_d, ch + 8, hb + n_gy, ch + 7))
    ):

        @pl.when(here)
        def _():
            for k in range(hb):
                for j in range(nct + 1):
                    tcx[j, at + rpd * k : at + rpd * k + rpd, :] = trecv[
                        slot + k, :, 128 * j : 128 * j + 128
                    ]
            close_edge(slice(at, at + 8))

        @pl.when(jnp.logical_not(here))
        def _():
            for j in range(nct + 1):
                tcx[j, at : at + 8, :] = jnp.broadcast_to(tcx[j, line : line + 1, :], (8, 128))

    prolong(0)
    prolong(npair - 1)
    for s in (0, 1, 2, nstrip - 2, nstrip - 1):
        heat_x(s)

    for side, (here, at) in enumerate(((has_u, 0), (has_d, hh + HALO))):
        rows = slice(at, at + 8)
        for f, (ref, c) in enumerate(fields):
            for t in range(nt):
                ref[c, t, rows, :] = jnp.where(here, rowrecv[side, nt * f + t], 0.0)
        kw[rows, :] = jnp.where(here, rowrecv[side, 6 * nt], 0.0)
        unpack(ck[2 * side], ck[2 * side + 1], rows, ~here)
    for i, rows in enumerate(keeps):
        for f, (ref, c) in enumerate(fields):
            for t in range(ntile):
                ref[c, t, rows, :] = keep[i, f, t]
    line = frows - 25
    final = [[su[c, t, line : line + 1, :] for t in range(ntile)] for c in range(2)]
    for c in range(2):
        for t in range(ntile):
            hist_n[SUBSTEPS, c, t, 0:1, :] = final[c][t]

    def border(i, carry):
        for c in range(2):
            for t in range(ntile):
                nx[c, t, 24:32, :] = hist_n[i, c, t]
                su[c, t, line : line + 1, :] = hist_u[i, c, t, 7:8, :]
        for at in (0, nstrip - 3):
            old = None
            for s in range(at, at + 3):
                new = edges(s)
                if old:
                    advance(s - 1, old)
                old = new
            advance(at + 2, old)
        return carry

    lax.fori_loop(0, SUBSTEPS, border, 0)
    for c in range(2):
        for t in range(ntile):
            su[c, t, line : line + 1, :] = hist_n[SUBSTEPS, c, t, 0:1, :]

    for t in range(nt):
        gcol = gy * ww + 128 * t + lane
        dam_x = jnp.where(grow >= 1, 1.0 - ss[0, t, own_r, :], 0.0)
        dam_y = jnp.where(gcol >= 1, 1.0 - ss[1, t, own_r, :], 0.0)
        gap[t] = dam_x + dam_y
        o_dam[0, t] = dam_x.astype(jnp.bfloat16)
        o_dam[1, t] = dam_y.astype(jnp.bfloat16)
    rows2 = jnp.concatenate(
        [
            gap[t, pl.ds(0, ch, stride=2), :] + gap[t, pl.ds(1, ch, stride=2), :]
            for t in range(ww // 128)
        ],
        axis=1,
    )
    pairs = ww // 256
    glow = full_dot(
        jnp.concatenate([rows2[:, 256 * t : 256 * t + 256] for t in range(pairs)], axis=0), tab_s[...]
    )
    resist = jnp.concatenate([glow[ch * t : ch * t + ch] for t in range(pairs)], axis=1)
    t_tile = jnp.concatenate([tcx[j, 8 : 8 + ch, :] for j in range(nct)], axis=1)
    cond = (1.0 + 0.5 * t_tile) / (1.0 + resist)
    for j in range(nct):
        cpad[j, 8 : 8 + ch, :] = cond[:, 128 * j : 128 * j + 128]
    erow[0] = cond[0:1, :]
    erow[1] = cond[ch - 1 : ch, :]
    first_col, last_col = cond[0:8, 0:128], pltpu.roll(cond[0:8, cw - 128 : cw], 1, 1)
    for i in range(1, ch // 8):
        rows = slice(8 * i, 8 * i + 8)
        here = lane8 == i
        first_col = jnp.where(here, pltpu.roll(cond[rows, 0:128], i, 1), first_col)
        last_col = jnp.where(here, pltpu.roll(cond[rows, cw - 128 : cw], i + 1, 1), last_col)
    ecol[0] = first_col
    ecol[1] = last_col
    beside = [
        (has_u, has_d, remote(erow.at[0], grow_c.at[1], s_sem.at[1], r_sem.at[6], (up, gy))),
        (has_d, has_u, remote(erow.at[1], grow_c.at[0], s_sem.at[2], r_sem.at[6], (down, gy))),
        (has_l, has_r, remote(ecol.at[0], gcol_c.at[1], s_sem.at[3], r_sem.at[6], (gx, left))),
        (has_r, has_l, remote(ecol.at[1], gcol_c.at[0], s_sem.at[4], r_sem.at[6], (gx, right))),
    ]
    for ok, _, copy in beside:
        start_if(ok, copy)
    for b in range(n_gy):
        cb4[b] = cond[rpd * b : rpd * b + rpd, :]
    my_cols = pl.ds(pl.multiple_of(gy * cw, 128), cw)
    to_owner = []
    for t in range(n_gy):
        lo, hi = max(0, t - hz), min(n_gy, t + hz + 1)
        src = cb4.at[pl.ds(lo, hi - lo)]
        dst = owc.at[pl.ds(lo - t + hz, hi - lo), :, my_cols]
        to_owner.append((gy != t, remote(src, dst, s_sem.at[0], r_sem.at[7], (gx, t))))
        here = pltpu.make_async_copy(src, dst, r_sem.at[7])

        @pl.when(gy == t)
        def _():
            here.start()

    for t in range(hz):
        n = hz - t
        src, dst = cb4.at[pl.ds(n_gy - n, n)], owc.at[pl.ds(0, n), :, my_cols]
        to_owner.append((has_d, remote(src, dst, s_sem.at[2], r_sem.at[7], (down, t))))
        src, dst = cb4.at[pl.ds(0, n)], owc.at[pl.ds(2 * hz + 1 - n, n), :, my_cols]
        to_owner.append((has_u, remote(src, dst, s_sem.at[1], r_sem.at[7], (up, n_gy - 1 - t))))
    for ok, copy in to_owner:
        start_if(ok, copy)

    for c in range(2):
        for t in range(nt):
            o_speed[c, t] = 2.5 * sv[c, t, own_r, :]

    pltpu.make_async_copy(arecv, arecv, r_sem.at[4]).wait()
    for k in range(n_gy):
        for j in range(nct):
            base_t[j, rpd * k : rpd * k + rpd, :] = arecv[k, :, 128 * j : 128 * j + 128]
    for v in (1, 2):
        for h in (1, 2):
            done_if(
                (n_v == v) & (n_h == h),
                r_sem.at[6],
                v * size(erow.at[0]) + h * size(ecol.at[0]),
            )
    for j in range(nct):
        cols = slice(128 * j, 128 * j + 128)
        cpad[j, 7:8, :] = jnp.where(has_u, grow_c[0, :, cols], 0.0)
        cpad[j, 8 + ch : 9 + ch, :] = jnp.where(has_d, grow_c[1, :, cols], 0.0)
    from_l, from_r = gcol_c[0], gcol_c[1]
    sub8 = row_iota((8, 128))
    peak = None
    for i in range(ch // 8):
        r0 = 8 + 8 * i
        mid = [cpad[j, r0 : r0 + 8, :] for j in range(nct)]
        fwd = [pltpu.roll(x, 1, 1) for x in mid]
        bwd = [pltpu.roll(x, 127, 1) for x in mid]
        fwd_in = [pltpu.roll(from_l, 128 - i, 1) if i else from_l] + fwd[:-1]
        bwd_in = bwd[1:] + [pltpu.roll(from_r, 127 - i, 1)]
        for j in range(nct):
            c = mid[j]
            f_u = c + cpad[j, r0 - 1 : r0 + 7, :]
            f_d = c + cpad[j, r0 + 1 : r0 + 9, :]
            f_l = c + jnp.where(first_lane, fwd_in[j], fwd[j])
            f_r = c + jnp.where(last_lane, bwd_in[j], bwd[j])
            if i == 0:
                f_u = jnp.where(~has_u & (sub8 == 0), 0.0, f_u)
            if i == ch // 8 - 1:
                f_d = jnp.where(~has_d & (sub8 == 7), 0.0, f_d)
            if j == 0:
                f_l = jnp.where(~has_l & first_lane, 0.0, f_l)
            if j == nct - 1:
                f_r = jnp.where(~has_r & last_lane, 0.0, f_r)
            off = 0.5 * ((f_u + f_d) + (f_l + f_r))
            ratio = off / (base_t[j, 8 * i : 8 * i + 8, :] + off)
            peak = ratio if peak is None else jnp.maximum(peak, ratio)
    msend[...] = jnp.full((1, 128), jnp.max(peak), F32)

    for k in range(1, ndev):
        t = lax.rem(me + k, ndev)
        remote(
            msend, mrecv.at[k - 1], s_sem.at[0], r_sem.at[8], (t // n_gy, t % n_gy)
        ).start()

    orows = 16
    n_swap = sum(jnp.where(came, 1, 0) for _, came, _ in swaps)
    for n in range(1, 2 * hz + 1):
        done_if(n_swap == n, r_sem.at[5], n * size(mine))
    reach = hz * rpd

    def gather(q, ref, fill):
        for b in range(2 * hz + 1):
            value = ref[b]
            if b != hz:
                there = me >= hz - b if b < hz else me + (b - hz) < ndev
                value = jnp.where(there, value, fill)
            field[q, rpd * b : rpd * b + rpd, :] = value

    for q in range(3):
        gather(q, own3.at[q], 1.0)
    rest = (2 * hz + 1) * rpd
    for q in range(4):
        field[q, rest:orows, :] = jnp.full((orows - rest, span), 0.0 if q == 3 else 1.0, F32)

    short_t = jnp.where(gx == 0, jnp.maximum(hz - gy, 0), 0)
    short_b = jnp.where(gx == n_gx - 1, jnp.maximum(hz - (n_gy - 1 - gy), 0), 0)
    for a in range(hz + 1):
        for b in range(hz + 1):
            got = owc.at[pl.ds(a, 2 * hz + 1 - a - b)]

            @pl.when((short_t == a) & (short_b == b))
            def _():
                pltpu.make_async_copy(got, got, r_sem.at[7]).wait()

    gather(3, owc, 0.0)
    oshape = (orows, span)
    row_g = me * rpd - reach + row_iota(oshape)
    col_g = lane_iota(oshape)
    total_rows = ndev * rpd

    def four(x):
        return (
            pltpu.roll(x, 1, 0),
            pltpu.roll(x, orows - 1, 0),
            pltpu.roll(x, 1, 1),
            pltpu.roll(x, span - 1, 1),
        )

    inside = (row_g >= 0) & (row_g < total_rows)
    masks = (
        inside & (row_g >= 1),
        inside & (row_g <= total_rows - 2),
        col_g >= 1,
        col_g <= span - 2,
    )
    cond = field[3]
    faces = [jnp.where(m, 0.5 * (cond + nb), 0.0) for m, nb in zip(masks, four(cond))]
    diagonal = field[1] + (faces[0] + faces[1] + faces[2] + faces[3])
    inv = 1.0 / diagonal
    t_all = field[0]
    near = sum(f * nb for f, nb in zip(faces, four(t_all)))
    z = (field[2] - (diagonal * t_all - near)) * inv
    faces = [f * inv for f in faces]
    for j in range(4):
        if j:
            z = z - sum(f * nb for f, nb in zip(faces, four(z)))
        zown[j] = z[reach : reach + rpd, :]

    pltpu.make_async_copy(mrecv, mrecv, r_sem.at[8]).wait()
    peak = jnp.maximum(jnp.max(mrecv[...], axis=0), msend[...])[0:1, :]
    low, high = 1.0 - peak, 1.0 + peak
    center = 0.5 * (high + low)
    spread = 0.5 * (high - low)
    sigma = center / spread
    rho = 1.0 / sigma
    zero = jnp.zeros_like(center)
    e = [zero + 1.0, zero, zero, zero]
    d = [1.0 / center, zero, zero, zero]
    total = list(d)
    for _ in range(3):
        e = [e[0]] + [e[i] - d[i - 1] for i in range(1, 4)]
        rho_next = 1.0 / (2.0 * sigma - rho)
        d = [rho_next * rho * d[i] + (2.0 * rho_next / spread) * e[i] for i in range(4)]
        total = [a + b for a, b in zip(total, d)]
        rho = rho_next
    for t in range(span // 128):
        cols = slice(128 * t, 128 * t + 128)
        x = warm[:, cols]
        for j in range(4):
            x = x + total[j] * zown[j, :, cols]
        o_warm[:, cols] = x

    for ok, _, copy in swaps:
        sent_if(ok, copy)
    always = (n_gy - 1) * (size(tsend.at[0]) + size(asend.at[0])) + (ndev - 1)
    blocks = [min(n_gy, t + hz + 1) - max(0, t - hz) for t in range(n_gy)]
    one = size(cb4.at[0])
    for t in range(n_gy):
        done_if(gy == t, s_sem.at[0], always + one * (sum(blocks) - blocks[t]))
    tall = size(rowsend.at[0]) + far_size + size(erow.at[0]) + one * (hz * (hz + 1) // 2)
    for i, ok in ((1, has_u), (2, has_d)):
        for h in (1, 2):
            done_if(ok & (n_h == h), s_sem.at[i], tall + h * size(ck.at[0]))
    for i, ok in ((3, has_l), (4, has_r)):
        done_if(ok, s_sem.at[i], size(pk.at[0]) + size(ecol.at[0]))


def put_out(su, speed, dam, warm, o_shift, o_speed, o_dam, o_warm, sem):
    nt, hh = dam.shape[1:3]
    for t in range(nt):
        cols = slice(128 * t, 128 * t + 128)
        for i, (src, dst) in enumerate(
            (
                (su.at[:, t, HALO : HALO + hh, :], o_shift.at[:, :, cols]),
                (speed.at[:, t], o_speed.at[:, :, cols]),
                (dam.at[:, t], o_dam.at[:, :, cols]),
            )
        ):
            pltpu.make_async_copy(src, dst, sem.at[i]).start()
    last = pltpu.make_async_copy(warm, o_warm, sem.at[3])
    last.start()
    for i, dst in enumerate((o_shift, o_speed, o_dam)):
        pltpu.make_async_copy(dst, dst, sem.at[i]).wait()
    last.wait()


def per_device(n_gx, n_gy, shift, speed, level, mark, warm, store, film, bath):
    _, hh, ww = shift.shape
    rpd, _ = warm.shape
    cw, ch = ww // 2, hh // 2
    wide = cw + 128
    nt, nct = ww // 128, cw // 128
    ntile = nt + 1
    crows, frows = ch + 16, hh + 2 * HALO
    nsl = n_gy + 2 * (HALO // rpd)
    hz = HALO // 2 // rpd
    vm = lambda *s: pltpu.VMEM(s, F32)
    dma = lambda n: pltpu.SemaphoreType.DMA((n,))
    hbm = pl.BlockSpec(memory_space=pltpu.HBM)
    vmem = pl.BlockSpec(memory_space=pltpu.VMEM)
    outs = pl.pallas_call(
        functools.partial(kernel, n_gx, n_gy),
        out_shape=(
            vm(2, ntile, frows, 128),
            vm(2, nt, hh, 128),
            pltpu.VMEM((2, nt, hh, 128), jnp.bfloat16),
            vm(*warm.shape),
        ),
        in_specs=[hbm] * 8,
        out_specs=(vmem,) * 4,
        scratch_shapes=[
            vm(n_gy, rpd, wide),
            vm(nsl, rpd, wide),
            vm(n_gy, rpd, cw),
            vm(n_gy, rpd, cw),
            vm(2, hh, 128),
            vm(2, hh, 128),
            vm(4, 8, 128),
            vm(2, 6 * nt + 1, 8, 128),
            vm(2, 6 * nt + 1, 8, 128),
            vm(2, 6, ntile, 8, 128),
            vm(SUBSTEPS + 1, 2, ntile, 8, 128),
            vm(SUBSTEPS, 2, ntile, 8, 128),
            pltpu.VMEM(level.shape, level.dtype),
            vm(*warm.shape),
            vm(*warm.shape),
            vm(*warm.shape),
            vm(*warm.shape),
            vm(2, ntile, frows, 128),
            vm(2, ntile, frows, 128),
            vm(frows, 128),
            vm(frows, 128),
            vm(ntile, frows, 128),
            vm(ntile, frows, 128),
            vm(ntile, frows, 128),
            vm(2, ntile, frows + 8, 128),
            vm(nct + 1, crows, 128),
            vm(nct + 1, frows, 128),
            vm(256, 128),
            vm(nt, hh, 128),
            vm(nct, ch, 128),
            vm(nct, crows, 128),
            vm(2, 1, cw),
            vm(2, 1, cw),
            vm(2, 8, 128),
            vm(2, 8, 128),
            vm(n_gy, rpd, cw),
            vm(2 * hz + 1, rpd, cw * n_gy),
            vm(3, 2 * hz + 1, rpd, cw * n_gy),
            vm(4, 16, cw * n_gy),
            vm(4, rpd, cw * n_gy),
            vm(1, 128),
            vm(n_gx * n_gy - 1, 1, 128),
            dma(5 + 2 * hz),
            dma(12),
            vm(3 * level.size // 128, 1, 128),
            pltpu.SMEM((1, hh // SR), mark.dtype),
        ],
        compiler_params=pltpu.CompilerParams(
            collective_id=0, has_side_effects=True
        ),
    )(shift, speed, level, mark.reshape(1, hh // SR), warm, store, film, bath)
    return pl.pallas_call(
        put_out,
        out_shape=tuple(
            jax.ShapeDtypeStruct(o.shape, d)
            for o, d in ((shift, F32), (speed, F32), (level, jnp.bfloat16), (warm, F32))
        ),
        in_specs=[vmem] * 4,
        out_specs=(hbm,) * 4,
        scratch_shapes=[dma(4)],
    )(*(pltpu.with_memory_space_constraint(o, pltpu.VMEM) for o in outs))


def solution(mesh):
    rows = P(("gx", "gy"), None)
    plate = P(None, "gx", "gy")
    return jax.shard_map(
        functools.partial(per_device, mesh.shape["gx"], mesh.shape["gy"]),
        mesh=mesh,
        in_specs=(plate, plate, plate, P("gx", "gy"), rows, rows, rows, rows),
        out_specs=(plate, plate, plate, rows),
        check_vma=False,
    )
```

```python
import functools
import math

import jax
import jax.numpy as jnp
from jax import lax
from jax.experimental import pallas as pl
from jax.experimental.pallas import tpu as pltpu
from jax.sharding import PartitionSpec as P

SR = 8
SEG = 128
SUBSTEPS = 8
HALO = 8
FIELDS = 7
MESH = pl.DeviceIdType.MESH
F32 = jnp.float32


def lane_iota(shape):
    return lax.broadcasted_iota(jnp.int32, shape, 1)


def row_iota(shape):
    return lax.broadcasted_iota(jnp.int32, shape, 0)


def full_dot(a, b):
    return jnp.dot(a, b, precision=lax.Precision.HIGHEST, preferred_element_type=F32)


def partner(me, k, n):
    if n & (n - 1):
        return lax.rem(me + k, n)
    t = me
    for b in range(n.bit_length() - 1):
        if k >> b & 1:
            t = t + (1 - 2 * (me // 2**b % 2)) * 2**b
    return t


def far_first(n, hops):
    return sorted(range(1, n), key=lambda k: (-hops(k), -k))


def pick(x, index):
    return jnp.take_along_axis(x, index, axis=1)


def kernel(
    n_gx,
    n_gy,
    shift,
    speed,
    level_h,
    mark_h,
    warm_h,
    store_h,
    film_h,
    bath_h,
    su,
    o_speed,
    o_dam,
    o_warm,
    tsend,
    trecv,
    asend,
    arecv,
    pk,
    rk,
    ck,
    rowsend,
    rowrecv,
    bu,
    bv,
    bs,
    bn,
    past,
    past_n,
    level,
    warm,
    store,
    film,
    bath,
    sv,
    ss,
    kw,
    kh,
    tx,
    ty,
    fine,
    nx,
    tcx,
    widebuf,
    tab_s,
    gap,
    base_t,
    cpad,
    erow,
    grow_c,
    ecol,
    gcol_c,
    cb4,
    owc,
    own3,
    field,
    zown,
    msend,
    mrecv,
    s_sem,
    r_sem,
    meter,
    mark,
):
    ndev = n_gx * n_gy
    gx = lax.axis_index("gx")
    gy = lax.axis_index("gy")
    me = gx * n_gy + gy
    _, hh, ww = shift.shape
    rpd, _ = warm_h.shape
    cw = ww // 2
    ch = hh // 2
    hb = HALO // rpd
    nsl = n_gy + 2 * hb
    nt = ww // 128
    ntile = nt + 1
    nct = cw // 128
    frows = hh + 2 * HALO
    nstrip = frows // 8
    up = lax.rem(gx + n_gx - 1, n_gx)
    down = lax.rem(gx + 1, n_gx)
    left = lax.rem(gy + n_gy - 1, n_gy)
    right = lax.rem(gy + 1, n_gy)
    has_u, has_d = gx > 0, gx < n_gx - 1
    has_l, has_r = gy > 0, gy < n_gy - 1
    hz = HALO // 2 // rpd
    span = cw * n_gy
    own_r = slice(HALO, HALO + hh)

    n_v = jnp.where(has_u, 1, 0) + jnp.where(has_d, 1, 0)
    n_h = jnp.where(has_l, 1, 0) + jnp.where(has_r, 1, 0)

    def size(ref):
        return math.prod(ref.shape) // 128

    def done(sem, lines):
        part = meter.at[pl.ds(0, lines)]
        pltpu.make_async_copy(part, part, sem).wait()

    def done_if(cond, sem, lines):
        if lines:

            @pl.when(cond)
            def _():
                done(sem, lines)

    barrier = pltpu.get_barrier_semaphore()
    warm_load = pltpu.make_async_copy(warm_h, warm, r_sem.at[9])
    warm_load.start()

    def greet(a, b):
        pl.semaphore_signal(barrier, inc=1, device_id=(a, b), device_id_type=MESH)

    for k in far_first(n_gy, lambda k: k // 2):
        greet(gx, partner(gy, k, n_gy))
    for k in range(1, n_gx):
        greet(lax.rem(gx + k, n_gx), gy)
    for a in (up, down):
        for b in (left, right):
            greet(a, b)

    loads = [
        pltpu.make_async_copy(src, dst, r_sem.at[i])
        for src, dst, i in (
            (mark_h, mark, 1),
            (level_h, level, 10),
            (store_h, store, 11),
            (film_h, film, 11),
            (bath_h, bath, 11),
        )
    ]
    loads[0].start()
    loads[1].start()
    for src, dst in ((shift, su), (speed, sv)):
        for t in range(nt):
            pltpu.make_async_copy(
                src.at[:, :, 128 * t : 128 * t + 128], dst.at[:, t, own_r, :], r_sem.at[10]
            ).start()
    for copy in loads[2:]:
        copy.start()

    lane_c = lane_iota((rpd, 128))

    def chunk(value, k):
        after = value[:, (cw * (k + 1)) % (cw * n_gy) :][:, 0:128]
        before = value[:, (cw * k - 128) % (cw * n_gy) :][:, 0:128]
        return value[:, cw * k : cw * k + cw], jnp.where(lane_c < 64, after, before)

    def remote(src, dst, ssem, rsem, where):
        return pltpu.make_async_remote_copy(
            src_ref=src, dst_ref=dst, send_sem=ssem, recv_sem=rsem, device_id=where,
            device_id_type=MESH,
        )

    warm_load.wait()
    t_own = warm[...]
    for k in range(n_gy):
        main, edge = chunk(t_own, k)
        tsend[k, :, 0:cw] = main
        tsend[k, :, cw : cw + 128] = edge

    pl.semaphore_wait(barrier, n_gy + n_gx + 2)

    for k in far_first(n_gy, lambda k: k // 2):
        t = partner(gy, k, n_gy)
        remote(tsend.at[t], trecv.at[gy + hb], s_sem.at[0], r_sem.at[3], (gx, t)).start()
    pltpu.make_async_copy(tsend.at[gy], trecv.at[gy + hb], r_sem.at[3]).start()

    sharp = -4.0 * math.log2(math.e)
    lane = lane_iota((hh, 128))
    loads[0].wait()
    done(r_sem.at[10], 3 * size(level))
    for s in range(hh // SR):
        kw[HALO + SR * s : HALO + SR * s + SR, :] = (
            jnp.full((SR, 128), mark[0, s], jnp.int32).astype(F32) * sharp
        )
    w_own = kw[own_r, :] * (0.125 / sharp)
    grow = gx * hh + row_iota((hh, 128))
    for t in range(nt):
        cols = slice(128 * t, 128 * t + 128)
        gcol = gy * ww + 128 * t + lane
        ss[0, t, own_r, :] = jnp.where(grow >= 1, 1.0 - level[0, :, cols].astype(F32) * w_own, 0.0)
        ss[1, t, own_r, :] = jnp.where(gcol >= 1, 1.0 - level[1, :, cols].astype(F32) * w_own, 0.0)
    for c in range(2):
        for t in range(nt):
            sv[c, t, own_r, :] = 0.4 * sv[c, t, own_r, :]
    acc_l = jnp.zeros((hh, 128), F32)
    acc_r = jnp.zeros((hh, 128), F32)
    fields = [(ref, c) for ref in (su, sv, ss) for c in range(2)]
    for f in range(FIELDS):
        if f < 6:
            ref, c = fields[f]
            first, last = ref[c, 0, own_r, :], ref[c, nt - 1, own_r, :]
        else:
            first = last = kw[own_r, :]
        here = (lane >= 8 * f) & (lane < 8 * f + 8)
        first = pltpu.roll(first, 8 * f, 1) if f else first
        acc_l = jnp.where(here, first, acc_l)
        acc_r = jnp.where(here, pltpu.roll(last, 8 * f + 8, 1), acc_r)
    pk[0] = acc_l
    pk[1] = acc_r
    side_l = remote(pk.at[0], rk.at[1], s_sem.at[3], r_sem.at[0], (gx, left))
    side_r = remote(pk.at[1], rk.at[0], s_sem.at[4], r_sem.at[0], (gx, right))
    top, end = slice(0, 8), slice(hh - 8, hh)
    corners = [
        (has_u & has_l, remote(pk.at[0, top], ck.at[3], s_sem.at[1], r_sem.at[2], (up, left)), 2),
        (has_u & has_r, remote(pk.at[1, top], ck.at[2], s_sem.at[1], r_sem.at[2], (up, right)), 3),
        (has_d & has_l, remote(pk.at[0, end], ck.at[1], s_sem.at[2], r_sem.at[2], (down, left)), 4),
        (has_d & has_r, remote(pk.at[1, end], ck.at[0], s_sem.at[2], r_sem.at[2], (down, right)), 5),
    ]
    rows_u = remote(rowsend.at[0], rowrecv.at[1], s_sem.at[1], r_sem.at[2], (up, gy))
    rows_d = remote(rowsend.at[1], rowrecv.at[0], s_sem.at[2], r_sem.at[2], (down, gy))
    sends = [(has_l, side_l), (has_r, side_r)] + [(a, b) for a, b, _ in corners]
    sends += [(has_u, rows_u), (has_d, rows_d)]

    def start_if(cond, copy):
        @pl.when(cond)
        def _():
            copy.start()

    def sent_if(cond, copy):
        @pl.when(cond)
        def _():
            copy.wait_send()

    for cond, copy in sends[0:6]:
        start_if(cond, copy)
    for side, at in ((0, HALO), (1, HALO + hh - 8)):
        for f, (ref, c) in enumerate(fields):
            for t in range(nt):
                rowsend[side, nt * f + t] = ref[c, t, at : at + 8, :]
        rowsend[side, 6 * nt] = kw[at : at + 8, :]
    for cond, copy in sends[6:8]:
        start_if(cond, copy)

    k_i, n_i = row_iota((256, 128)), lane_iota((256, 128))
    pos = (k_i % SEG).astype(F32)
    col = (2 * (n_i % 64)).astype(F32)
    tab = jnp.exp(jnp.abs(pos - col) * (-4.0 / SEG)) + jnp.exp(jnp.abs(pos - col - 1.0) * (-4.0 / SEG))
    tab_s[...] = jnp.where(k_i // SEG == n_i // 64, tab * (1.0 / SEG), 0.0)
    done(r_sem.at[11], 3 * size(store))
    base = store[...] + film[...]
    own3[0, hz] = t_own
    own3[1, hz] = base
    own3[2, hz] = store[...] * t_own + film[...] * bath[...]
    for k in range(n_gy):
        asend[k] = base[:, cw * k : cw * k + cw]
    strip = (nstrip - 2) * 8
    nx[:, :, strip : strip + 8, :] = jnp.zeros((2, ntile, 8, 128), F32)
    bn[:, :, :, 32:40, :] = jnp.zeros((2, 2, ntile, 8, 128), F32)

    mid = trecv.at[pl.ds(hb, n_gy)]
    pltpu.make_async_copy(mid, mid, r_sem.at[3]).wait()
    far_u = remote(
        trecv.at[pl.ds(hb, hb)], trecv.at[pl.ds(hb + n_gy, hb)], s_sem.at[1], r_sem.at[2], (up, gy)
    )
    far_d = remote(
        trecv.at[pl.ds(n_gy, hb)], trecv.at[pl.ds(0, hb)], s_sem.at[2], r_sem.at[2], (down, gy)
    )
    start_if(has_u, far_u)
    start_if(has_d, far_d)

    for k in range(1, n_gy):
        t = partner(gy, k, n_gy)
        remote(asend.at[t], arecv.at[gy], s_sem.at[0], r_sem.at[4], (gx, t)).start()
    pltpu.make_async_copy(asend.at[gy], arecv.at[gy], r_sem.at[4]).start()
    mine = own3.at[:, hz]
    swaps = []
    for d in range(1, hz + 1):
        for i, to, ok, came in (
            (d - 1, me + d, me + d < ndev, me >= d),
            (hz + d - 1, me - d, me >= d, me + d < ndev),
        ):
            at = hz - d if i < hz else hz + d
            to = lax.rem(to + ndev, ndev)
            copy = remote(mine, own3.at[:, at], s_sem.at[5 + i], r_sem.at[5], (to // n_gy, to % n_gy))
            swaps.append((ok, came, copy))
    for ok, _, copy in swaps:
        start_if(ok, copy)
    lane8 = lane_iota((8, 128))
    first_lane, last_lane = lane8 == 0, lane8 == 127

    def close_edge(rows):
        edge = tcx[nct, rows, :]
        edge = jnp.where(~has_l & last_lane, pltpu.roll(tcx[0, rows, :], 127, 1), edge)
        edge = jnp.where(~has_r & first_lane, pltpu.roll(tcx[nct - 1, rows, :], 1, 1), edge)
        tcx[nct, rows, :] = edge

    for k in range(hb, hb + n_gy):
        for j in range(nct + 1):
            tcx[j, rpd * k : rpd * k + rpd, :] = trecv[k, :, 128 * j : 128 * j + 128]
    for c in range(8, 8 + ch, 8):
        close_edge(slice(c, c + 8))
    half = lane8 // 2
    step = jnp.where(lane8 % 2 == 0, -1, 1)
    lo_g, lo_h = half, jnp.maximum(half + step, 0)
    hi_g, hi_h = half + 64, jnp.minimum(half + 64 + step, 127)
    ed_g = jnp.where(lane8 < 64, half, half + 64)
    ed_h = jnp.minimum(jnp.maximum(ed_g + step, 0), 127)

    def before(tiles):
        turned = [pltpu.roll(x, 1, 1) for x in tiles]
        return [jnp.where(first_lane, turned[t - 1], turned[t]) for t in range(len(tiles))]

    def after(tiles):
        turned = [pltpu.roll(x, 127, 1) for x in tiles]
        n = len(tiles)
        return [jnp.where(last_lane, turned[(t + 1) % n], turned[t]) for t in range(n)]

    def above(ref, s):
        return ref[8 * s - 1 : 8 * s + 7, :] if s else pltpu.roll(ref[0:8, :], 1, 0)

    def heat_x(s):
        rows = slice(8 * s, 8 * s + 8)
        for t in range(ntile):
            tx[t, rows, :] = 0.3 * (fine[t, rows, :] + above(fine.at[t], s))

    def prolong(p):
        c = 8 * p + 4
        for j in range(nct + 1):
            here = 0.75 * tcx[j, c : c + 8, :]
            widebuf[j, pl.ds(16 * p, 8, stride=2), :] = here + 0.25 * tcx[j, c - 1 : c + 7, :]
            widebuf[j, pl.ds(16 * p + 1, 8, stride=2), :] = here + 0.25 * tcx[j, c + 1 : c + 9, :]
        for s in (2 * p, 2 * p + 1):
            rows = slice(8 * s, 8 * s + 8)
            r = [widebuf[j, rows, :] for j in range(nct + 1)]
            fwd = [pltpu.roll(x, 1, 1) for x in r]
            bwd = [pltpu.roll(x, 127, 1) for x in r]
            f = []
            for j in range(nct):
                f.append(
                    0.75 * pick(r[j], lo_g)
                    + 0.25 * jnp.where(first_lane, fwd[j - 1], pick(r[j], lo_h))
                )
                f.append(
                    0.75 * pick(r[j], hi_g)
                    + 0.25 * jnp.where(last_lane, bwd[j + 1], pick(r[j], hi_h))
                )
            e = pick(r[nct], ed_h)
            e = jnp.where(first_lane, fwd[nct - 1], jnp.where(last_lane, bwd[0], e))
            f.append(0.75 * pick(r[nct], ed_g) + 0.25 * e)
            prev = before(f)
            for t in range(ntile):
                fine[t, rows, :] = f[t]
                ty[t, rows, :] = 0.3 * (f[t] + prev[t])

    npair = nstrip // 2
    for p in range(1, npair - 1):
        prolong(p)
    for s in range(2, nstrip - 2):
        heat_x(s)

    for h in (1, 2):
        done_if(n_h == h, r_sem.at[0], h * size(pk.at[0]))

    def unpack(got_l, got_r, targets, rows, lines, outside):
        shape = got_l.shape
        lanes = lane_iota(shape)
        gone = outside | (~has_l & (lanes >= 64)) | (~has_r & (lanes < 64))
        for f in range(FIELDS):
            from_r = pltpu.roll(got_r, 128 - 8 * f, 1) if f else got_r
            from_l = pltpu.roll(got_l, 120 - 8 * f, 1)
            side = jnp.where(lanes < 8, from_r, jnp.where(lanes >= 120, from_l, 0.0))
            side = jnp.where(gone, 0.0, side)
            if f < 6:
                ref, c = targets[f]
                ref[c, nt, rows, :] = side
            else:
                kh[lines, :] = side

    unpack(rk[0], rk[1], fields, own_r, own_r, False)
    rims = [
        [(ref.at[side], c) for ref in (bu, bv, bs) for c in range(2)] for side in range(2)
    ]
    for side, (at, to) in enumerate(((8, 8), (frows - 16, 16))):
        for (ref, c), (rim, _) in zip(fields, rims[side]):
            for t in range(ntile):
                rim[c, t, to : to + 8, :] = ref[c, t, at : at + 8, :]

    def edges(s):
        rows = slice(8 * s, 8 * s + 8)
        u0 = [su[0, t, rows, :] for t in range(ntile)]
        u1 = [su[1, t, rows, :] for t in range(ntile)]
        k_main, k_side = kw[rows, :], kh[rows, :]
        b0, b1 = before(u0), before(u1)
        ay, ny = [], []
        for t in range(ntile):
            k = k_main if t < nt else k_side
            open_x = u0[t] - above(su.at[0, t], s) - tx[t, rows, :]
            st = jnp.maximum(open_x, 0.0)
            sp = jnp.minimum(ss[0, t, rows, :], jnp.exp2(st * st * k))
            ss[0, t, rows, :] = sp
            nx[0, t, rows, :] = sp * open_x
            nx[1, t, rows, :] = sp * (u1[t] - above(su.at[1, t], s))
            open_y = u1[t] - b1[t] - ty[t, rows, :]
            st = jnp.maximum(open_y, 0.0)
            sp = jnp.minimum(ss[1, t, rows, :], jnp.exp2(st * st * k))
            ss[1, t, rows, :] = sp
            ny.append(sp * open_y)
            ay.append(sp * (u0[t] - b0[t]))
        fy0 = [a - b for a, b in zip(after(ay), ay)]
        fy1 = [a - b for a, b in zip(after(ny), ny)]
        return fy0, fy1

    def advance(s, fy):
        rows = slice(8 * s, 8 * s + 8)
        below = slice(8 * s + 1, 8 * s + 9)
        for c in range(2):
            for t in range(ntile):
                force = (nx[c, t, below, :] - nx[c, t, rows, :]) + fy[c][t]
                v = 0.98 * sv[c, t, rows, :] + 0.16 * force
                sv[c, t, rows, :] = v
                su[c, t, rows, :] = su[c, t, rows, :] + v

    def interior(i, carry):
        for f, (ref, c) in enumerate(fields):
            at = frows - 24 + (f == 4)
            for t in range(ntile):
                past[i, 0, f, t] = ref[c, t, 16:24, :]
                past[i, 1, f, t] = ref[c, t, at : at + 8, :]
        old = None
        for s in range(2, nstrip - 2):
            new = edges(s)
            if old:
                advance(s - 1, old)
            old = new
        advance(nstrip - 3, old)
        for c in range(2):
            for t in range(ntile):
                past_n[i, 0, c, t] = nx[c, t, 17:25, :]
                past_n[i, 1, c, t] = nx[c, t, frows - 24 : frows - 16, :]
        return carry

    lax.fori_loop(0, SUBSTEPS, interior, 0)

    far_size = hb * size(trecv.at[0])
    for v in (1, 2):
        for h in (1, 2):
            done_if(
                (n_v == v) & (n_h == h),
                r_sem.at[2],
                v * (size(rowsend.at[0]) + far_size + h * size(ck.at[0])),
            )
    for side, (here, at, slot, line) in enumerate(
        ((has_u, 0, 0, 8), (has_d, ch + 8, hb + n_gy, ch + 7))
    ):

        @pl.when(here)
        def _():
            for k in range(hb):
                for j in range(nct + 1):
                    tcx[j, at + rpd * k : at + rpd * k + rpd, :] = trecv[
                        slot + k, :, 128 * j : 128 * j + 128
                    ]
            close_edge(slice(at, at + 8))

        @pl.when(jnp.logical_not(here))
        def _():
            for j in range(nct + 1):
                tcx[j, at : at + 8, :] = jnp.broadcast_to(tcx[j, line : line + 1, :], (8, 128))

    prolong(0)
    prolong(npair - 1)
    for s in (0, 1, 2, nstrip - 2, nstrip - 1):
        heat_x(s)

    for side, (here, at, to) in enumerate(((has_u, 0, 0), (has_d, hh + HALO, 24))):
        rows = slice(to, to + 8)
        lines = slice(at, at + 8)
        for f, (rim, c) in enumerate(rims[side]):
            for t in range(nt):
                rim[c, t, rows, :] = jnp.where(here, rowrecv[side, nt * f + t], 0.0)
        kw[lines, :] = jnp.where(here, rowrecv[side, 6 * nt], 0.0)
        unpack(ck[2 * side], ck[2 * side + 1], rims[side], rows, lines, ~here)
    for t in range(ntile):
        bs[1, 0, t, 8:9, :] = ss[0, t, frows - 24 : frows - 23, :]

    def rim_edges(side, x, y):
        shift_by = (frows - 32) * side
        u, spring, flow = bu.at[side], bs.at[side], bn.at[side]
        ex, ex_up, ey = pl.ds(x, 8), pl.ds(x - 1, 8), pl.ds(y, 8)
        gx_rows, gy_rows = pl.ds(x + shift_by, 8), pl.ds(y + shift_by, 8)
        u0 = [u[0, t, ey, :] for t in range(ntile)]
        u1 = [u[1, t, ey, :] for t in range(ntile)]
        b0, b1 = before(u0), before(u1)
        kx = [kw[gx_rows, :], kh[gx_rows, :]]
        ky = [kw[gy_rows, :], kh[gy_rows, :]]
        ay, ny = [], []
        for t in range(ntile):
            open_x = u[0, t, ex, :] - u[0, t, ex_up, :] - tx[t, gx_rows, :]
            st = jnp.maximum(open_x, 0.0)
            sp = jnp.minimum(spring[0, t, ex, :], jnp.exp2(st * st * kx[t // nt]))
            spring[0, t, ex, :] = sp
            flow[0, t, ex, :] = sp * open_x
            flow[1, t, ex, :] = sp * (u[1, t, ex, :] - u[1, t, ex_up, :])
            open_y = u1[t] - b1[t] - ty[t, gy_rows, :]
            st = jnp.maximum(open_y, 0.0)
            sp = jnp.minimum(spring[1, t, ey, :], jnp.exp2(st * st * ky[t // nt]))
            spring[1, t, ey, :] = sp
            ny.append(sp * open_y)
            ay.append(sp * (u0[t] - b0[t]))
        fy0 = [a - b for a, b in zip(after(ay), ay)]
        fy1 = [a - b for a, b in zip(after(ny), ny)]
        return fy0, fy1

    def rim_advance(side, y, fy):
        rows, below = pl.ds(y, 8), pl.ds(y + 1, 8)
        for c in range(2):
            for t in range(ntile):
                force = (bn[side, c, t, below, :] - bn[side, c, t, rows, :]) + fy[c][t]
                v = 0.98 * bv[side, c, t, rows, :] + 0.16 * force
                bv[side, c, t, rows, :] = v
                bu[side, c, t, rows, :] = bu[side, c, t, rows, :] + v

    for i in range(SUBSTEPS):
        for t in range(ntile):
            for f in range(6):
                rim, c = rims[0][f]
                rim[c, t, 16 + i : 17 + i, :] = past[i, 0, f, t, i : i + 1, :]
                rim, c = rims[1][f]
                to = 15 - i + (f == 4)
                rim[c, t, to : to + 1, :] = past[i, 1, f, t, 7 - i : 8 - i, :]
            for c in range(2):
                bn[0, c, t, 17 + i : 18 + i, :] = past_n[i, 0, c, t, i : i + 1, :]
                bn[1, c, t, 15 - i : 16 - i, :] = past_n[i, 1, c, t, 7 - i : 8 - i, :]
        for side, x, y in ((0, i + 1, i + 1), (1, 16 - i, 15 - i)):
            first = rim_edges(side, x, y)
            second = rim_edges(side, x + 8, y + 8)
            rim_advance(side, y, first)
            rim_advance(side, y + 8, second)
    for side, at in ((0, 8), (1, frows - 24)):
        for (ref, c), (rim, _) in zip(fields, rims[side]):
            for t in range(nt):
                ref[c, t, at : at + 16, :] = rim[c, t, 8:24, :]

    for t in range(nt):
        gcol = gy * ww + 128 * t + lane
        dam_x = jnp.where(grow >= 1, 1.0 - ss[0, t, own_r, :], 0.0)
        dam_y = jnp.where(gcol >= 1, 1.0 - ss[1, t, own_r, :], 0.0)
        gap[t] = dam_x + dam_y
        o_dam[0, t] = dam_x.astype(jnp.bfloat16)
        o_dam[1, t] = dam_y.astype(jnp.bfloat16)
    rows2 = jnp.concatenate(
        [
            gap[t, pl.ds(0, ch, stride=2), :] + gap[t, pl.ds(1, ch, stride=2), :]
            for t in range(ww // 128)
        ],
        axis=1,
    )
    pairs = ww // 256
    glow = full_dot(
        jnp.concatenate([rows2[:, 256 * t : 256 * t + 256] for t in range(pairs)], axis=0), tab_s[...]
    )
    resist = jnp.concatenate([glow[ch * t : ch * t + ch] for t in range(pairs)], axis=1)
    t_tile = jnp.concatenate([tcx[j, 8 : 8 + ch, :] for j in range(nct)], axis=1)
    cond = (1.0 + 0.5 * t_tile) / (1.0 + resist)
    for j in range(nct):
        cpad[j, 8 : 8 + ch, :] = cond[:, 128 * j : 128 * j + 128]
    erow[0] = cond[0:1, :]
    erow[1] = cond[ch - 1 : ch, :]
    first_col, last_col = cond[0:8, 0:128], pltpu.roll(cond[0:8, cw - 128 : cw], 1, 1)
    for i in range(1, ch // 8):
        rows = slice(8 * i, 8 * i + 8)
        here = lane8 == i
        first_col = jnp.where(here, pltpu.roll(cond[rows, 0:128], i, 1), first_col)
        last_col = jnp.where(here, pltpu.roll(cond[rows, cw - 128 : cw], i + 1, 1), last_col)
    ecol[0] = first_col
    ecol[1] = last_col
    beside = [
        (has_u, has_d, remote(erow.at[0], grow_c.at[1], s_sem.at[1], r_sem.at[6], (up, gy))),
        (has_d, has_u, remote(erow.at[1], grow_c.at[0], s_sem.at[2], r_sem.at[6], (down, gy))),
        (has_l, has_r, remote(ecol.at[0], gcol_c.at[1], s_sem.at[3], r_sem.at[6], (gx, left))),
        (has_r, has_l, remote(ecol.at[1], gcol_c.at[0], s_sem.at[4], r_sem.at[6], (gx, right))),
    ]
    for ok, _, copy in beside:
        start_if(ok, copy)
    for b in range(n_gy):
        cb4[b] = cond[rpd * b : rpd * b + rpd, :]
    my_cols = pl.ds(pl.multiple_of(gy * cw, 128), cw)
    to_owner = []
    for t in range(n_gy):
        lo, hi = max(0, t - hz), min(n_gy, t + hz + 1)
        src = cb4.at[pl.ds(lo, hi - lo)]
        dst = owc.at[pl.ds(lo - t + hz, hi - lo), :, my_cols]
        to_owner.append((gy != t, remote(src, dst, s_sem.at[0], r_sem.at[7], (gx, t))))
        here = pltpu.make_async_copy(src, dst, r_sem.at[7])

        @pl.when(gy == t)
        def _():
            here.start()

    for t in range(hz):
        n = hz - t
        src, dst = cb4.at[pl.ds(n_gy - n, n)], owc.at[pl.ds(0, n), :, my_cols]
        to_owner.append((has_d, remote(src, dst, s_sem.at[2], r_sem.at[7], (down, t))))
        src, dst = cb4.at[pl.ds(0, n)], owc.at[pl.ds(2 * hz + 1 - n, n), :, my_cols]
        to_owner.append((has_u, remote(src, dst, s_sem.at[1], r_sem.at[7], (up, n_gy - 1 - t))))
    for ok, copy in to_owner:
        start_if(ok, copy)

    for c in range(2):
        for t in range(nt):
            o_speed[c, t] = 2.5 * sv[c, t, own_r, :]

    pltpu.make_async_copy(arecv, arecv, r_sem.at[4]).wait()
    for k in range(n_gy):
        for j in range(nct):
            base_t[j, rpd * k : rpd * k + rpd, :] = arecv[k, :, 128 * j : 128 * j + 128]
    for v in (1, 2):
        for h in (1, 2):
            done_if(
                (n_v == v) & (n_h == h),
                r_sem.at[6],
                v * size(erow.at[0]) + h * size(ecol.at[0]),
            )
    for j in range(nct):
        cols = slice(128 * j, 128 * j + 128)
        cpad[j, 7:8, :] = jnp.where(has_u, grow_c[0, :, cols], 0.0)
        cpad[j, 8 + ch : 9 + ch, :] = jnp.where(has_d, grow_c[1, :, cols], 0.0)
    from_l, from_r = gcol_c[0], gcol_c[1]
    sub8 = row_iota((8, 128))
    peak = None
    for i in range(ch // 8):
        r0 = 8 + 8 * i
        mid = [cpad[j, r0 : r0 + 8, :] for j in range(nct)]
        fwd = [pltpu.roll(x, 1, 1) for x in mid]
        bwd = [pltpu.roll(x, 127, 1) for x in mid]
        fwd_in = [pltpu.roll(from_l, 128 - i, 1) if i else from_l] + fwd[:-1]
        bwd_in = bwd[1:] + [pltpu.roll(from_r, 127 - i, 1)]
        for j in range(nct):
            c = mid[j]
            f_u = c + cpad[j, r0 - 1 : r0 + 7, :]
            f_d = c + cpad[j, r0 + 1 : r0 + 9, :]
            f_l = c + jnp.where(first_lane, fwd_in[j], fwd[j])
            f_r = c + jnp.where(last_lane, bwd_in[j], bwd[j])
            if i == 0:
                f_u = jnp.where(~has_u & (sub8 == 0), 0.0, f_u)
            if i == ch // 8 - 1:
                f_d = jnp.where(~has_d & (sub8 == 7), 0.0, f_d)
            if j == 0:
                f_l = jnp.where(~has_l & first_lane, 0.0, f_l)
            if j == nct - 1:
                f_r = jnp.where(~has_r & last_lane, 0.0, f_r)
            off = 0.5 * ((f_u + f_d) + (f_l + f_r))
            ratio = off / (base_t[j, 8 * i : 8 * i + 8, :] + off)
            peak = ratio if peak is None else jnp.maximum(peak, ratio)
    msend[...] = jnp.full((1, 128), jnp.max(peak), F32)

    for k in far_first(ndev, lambda k: k % n_gy // 2 + (k // n_gy).bit_count()):
        t = partner(me, k, ndev)
        remote(
            msend, mrecv.at[k - 1], s_sem.at[0], r_sem.at[8], (t // n_gy, t % n_gy)
        ).start()

    orows = 16
    n_swap = sum(jnp.where(came, 1, 0) for _, came, _ in swaps)
    for n in range(1, 2 * hz + 1):
        done_if(n_swap == n, r_sem.at[5], n * size(mine))
    reach = hz * rpd

    def gather(q, ref, fill):
        for b in range(2 * hz + 1):
            value = ref[b]
            if b != hz:
                there = me >= hz - b if b < hz else me + (b - hz) < ndev
                value = jnp.where(there, value, fill)
            field[q, rpd * b : rpd * b + rpd, :] = value

    for q in range(3):
        gather(q, own3.at[q], 1.0)
    rest = (2 * hz + 1) * rpd
    for q in range(4):
        field[q, rest:orows, :] = jnp.full((orows - rest, span), 0.0 if q == 3 else 1.0, F32)

    short_t = jnp.where(gx == 0, jnp.maximum(hz - gy, 0), 0)
    short_b = jnp.where(gx == n_gx - 1, jnp.maximum(hz - (n_gy - 1 - gy), 0), 0)
    for a in range(hz + 1):
        for b in range(hz + 1):
            got = owc.at[pl.ds(a, 2 * hz + 1 - a - b)]

            @pl.when((short_t == a) & (short_b == b))
            def _():
                pltpu.make_async_copy(got, got, r_sem.at[7]).wait()

    gather(3, owc, 0.0)
    oshape = (orows, span)
    row_g = me * rpd - reach + row_iota(oshape)
    col_g = lane_iota(oshape)
    total_rows = ndev * rpd

    def four(x):
        return (
            pltpu.roll(x, 1, 0),
            pltpu.roll(x, orows - 1, 0),
            pltpu.roll(x, 1, 1),
            pltpu.roll(x, span - 1, 1),
        )

    inside = (row_g >= 0) & (row_g < total_rows)
    masks = (
        inside & (row_g >= 1),
        inside & (row_g <= total_rows - 2),
        col_g >= 1,
        col_g <= span - 2,
    )
    cond = field[3]
    faces = [jnp.where(m, 0.5 * (cond + nb), 0.0) for m, nb in zip(masks, four(cond))]
    diagonal = field[1] + (faces[0] + faces[1] + faces[2] + faces[3])
    inv = 1.0 / diagonal
    t_all = field[0]
    near = sum(f * nb for f, nb in zip(faces, four(t_all)))
    z = (field[2] - (diagonal * t_all - near)) * inv
    faces = [f * inv for f in faces]
    for j in range(4):
        if j:
            z = z - sum(f * nb for f, nb in zip(faces, four(z)))
        zown[j] = z[reach : reach + rpd, :]

    pltpu.make_async_copy(mrecv, mrecv, r_sem.at[8]).wait()
    peak = jnp.maximum(jnp.max(mrecv[...], axis=0), msend[...])[0:1, :]
    low, high = 1.0 - peak, 1.0 + peak
    center = 0.5 * (high + low)
    spread = 0.5 * (high - low)
    sigma = center / spread
    rho = 1.0 / sigma
    zero = jnp.zeros_like(center)
    e = [zero + 1.0, zero, zero, zero]
    d = [1.0 / center, zero, zero, zero]
    total = list(d)
    for _ in range(3):
        e = [e[0]] + [e[i] - d[i - 1] for i in range(1, 4)]
        rho_next = 1.0 / (2.0 * sigma - rho)
        d = [rho_next * rho * d[i] + (2.0 * rho_next / spread) * e[i] for i in range(4)]
        total = [a + b for a, b in zip(total, d)]
        rho = rho_next
    for t in range(span // 128):
        cols = slice(128 * t, 128 * t + 128)
        x = warm[:, cols]
        for j in range(4):
            x = x + total[j] * zown[j, :, cols]
        o_warm[:, cols] = x

    for ok, _, copy in swaps:
        sent_if(ok, copy)
    always = (n_gy - 1) * (size(tsend.at[0]) + size(asend.at[0])) + (ndev - 1)
    blocks = [min(n_gy, t + hz + 1) - max(0, t - hz) for t in range(n_gy)]
    one = size(cb4.at[0])
    for t in range(n_gy):
        done_if(gy == t, s_sem.at[0], always + one * (sum(blocks) - blocks[t]))
    tall = size(rowsend.at[0]) + far_size + size(erow.at[0]) + one * (hz * (hz + 1) // 2)
    for i, ok in ((1, has_u), (2, has_d)):
        for h in (1, 2):
            done_if(ok & (n_h == h), s_sem.at[i], tall + h * size(ck.at[0]))
    for i, ok in ((3, has_l), (4, has_r)):
        done_if(ok, s_sem.at[i], size(pk.at[0]) + size(ecol.at[0]))


def put_out(su, speed, dam, warm, o_shift, o_speed, o_dam, o_warm, sem):
    nt, hh = dam.shape[1:3]
    for t in range(nt):
        cols = slice(128 * t, 128 * t + 128)
        for i, (src, dst) in enumerate(
            (
                (su.at[:, t, HALO : HALO + hh, :], o_shift.at[:, :, cols]),
                (speed.at[:, t], o_speed.at[:, :, cols]),
                (dam.at[:, t], o_dam.at[:, :, cols]),
            )
        ):
            pltpu.make_async_copy(src, dst, sem.at[i]).start()
    last = pltpu.make_async_copy(warm, o_warm, sem.at[3])
    last.start()
    for i, dst in enumerate((o_shift, o_speed, o_dam)):
        pltpu.make_async_copy(dst, dst, sem.at[i]).wait()
    last.wait()


def per_device(n_gx, n_gy, shift, speed, level, mark, warm, store, film, bath):
    _, hh, ww = shift.shape
    rpd, _ = warm.shape
    cw, ch = ww // 2, hh // 2
    wide = cw + 128
    nt, nct = ww // 128, cw // 128
    ntile = nt + 1
    crows, frows = ch + 16, hh + 2 * HALO
    nsl = n_gy + 2 * (HALO // rpd)
    hz = HALO // 2 // rpd
    vm = lambda *s: pltpu.VMEM(s, F32)
    dma = lambda n: pltpu.SemaphoreType.DMA((n,))
    hbm = pl.BlockSpec(memory_space=pltpu.HBM)
    vmem = pl.BlockSpec(memory_space=pltpu.VMEM)
    outs = pl.pallas_call(
        functools.partial(kernel, n_gx, n_gy),
        out_shape=(
            vm(2, ntile, frows, 128),
            vm(2, nt, hh, 128),
            pltpu.VMEM((2, nt, hh, 128), jnp.bfloat16),
            vm(*warm.shape),
        ),
        in_specs=[hbm] * 8,
        out_specs=(vmem,) * 4,
        scratch_shapes=[
            vm(n_gy, rpd, wide),
            vm(nsl, rpd, wide),
            vm(n_gy, rpd, cw),
            vm(n_gy, rpd, cw),
            vm(2, hh, 128),
            vm(2, hh, 128),
            vm(4, 8, 128),
            vm(2, 6 * nt + 1, 8, 128),
            vm(2, 6 * nt + 1, 8, 128),
            vm(2, 2, ntile, 32, 128),
            vm(2, 2, ntile, 32, 128),
            vm(2, 2, ntile, 32, 128),
            vm(2, 2, ntile, 40, 128),
            vm(SUBSTEPS, 2, 6, ntile, 8, 128),
            vm(SUBSTEPS, 2, 2, ntile, 8, 128),
            pltpu.VMEM(level.shape, level.dtype),
            vm(*warm.shape),
            vm(*warm.shape),
            vm(*warm.shape),
            vm(*warm.shape),
            vm(2, ntile, frows, 128),
            vm(2, ntile, frows, 128),
            vm(frows, 128),
            vm(frows, 128),
            vm(ntile, frows, 128),
            vm(ntile, frows, 128),
            vm(ntile, frows, 128),
            vm(2, ntile, frows + 8, 128),
            vm(nct + 1, crows, 128),
            vm(nct + 1, frows, 128),
            vm(256, 128),
            vm(nt, hh, 128),
            vm(nct, ch, 128),
            vm(nct, crows, 128),
            vm(2, 1, cw),
            vm(2, 1, cw),
            vm(2, 8, 128),
            vm(2, 8, 128),
            vm(n_gy, rpd, cw),
            vm(2 * hz + 1, rpd, cw * n_gy),
            vm(3, 2 * hz + 1, rpd, cw * n_gy),
            vm(4, 16, cw * n_gy),
            vm(4, rpd, cw * n_gy),
            vm(1, 128),
            vm(n_gx * n_gy - 1, 1, 128),
            dma(5 + 2 * hz),
            dma(12),
            vm(3 * level.size // 128, 1, 128),
            pltpu.SMEM((1, hh // SR), mark.dtype),
        ],
        compiler_params=pltpu.CompilerParams(
            collective_id=0, has_side_effects=True
        ),
    )(shift, speed, level, mark.reshape(1, hh // SR), warm, store, film, bath)
    return pl.pallas_call(
        put_out,
        out_shape=tuple(
            jax.ShapeDtypeStruct(o.shape, d)
            for o, d in ((shift, F32), (speed, F32), (level, jnp.bfloat16), (warm, F32))
        ),
        in_specs=[vmem] * 4,
        out_specs=(hbm,) * 4,
        scratch_shapes=[dma(4)],
    )(*(pltpu.with_memory_space_constraint(o, pltpu.VMEM) for o in outs))


def solution(mesh):
    rows = P(("gx", "gy"), None)
    plate = P(None, "gx", "gy")
    return jax.shard_map(
        functools.partial(per_device, mesh.shape["gx"], mesh.shape["gy"]),
        mesh=mesh,
        in_specs=(plate, plate, plate, P("gx", "gy"), rows, rows, rows, rows),
        out_specs=(plate, plate, plate, rows),
        check_vma=False,
    )
```

```python
import functools
import math

import jax
import jax.numpy as jnp
from jax import lax
from jax.experimental import pallas as pl
from jax.experimental.pallas import tpu as pltpu
from jax.sharding import PartitionSpec as P

SR = 8
SEG = 128
SUBSTEPS = 8
HALO = 8
FIELDS = 7
MESH = pl.DeviceIdType.MESH
F32 = jnp.float32


def lane_iota(shape):
    return lax.broadcasted_iota(jnp.int32, shape, 1)


def row_iota(shape):
    return lax.broadcasted_iota(jnp.int32, shape, 0)


def full_dot(a, b):
    return jnp.dot(a, b, precision=lax.Precision.HIGHEST, preferred_element_type=F32)


def partner(me, k, n):
    if n & (n - 1):
        return lax.rem(me + k, n)
    t = me
    for b in range(n.bit_length() - 1):
        if k >> b & 1:
            t = t + (1 - 2 * (me // 2**b % 2)) * 2**b
    return t


def far_first(n, hops):
    return sorted(range(1, n), key=lambda k: (-hops(k), -k))


def pick(x, index):
    return jnp.take_along_axis(x, index, axis=1)


def kernel(
    n_gx,
    n_gy,
    shift,
    speed,
    level_h,
    mark_h,
    warm_h,
    store_h,
    film_h,
    bath_h,
    su,
    o_speed,
    o_dam,
    o_warm,
    tsend,
    trecv,
    asend,
    arecv,
    pk,
    rk,
    ck,
    rowsend,
    rowrecv,
    bu,
    bv,
    bs,
    bn,
    past,
    past_n,
    level,
    warm,
    store,
    film,
    bath,
    sv,
    ss,
    kw,
    kh,
    tx,
    ty,
    fine,
    nx,
    tcx,
    widebuf,
    tab_s,
    gap,
    base_t,
    cpad,
    erow,
    grow_c,
    ecol,
    gcol_c,
    cb4,
    owc,
    own3,
    field,
    zown,
    msend,
    mrecv,
    s_sem,
    r_sem,
    meter,
    mark,
):
    ndev = n_gx * n_gy
    gx = lax.axis_index("gx")
    gy = lax.axis_index("gy")
    me = gx * n_gy + gy
    _, hh, ww = shift.shape
    rpd, _ = warm_h.shape
    cw = ww // 2
    ch = hh // 2
    hb = HALO // rpd
    nsl = n_gy + 2 * hb
    nt = ww // 128
    ntile = nt + 1
    nct = cw // 128
    frows = hh + 2 * HALO
    nstrip = frows // 8
    up = lax.rem(gx + n_gx - 1, n_gx)
    down = lax.rem(gx + 1, n_gx)
    left = lax.rem(gy + n_gy - 1, n_gy)
    right = lax.rem(gy + 1, n_gy)
    has_u, has_d = gx > 0, gx < n_gx - 1
    has_l, has_r = gy > 0, gy < n_gy - 1
    hz = HALO // 2 // rpd
    span = cw * n_gy
    own_r = slice(HALO, HALO + hh)

    n_v = jnp.where(has_u, 1, 0) + jnp.where(has_d, 1, 0)
    n_h = jnp.where(has_l, 1, 0) + jnp.where(has_r, 1, 0)

    def size(ref):
        return math.prod(ref.shape) // 128

    def done(sem, lines):
        part = meter.at[pl.ds(0, lines)]
        pltpu.make_async_copy(part, part, sem).wait()

    def done_if(cond, sem, lines):
        if lines:

            @pl.when(cond)
            def _():
                done(sem, lines)

    barrier = pltpu.get_barrier_semaphore()
    warm_load = pltpu.make_async_copy(warm_h, warm, r_sem.at[9])
    warm_load.start()

    def greet(a, b):
        pl.semaphore_signal(barrier, inc=1, device_id=(a, b), device_id_type=MESH)

    for k in far_first(n_gy, lambda k: k // 2):
        greet(gx, partner(gy, k, n_gy))
    calls = n_gy - 1
    for k in range(1, n_gx):
        if k == 1 or k > 3:
            for ok, a in ((gx >= k, gx - k), (gx + k < n_gx, gx + k)):
                sides = ((True, gy), (has_l, left), (has_r, right)) if k == 1 else ((True, gy),)
                for beside, b in sides:
                    calls = calls + jnp.where(ok & beside, 1, 0)

                    @pl.when(ok & beside)
                    def _():
                        greet(a, b)

    loads = [
        pltpu.make_async_copy(src, dst, r_sem.at[i])
        for src, dst, i in (
            (mark_h, mark, 1),
            (level_h, level, 10),
            (store_h, store, 11),
            (film_h, film, 11),
            (bath_h, bath, 11),
        )
    ]
    loads[0].start()
    loads[1].start()
    for src, dst in ((shift, su), (speed, sv)):
        for t in range(nt):
            pltpu.make_async_copy(
                src.at[:, :, 128 * t : 128 * t + 128], dst.at[:, t, own_r, :], r_sem.at[10]
            ).start()
    for copy in loads[2:]:
        copy.start()

    lane_c = lane_iota((rpd, 128))

    def chunk(value, k):
        after = value[:, (cw * (k + 1)) % (cw * n_gy) :][:, 0:128]
        before = value[:, (cw * k - 128) % (cw * n_gy) :][:, 0:128]
        return value[:, cw * k : cw * k + cw], jnp.where(lane_c < 64, after, before)

    def remote(src, dst, ssem, rsem, where):
        return pltpu.make_async_remote_copy(
            src_ref=src, dst_ref=dst, send_sem=ssem, recv_sem=rsem, device_id=where,
            device_id_type=MESH,
        )

    warm_load.wait()
    t_own = warm[...]
    for k in range(n_gy):
        main, edge = chunk(t_own, k)
        tsend[k, :, 0:cw] = main
        tsend[k, :, cw : cw + 128] = edge

    sharp = -4.0 * math.log2(math.e)
    lane = lane_iota((hh, 128))
    loads[0].wait()
    done(r_sem.at[10], 3 * size(level))
    for s in range(hh // SR):
        kw[HALO + SR * s : HALO + SR * s + SR, :] = (
            jnp.full((SR, 128), mark[0, s], jnp.int32).astype(F32) * sharp
        )
    w_own = kw[own_r, :] * (0.125 / sharp)
    grow = gx * hh + row_iota((hh, 128))
    for t in range(nt):
        cols = slice(128 * t, 128 * t + 128)
        gcol = gy * ww + 128 * t + lane
        ss[0, t, own_r, :] = jnp.where(grow >= 1, 1.0 - level[0, :, cols].astype(F32) * w_own, 0.0)
        ss[1, t, own_r, :] = jnp.where(gcol >= 1, 1.0 - level[1, :, cols].astype(F32) * w_own, 0.0)
    for c in range(2):
        for t in range(nt):
            sv[c, t, own_r, :] = 0.4 * sv[c, t, own_r, :]
    lines_of = (8, 8, 7, 7, 8, 7)
    line_at = [nt * sum(lines_of[:f]) for f in range(7)]
    acc_l = jnp.zeros((hh, 128), F32)
    acc_r = jnp.zeros((hh, 128), F32)
    fields = [(ref, c) for ref in (su, sv, ss) for c in range(2)]
    for f in range(FIELDS):
        if f < 6:
            ref, c = fields[f]
            first, last = ref[c, 0, own_r, :], ref[c, nt - 1, own_r, :]
        else:
            first = last = kw[own_r, :]
        here = (lane >= 8 * f) & (lane < 8 * f + 8)
        first = pltpu.roll(first, 8 * f, 1) if f else first
        acc_l = jnp.where(here, first, acc_l)
        acc_r = jnp.where(here, pltpu.roll(last, 8 * f + 8, 1), acc_r)
    pk[0] = acc_l
    pk[1] = acc_r
    side_l = remote(pk.at[0], rk.at[1], s_sem.at[3], r_sem.at[0], (gx, left))
    side_r = remote(pk.at[1], rk.at[0], s_sem.at[4], r_sem.at[0], (gx, right))
    top, end = slice(0, 8), slice(hh - 8, hh)
    corners = [
        (has_u & has_l, remote(pk.at[0, top], ck.at[3], s_sem.at[1], r_sem.at[2], (up, left)), 2),
        (has_u & has_r, remote(pk.at[1, top], ck.at[2], s_sem.at[1], r_sem.at[2], (up, right)), 3),
        (has_d & has_l, remote(pk.at[0, end], ck.at[1], s_sem.at[2], r_sem.at[2], (down, left)), 4),
        (has_d & has_r, remote(pk.at[1, end], ck.at[0], s_sem.at[2], r_sem.at[2], (down, right)), 5),
    ]
    rows_u = remote(rowsend.at[0], rowrecv.at[1], s_sem.at[1], r_sem.at[2], (up, gy))
    rows_d = remote(rowsend.at[1], rowrecv.at[0], s_sem.at[2], r_sem.at[2], (down, gy))
    sends = [(has_l, side_l), (has_r, side_r)] + [(a, b) for a, b, _ in corners]
    sends += [(has_u, rows_u), (has_d, rows_d)]

    def start_if(cond, copy):
        @pl.when(cond)
        def _():
            copy.start()

    def sent_if(cond, copy):
        @pl.when(cond)
        def _():
            copy.wait_send()

    for side, at in ((0, HALO), (1, HALO + hh - 8)):
        for f, (ref, c) in enumerate(fields):
            skip = side if lines_of[f] == 7 else 0
            for t in range(nt):
                to = line_at[f] + lines_of[f] * t
                rowsend[side, to : to + lines_of[f], :] = ref[
                    c, t, at + skip : at + skip + lines_of[f], :
                ]
        rowsend[side, line_at[6] : line_at[6] + 1, :] = kw[at : at + 1, :]
    pl.semaphore_wait(barrier, calls)

    for k in far_first(n_gy, lambda k: k // 2):
        t = partner(gy, k, n_gy)
        remote(tsend.at[t], trecv.at[gy + hb], s_sem.at[0], r_sem.at[3], (gx, t)).start()
    pltpu.make_async_copy(tsend.at[gy], trecv.at[gy + hb], r_sem.at[3]).start()

    for cond, copy in sends[6:8]:
        start_if(cond, copy)
    for cond, copy in sends[0:6]:
        start_if(cond, copy)

    k_i, n_i = row_iota((256, 128)), lane_iota((256, 128))
    pos = (k_i % SEG).astype(F32)
    col = (2 * (n_i % 64)).astype(F32)
    tab = jnp.exp(jnp.abs(pos - col) * (-4.0 / SEG)) + jnp.exp(jnp.abs(pos - col - 1.0) * (-4.0 / SEG))
    tab_s[...] = jnp.where(k_i // SEG == n_i // 64, tab * (1.0 / SEG), 0.0)
    done(r_sem.at[11], 3 * size(store))
    base = store[...] + film[...]
    own3[0, hz] = t_own
    own3[1, hz] = base
    own3[2, hz] = store[...] * t_own + film[...] * bath[...]
    for k in range(n_gy):
        asend[k] = base[:, cw * k : cw * k + cw]
    strip = (nstrip - 2) * 8
    nx[:, :, strip : strip + 8, :] = jnp.zeros((2, ntile, 8, 128), F32)
    bn[:, :, :, 32:40, :] = jnp.zeros((2, 2, ntile, 8, 128), F32)

    mid = trecv.at[pl.ds(hb, n_gy)]
    pltpu.make_async_copy(mid, mid, r_sem.at[3]).wait()
    far_u = remote(
        trecv.at[pl.ds(hb, hb)], trecv.at[pl.ds(hb + n_gy, hb)], s_sem.at[1], r_sem.at[12], (up, gy)
    )
    far_d = remote(
        trecv.at[pl.ds(n_gy, hb)], trecv.at[pl.ds(0, hb)], s_sem.at[2], r_sem.at[12], (down, gy)
    )
    start_if(has_u, far_u)
    start_if(has_d, far_d)

    for k in range(1, n_gy):
        t = partner(gy, k, n_gy)
        remote(asend.at[t], arecv.at[gy], s_sem.at[0], r_sem.at[4], (gx, t)).start()
    pltpu.make_async_copy(asend.at[gy], arecv.at[gy], r_sem.at[4]).start()
    mine = own3.at[:, hz]
    swaps = []
    for d in range(1, hz + 1):
        for i, to, ok, came in (
            (d - 1, me + d, me + d < ndev, me >= d),
            (hz + d - 1, me - d, me >= d, me + d < ndev),
        ):
            at = hz - d if i < hz else hz + d
            to = lax.rem(to + ndev, ndev)
            copy = remote(mine, own3.at[:, at], s_sem.at[5 + i], r_sem.at[5], (to // n_gy, to % n_gy))
            swaps.append((ok, came, copy))
    for ok, _, copy in swaps:
        start_if(ok, copy)
    lane8 = lane_iota((8, 128))
    first_lane, last_lane = lane8 == 0, lane8 == 127

    def close_edge(rows):
        edge = tcx[nct, rows, :]
        edge = jnp.where(~has_l & last_lane, pltpu.roll(tcx[0, rows, :], 127, 1), edge)
        edge = jnp.where(~has_r & first_lane, pltpu.roll(tcx[nct - 1, rows, :], 1, 1), edge)
        tcx[nct, rows, :] = edge

    for k in range(hb, hb + n_gy):
        for j in range(nct + 1):
            tcx[j, rpd * k : rpd * k + rpd, :] = trecv[k, :, 128 * j : 128 * j + 128]
    for c in range(8, 8 + ch, 8):
        close_edge(slice(c, c + 8))
    half = lane8 // 2
    step = jnp.where(lane8 % 2 == 0, -1, 1)
    lo_g, lo_h = half, jnp.maximum(half + step, 0)
    hi_g, hi_h = half + 64, jnp.minimum(half + 64 + step, 127)
    ed_g = jnp.where(lane8 < 64, half, half + 64)
    ed_h = jnp.minimum(jnp.maximum(ed_g + step, 0), 127)

    def before(tiles):
        turned = [pltpu.roll(x, 1, 1) for x in tiles]
        return [jnp.where(first_lane, turned[t - 1], turned[t]) for t in range(len(tiles))]

    def after(tiles):
        turned = [pltpu.roll(x, 127, 1) for x in tiles]
        n = len(tiles)
        return [jnp.where(last_lane, turned[(t + 1) % n], turned[t]) for t in range(n)]

    def above(ref, s):
        return ref[8 * s - 1 : 8 * s + 7, :] if s else pltpu.roll(ref[0:8, :], 1, 0)

    def heat_x(s):
        rows = slice(8 * s, 8 * s + 8)
        for t in range(ntile):
            tx[t, rows, :] = 0.3 * (fine[t, rows, :] + above(fine.at[t], s))

    def prolong(p):
        c = 8 * p + 4
        for j in range(nct + 1):
            here = 0.75 * tcx[j, c : c + 8, :]
            widebuf[j, pl.ds(16 * p, 8, stride=2), :] = here + 0.25 * tcx[j, c - 1 : c + 7, :]
            widebuf[j, pl.ds(16 * p + 1, 8, stride=2), :] = here + 0.25 * tcx[j, c + 1 : c + 9, :]
        for s in (2 * p, 2 * p + 1):
            rows = slice(8 * s, 8 * s + 8)
            r = [widebuf[j, rows, :] for j in range(nct + 1)]
            fwd = [pltpu.roll(x, 1, 1) for x in r]
            bwd = [pltpu.roll(x, 127, 1) for x in r]
            f = []
            for j in range(nct):
                f.append(
                    0.75 * pick(r[j], lo_g)
                    + 0.25 * jnp.where(first_lane, fwd[j - 1], pick(r[j], lo_h))
                )
                f.append(
                    0.75 * pick(r[j], hi_g)
                    + 0.25 * jnp.where(last_lane, bwd[j + 1], pick(r[j], hi_h))
                )
            e = pick(r[nct], ed_h)
            e = jnp.where(first_lane, fwd[nct - 1], jnp.where(last_lane, bwd[0], e))
            f.append(0.75 * pick(r[nct], ed_g) + 0.25 * e)
            prev = before(f)
            for t in range(ntile):
                fine[t, rows, :] = f[t]
                ty[t, rows, :] = 0.3 * (f[t] + prev[t])

    npair = nstrip // 2
    for p in range(1, npair - 1):
        prolong(p)
    for s in range(2, nstrip - 2):
        heat_x(s)

    for h in (1, 2):
        done_if(n_h == h, r_sem.at[0], h * size(pk.at[0]))

    def unpack(got_l, got_r, targets, rows, lines, outside):
        shape = got_l.shape
        lanes = lane_iota(shape)
        gone = outside | (~has_l & (lanes >= 64)) | (~has_r & (lanes < 64))
        for f in range(FIELDS):
            from_r = pltpu.roll(got_r, 128 - 8 * f, 1) if f else got_r
            from_l = pltpu.roll(got_l, 120 - 8 * f, 1)
            side = jnp.where(lanes < 8, from_r, jnp.where(lanes >= 120, from_l, 0.0))
            side = jnp.where(gone, 0.0, side)
            if f < 6:
                ref, c = targets[f]
                ref[c, nt, rows, :] = side
            else:
                kh[lines, :] = side

    unpack(rk[0], rk[1], fields, own_r, own_r, False)
    rims = [
        [(ref.at[side], c) for ref in (bu, bv, bs) for c in range(2)] for side in range(2)
    ]
    for side, (at, to) in enumerate(((8, 8), (frows - 16, 16))):
        for (ref, c), (rim, _) in zip(fields, rims[side]):
            for t in range(ntile):
                rim[c, t, to : to + 8, :] = ref[c, t, at : at + 8, :]

    def edges(s):
        rows = slice(8 * s, 8 * s + 8)
        u0 = [su[0, t, rows, :] for t in range(ntile)]
        u1 = [su[1, t, rows, :] for t in range(ntile)]
        k_main, k_side = kw[rows, :], kh[rows, :]
        b0, b1 = before(u0), before(u1)
        ay, ny = [], []
        for t in range(ntile):
            k = k_main if t < nt else k_side
            open_x = u0[t] - above(su.at[0, t], s) - tx[t, rows, :]
            st = jnp.maximum(open_x, 0.0)
            sp = jnp.minimum(ss[0, t, rows, :], jnp.exp2(st * st * k))
            ss[0, t, rows, :] = sp
            nx[0, t, rows, :] = sp * open_x
            nx[1, t, rows, :] = sp * (u1[t] - above(su.at[1, t], s))
            open_y = u1[t] - b1[t] - ty[t, rows, :]
            st = jnp.maximum(open_y, 0.0)
            sp = jnp.minimum(ss[1, t, rows, :], jnp.exp2(st * st * k))
            ss[1, t, rows, :] = sp
            ny.append(sp * open_y)
            ay.append(sp * (u0[t] - b0[t]))
        fy0 = [a - b for a, b in zip(after(ay), ay)]
        fy1 = [a - b for a, b in zip(after(ny), ny)]
        return fy0, fy1

    def advance(s, fy):
        rows = slice(8 * s, 8 * s + 8)
        below = slice(8 * s + 1, 8 * s + 9)
        for c in range(2):
            for t in range(ntile):
                force = (nx[c, t, below, :] - nx[c, t, rows, :]) + fy[c][t]
                v = 0.98 * sv[c, t, rows, :] + 0.16 * force
                sv[c, t, rows, :] = v
                su[c, t, rows, :] = su[c, t, rows, :] + v

    def interior(i, carry):
        for f, (ref, c) in enumerate(fields):
            at = frows - 24 + (f == 4)
            for t in range(ntile):
                past[i, 0, f, t] = ref[c, t, 16:24, :]
                past[i, 1, f, t] = ref[c, t, at : at + 8, :]
        old = None
        for s in range(2, nstrip - 2):
            new = edges(s)
            if old:
                advance(s - 1, old)
            old = new
        advance(nstrip - 3, old)
        for c in range(2):
            for t in range(ntile):
                past_n[i, 0, c, t] = nx[c, t, 17:25, :]
                past_n[i, 1, c, t] = nx[c, t, frows - 24 : frows - 16, :]
        return carry

    lax.fori_loop(0, SUBSTEPS, interior, 0)

    far_size = hb * size(trecv.at[0])
    for v in (1, 2):
        for h in (1, 2):
            done_if(
                (n_v == v) & (n_h == h),
                r_sem.at[2],
                v * (size(rowsend.at[0]) + h * size(ck.at[0])),
            )
    for side, (here, at, to) in enumerate(((has_u, 0, 0), (has_d, hh + HALO, 24))):
        rows = slice(to, to + 8)
        lines = slice(at, at + 8)
        for f, (rim, c) in enumerate(rims[side]):
            first = to if side or lines_of[f] == 8 else to + 1
            for t in range(nt):
                line = line_at[f] + lines_of[f] * t
                got = rowrecv[side, line : line + lines_of[f], :]
                rim[c, t, first : first + lines_of[f], :] = jnp.where(here, got, 0.0)
        got = jnp.broadcast_to(rowrecv[side, line_at[6] : line_at[6] + 1, :], (8, 128))
        kw[lines, :] = jnp.where(here, got, 0.0)
        unpack(ck[2 * side], ck[2 * side + 1], rims[side], rows, lines, ~here)
    for v in (1, 2):
        done_if(n_v == v, r_sem.at[12], v * far_size)
    for side, (here, at, slot, line) in enumerate(
        ((has_u, 0, 0, 8), (has_d, ch + 8, hb + n_gy, ch + 7))
    ):

        @pl.when(here)
        def _():
            for k in range(hb):
                for j in range(nct + 1):
                    tcx[j, at + rpd * k : at + rpd * k + rpd, :] = trecv[
                        slot + k, :, 128 * j : 128 * j + 128
                    ]
            close_edge(slice(at, at + 8))

        @pl.when(jnp.logical_not(here))
        def _():
            for j in range(nct + 1):
                tcx[j, at : at + 8, :] = jnp.broadcast_to(tcx[j, line : line + 1, :], (8, 128))

    prolong(0)
    prolong(npair - 1)
    for s in (0, 1, 2, nstrip - 2, nstrip - 1):
        heat_x(s)

    for t in range(ntile):
        bs[1, 0, t, 8:9, :] = ss[0, t, frows - 24 : frows - 23, :]

    def rim_edges(side, x, y):
        shift_by = (frows - 32) * side
        u, spring, flow = bu.at[side], bs.at[side], bn.at[side]
        ex, ex_up, ey = pl.ds(x, 8), pl.ds(x - 1, 8), pl.ds(y, 8)
        gx_rows, gy_rows = pl.ds(x + shift_by, 8), pl.ds(y + shift_by, 8)
        u0 = [u[0, t, ey, :] for t in range(ntile)]
        u1 = [u[1, t, ey, :] for t in range(ntile)]
        b0, b1 = before(u0), before(u1)
        kx = [kw[gx_rows, :], kh[gx_rows, :]]
        ky = [kw[gy_rows, :], kh[gy_rows, :]]
        ay, ny = [], []
        for t in range(ntile):
            open_x = u[0, t, ex, :] - u[0, t, ex_up, :] - tx[t, gx_rows, :]
            st = jnp.maximum(open_x, 0.0)
            sp = jnp.minimum(spring[0, t, ex, :], jnp.exp2(st * st * kx[t // nt]))
            spring[0, t, ex, :] = sp
            flow[0, t, ex, :] = sp * open_x
            flow[1, t, ex, :] = sp * (u[1, t, ex, :] - u[1, t, ex_up, :])
            open_y = u1[t] - b1[t] - ty[t, gy_rows, :]
            st = jnp.maximum(open_y, 0.0)
            sp = jnp.minimum(spring[1, t, ey, :], jnp.exp2(st * st * ky[t // nt]))
            spring[1, t, ey, :] = sp
            ny.append(sp * open_y)
            ay.append(sp * (u0[t] - b0[t]))
        fy0 = [a - b for a, b in zip(after(ay), ay)]
        fy1 = [a - b for a, b in zip(after(ny), ny)]
        return fy0, fy1

    def rim_advance(side, y, fy):
        rows, below = pl.ds(y, 8), pl.ds(y + 1, 8)
        for c in range(2):
            for t in range(ntile):
                force = (bn[side, c, t, below, :] - bn[side, c, t, rows, :]) + fy[c][t]
                v = 0.98 * bv[side, c, t, rows, :] + 0.16 * force
                bv[side, c, t, rows, :] = v
                bu[side, c, t, rows, :] = bu[side, c, t, rows, :] + v

    for i in range(SUBSTEPS):
        for t in range(ntile):
            for f in range(6):
                rim, c = rims[0][f]
                rim[c, t, 16 + i : 17 + i, :] = past[i, 0, f, t, i : i + 1, :]
                rim, c = rims[1][f]
                to = 15 - i + (f == 4)
                rim[c, t, to : to + 1, :] = past[i, 1, f, t, 7 - i : 8 - i, :]
            for c in range(2):
                bn[0, c, t, 17 + i : 18 + i, :] = past_n[i, 0, c, t, i : i + 1, :]
                bn[1, c, t, 15 - i : 16 - i, :] = past_n[i, 1, c, t, 7 - i : 8 - i, :]
        for side, x, y in ((0, i + 1, i + 1), (1, 16 - i, 15 - i)):
            first = rim_edges(side, x, y)
            second = rim_edges(side, x + 8, y + 8)
            rim_advance(side, y, first)
            rim_advance(side, y + 8, second)
    for side, at in ((0, 8), (1, frows - 24)):
        for (ref, c), (rim, _) in zip(fields, rims[side]):
            for t in range(nt):
                ref[c, t, at : at + 16, :] = rim[c, t, 8:24, :]

    for t in range(nt):
        gcol = gy * ww + 128 * t + lane
        dam_x = jnp.where(grow >= 1, 1.0 - ss[0, t, own_r, :], 0.0)
        dam_y = jnp.where(gcol >= 1, 1.0 - ss[1, t, own_r, :], 0.0)
        gap[t] = dam_x + dam_y
        o_dam[0, t] = dam_x.astype(jnp.bfloat16)
        o_dam[1, t] = dam_y.astype(jnp.bfloat16)
    rows2 = jnp.concatenate(
        [
            gap[t, pl.ds(0, ch, stride=2), :] + gap[t, pl.ds(1, ch, stride=2), :]
            for t in range(ww // 128)
        ],
        axis=1,
    )
    pairs = ww // 256
    glow = full_dot(
        jnp.concatenate([rows2[:, 256 * t : 256 * t + 256] for t in range(pairs)], axis=0), tab_s[...]
    )
    resist = jnp.concatenate([glow[ch * t : ch * t + ch] for t in range(pairs)], axis=1)
    t_tile = jnp.concatenate([tcx[j, 8 : 8 + ch, :] for j in range(nct)], axis=1)
    cond = (1.0 + 0.5 * t_tile) / (1.0 + resist)
    for j in range(nct):
        cpad[j, 8 : 8 + ch, :] = cond[:, 128 * j : 128 * j + 128]
    erow[0] = cond[0:1, :]
    erow[1] = cond[ch - 1 : ch, :]
    first_col, last_col = cond[0:8, 0:128], pltpu.roll(cond[0:8, cw - 128 : cw], 1, 1)
    for i in range(1, ch // 8):
        rows = slice(8 * i, 8 * i + 8)
        here = lane8 == i
        first_col = jnp.where(here, pltpu.roll(cond[rows, 0:128], i, 1), first_col)
        last_col = jnp.where(here, pltpu.roll(cond[rows, cw - 128 : cw], i + 1, 1), last_col)
    ecol[0] = first_col
    ecol[1] = last_col
    beside = [
        (has_u, has_d, remote(erow.at[0], grow_c.at[1], s_sem.at[1], r_sem.at[6], (up, gy))),
        (has_d, has_u, remote(erow.at[1], grow_c.at[0], s_sem.at[2], r_sem.at[6], (down, gy))),
        (has_l, has_r, remote(ecol.at[0], gcol_c.at[1], s_sem.at[3], r_sem.at[6], (gx, left))),
        (has_r, has_l, remote(ecol.at[1], gcol_c.at[0], s_sem.at[4], r_sem.at[6], (gx, right))),
    ]
    for ok, _, copy in beside:
        start_if(ok, copy)
    for b in range(n_gy):
        cb4[b] = cond[rpd * b : rpd * b + rpd, :]
    my_cols = pl.ds(pl.multiple_of(gy * cw, 128), cw)
    to_owner = []
    for t in range(n_gy):
        lo, hi = max(0, t - hz), min(n_gy, t + hz + 1)
        src = cb4.at[pl.ds(lo, hi - lo)]
        dst = owc.at[pl.ds(lo - t + hz, hi - lo), :, my_cols]
        to_owner.append((gy != t, remote(src, dst, s_sem.at[0], r_sem.at[7], (gx, t))))
        here = pltpu.make_async_copy(src, dst, r_sem.at[7])

        @pl.when(gy == t)
        def _():
            here.start()

    for t in range(hz):
        n = hz - t
        src, dst = cb4.at[pl.ds(n_gy - n, n)], owc.at[pl.ds(0, n), :, my_cols]
        to_owner.append((has_d, remote(src, dst, s_sem.at[2], r_sem.at[7], (down, t))))
        src, dst = cb4.at[pl.ds(0, n)], owc.at[pl.ds(2 * hz + 1 - n, n), :, my_cols]
        to_owner.append((has_u, remote(src, dst, s_sem.at[1], r_sem.at[7], (up, n_gy - 1 - t))))
    for ok, copy in to_owner:
        start_if(ok, copy)

    for c in range(2):
        for t in range(nt):
            o_speed[c, t] = 2.5 * sv[c, t, own_r, :]

    pltpu.make_async_copy(arecv, arecv, r_sem.at[4]).wait()
    for k in range(n_gy):
        for j in range(nct):
            base_t[j, rpd * k : rpd * k + rpd, :] = arecv[k, :, 128 * j : 128 * j + 128]
    for v in (1, 2):
        for h in (1, 2):
            done_if(
                (n_v == v) & (n_h == h),
                r_sem.at[6],
                v * size(erow.at[0]) + h * size(ecol.at[0]),
            )
    for j in range(nct):
        cols = slice(128 * j, 128 * j + 128)
        cpad[j, 7:8, :] = jnp.where(has_u, grow_c[0, :, cols], 0.0)
        cpad[j, 8 + ch : 9 + ch, :] = jnp.where(has_d, grow_c[1, :, cols], 0.0)
    from_l, from_r = gcol_c[0], gcol_c[1]
    sub8 = row_iota((8, 128))
    peak = None
    for i in range(ch // 8):
        r0 = 8 + 8 * i
        mid = [cpad[j, r0 : r0 + 8, :] for j in range(nct)]
        fwd = [pltpu.roll(x, 1, 1) for x in mid]
        bwd = [pltpu.roll(x, 127, 1) for x in mid]
        fwd_in = [pltpu.roll(from_l, 128 - i, 1) if i else from_l] + fwd[:-1]
        bwd_in = bwd[1:] + [pltpu.roll(from_r, 127 - i, 1)]
        for j in range(nct):
            c = mid[j]
            f_u = c + cpad[j, r0 - 1 : r0 + 7, :]
            f_d = c + cpad[j, r0 + 1 : r0 + 9, :]
            f_l = c + jnp.where(first_lane, fwd_in[j], fwd[j])
            f_r = c + jnp.where(last_lane, bwd_in[j], bwd[j])
            if i == 0:
                f_u = jnp.where(~has_u & (sub8 == 0), 0.0, f_u)
            if i == ch // 8 - 1:
                f_d = jnp.where(~has_d & (sub8 == 7), 0.0, f_d)
            if j == 0:
                f_l = jnp.where(~has_l & first_lane, 0.0, f_l)
            if j == nct - 1:
                f_r = jnp.where(~has_r & last_lane, 0.0, f_r)
            off = 0.5 * ((f_u + f_d) + (f_l + f_r))
            ratio = off / (base_t[j, 8 * i : 8 * i + 8, :] + off)
            peak = ratio if peak is None else jnp.maximum(peak, ratio)
    msend[...] = jnp.full((1, 128), jnp.max(peak), F32)

    for k in far_first(ndev, lambda k: k % n_gy // 2 + (k // n_gy).bit_count()):
        t = partner(me, k, ndev)
        remote(
            msend, mrecv.at[k - 1], s_sem.at[0], r_sem.at[8], (t // n_gy, t % n_gy)
        ).start()

    orows = 16
    n_swap = sum(jnp.where(came, 1, 0) for _, came, _ in swaps)
    for n in range(1, 2 * hz + 1):
        done_if(n_swap == n, r_sem.at[5], n * size(mine))
    reach = hz * rpd

    def gather(q, ref, fill):
        for b in range(2 * hz + 1):
            value = ref[b]
            if b != hz:
                there = me >= hz - b if b < hz else me + (b - hz) < ndev
                value = jnp.where(there, value, fill)
            field[q, rpd * b : rpd * b + rpd, :] = value

    for q in range(3):
        gather(q, own3.at[q], 1.0)
    rest = (2 * hz + 1) * rpd
    for q in range(4):
        field[q, rest:orows, :] = jnp.full((orows - rest, span), 0.0 if q == 3 else 1.0, F32)

    short_t = jnp.where(gx == 0, jnp.maximum(hz - gy, 0), 0)
    short_b = jnp.where(gx == n_gx - 1, jnp.maximum(hz - (n_gy - 1 - gy), 0), 0)
    for a in range(hz + 1):
        for b in range(hz + 1):
            got = owc.at[pl.ds(a, 2 * hz + 1 - a - b)]

            @pl.when((short_t == a) & (short_b == b))
            def _():
                pltpu.make_async_copy(got, got, r_sem.at[7]).wait()

    gather(3, owc, 0.0)
    oshape = (orows, span)
    row_g = me * rpd - reach + row_iota(oshape)
    col_g = lane_iota(oshape)
    total_rows = ndev * rpd

    def four(x):
        return (
            pltpu.roll(x, 1, 0),
            pltpu.roll(x, orows - 1, 0),
            pltpu.roll(x, 1, 1),
            pltpu.roll(x, span - 1, 1),
        )

    inside = (row_g >= 0) & (row_g < total_rows)
    masks = (
        inside & (row_g >= 1),
        inside & (row_g <= total_rows - 2),
        col_g >= 1,
        col_g <= span - 2,
    )
    cond = field[3]
    faces = [jnp.where(m, 0.5 * (cond + nb), 0.0) for m, nb in zip(masks, four(cond))]
    diagonal = field[1] + (faces[0] + faces[1] + faces[2] + faces[3])
    inv = 1.0 / diagonal
    t_all = field[0]
    near = sum(f * nb for f, nb in zip(faces, four(t_all)))
    z = (field[2] - (diagonal * t_all - near)) * inv
    faces = [f * inv for f in faces]
    for j in range(4):
        if j:
            z = z - sum(f * nb for f, nb in zip(faces, four(z)))
        zown[j] = z[reach : reach + rpd, :]

    pltpu.make_async_copy(mrecv, mrecv, r_sem.at[8]).wait()
    peak = jnp.maximum(jnp.max(mrecv[...], axis=0), msend[...])[0:1, :]
    low, high = 1.0 - peak, 1.0 + peak
    center = 0.5 * (high + low)
    spread = 0.5 * (high - low)
    sigma = center / spread
    rho = 1.0 / sigma
    zero = jnp.zeros_like(center)
    e = [zero + 1.0, zero, zero, zero]
    d = [1.0 / center, zero, zero, zero]
    total = list(d)
    for _ in range(3):
        e = [e[0]] + [e[i] - d[i - 1] for i in range(1, 4)]
        rho_next = 1.0 / (2.0 * sigma - rho)
        d = [rho_next * rho * d[i] + (2.0 * rho_next / spread) * e[i] for i in range(4)]
        total = [a + b for a, b in zip(total, d)]
        rho = rho_next
    for t in range(span // 128):
        cols = slice(128 * t, 128 * t + 128)
        x = warm[:, cols]
        for j in range(4):
            x = x + total[j] * zown[j, :, cols]
        o_warm[:, cols] = x

    for ok, _, copy in swaps:
        sent_if(ok, copy)
    always = (n_gy - 1) * (size(tsend.at[0]) + size(asend.at[0])) + (ndev - 1)
    blocks = [min(n_gy, t + hz + 1) - max(0, t - hz) for t in range(n_gy)]
    one = size(cb4.at[0])
    for t in range(n_gy):
        done_if(gy == t, s_sem.at[0], always + one * (sum(blocks) - blocks[t]))
    tall = size(rowsend.at[0]) + far_size + size(erow.at[0]) + one * (hz * (hz + 1) // 2)
    for i, ok in ((1, has_u), (2, has_d)):
        for h in (1, 2):
            done_if(ok & (n_h == h), s_sem.at[i], tall + h * size(ck.at[0]))
    for i, ok in ((3, has_l), (4, has_r)):
        done_if(ok, s_sem.at[i], size(pk.at[0]) + size(ecol.at[0]))


def put_out(su, speed, dam, warm, o_shift, o_speed, o_dam, o_warm, sem):
    nt, hh = dam.shape[1:3]
    for t in range(nt):
        cols = slice(128 * t, 128 * t + 128)
        for i, (src, dst) in enumerate(
            (
                (su.at[:, t, HALO : HALO + hh, :], o_shift.at[:, :, cols]),
                (speed.at[:, t], o_speed.at[:, :, cols]),
                (dam.at[:, t], o_dam.at[:, :, cols]),
            )
        ):
            pltpu.make_async_copy(src, dst, sem.at[i]).start()
    last = pltpu.make_async_copy(warm, o_warm, sem.at[3])
    last.start()
    for i, dst in enumerate((o_shift, o_speed, o_dam)):
        pltpu.make_async_copy(dst, dst, sem.at[i]).wait()
    last.wait()


def per_device(n_gx, n_gy, shift, speed, level, mark, warm, store, film, bath):
    _, hh, ww = shift.shape
    rpd, _ = warm.shape
    cw, ch = ww // 2, hh // 2
    wide = cw + 128
    nt, nct = ww // 128, cw // 128
    ntile = nt + 1
    crows, frows = ch + 16, hh + 2 * HALO
    nsl = n_gy + 2 * (HALO // rpd)
    hz = HALO // 2 // rpd
    vm = lambda *s: pltpu.VMEM(s, F32)
    dma = lambda n: pltpu.SemaphoreType.DMA((n,))
    hbm = pl.BlockSpec(memory_space=pltpu.HBM)
    vmem = pl.BlockSpec(memory_space=pltpu.VMEM)
    outs = pl.pallas_call(
        functools.partial(kernel, n_gx, n_gy),
        out_shape=(
            vm(2, ntile, frows, 128),
            vm(2, nt, hh, 128),
            pltpu.VMEM((2, nt, hh, 128), jnp.bfloat16),
            vm(*warm.shape),
        ),
        in_specs=[hbm] * 8,
        out_specs=(vmem,) * 4,
        scratch_shapes=[
            vm(n_gy, rpd, wide),
            vm(nsl, rpd, wide),
            vm(n_gy, rpd, cw),
            vm(n_gy, rpd, cw),
            vm(2, hh, 128),
            vm(2, hh, 128),
            vm(4, 8, 128),
            vm(2, 45 * nt + 1, 128),
            vm(2, 45 * nt + 1, 128),
            vm(2, 2, ntile, 32, 128),
            vm(2, 2, ntile, 32, 128),
            vm(2, 2, ntile, 32, 128),
            vm(2, 2, ntile, 40, 128),
            vm(SUBSTEPS, 2, 6, ntile, 8, 128),
            vm(SUBSTEPS, 2, 2, ntile, 8, 128),
            pltpu.VMEM(level.shape, level.dtype),
            vm(*warm.shape),
            vm(*warm.shape),
            vm(*warm.shape),
            vm(*warm.shape),
            vm(2, ntile, frows, 128),
            vm(2, ntile, frows, 128),
            vm(frows, 128),
            vm(frows, 128),
            vm(ntile, frows, 128),
            vm(ntile, frows, 128),
            vm(ntile, frows, 128),
            vm(2, ntile, frows + 8, 128),
            vm(nct + 1, crows, 128),
            vm(nct + 1, frows, 128),
            vm(256, 128),
            vm(nt, hh, 128),
            vm(nct, ch, 128),
            vm(nct, crows, 128),
            vm(2, 1, cw),
            vm(2, 1, cw),
            vm(2, 8, 128),
            vm(2, 8, 128),
            vm(n_gy, rpd, cw),
            vm(2 * hz + 1, rpd, cw * n_gy),
            vm(3, 2 * hz + 1, rpd, cw * n_gy),
            vm(4, 16, cw * n_gy),
            vm(4, rpd, cw * n_gy),
            vm(1, 128),
            vm(n_gx * n_gy - 1, 1, 128),
            dma(5 + 2 * hz),
            dma(13),
            vm(3 * level.size // 128, 1, 128),
            pltpu.SMEM((1, hh // SR), mark.dtype),
        ],
        compiler_params=pltpu.CompilerParams(
            collective_id=0, has_side_effects=True
        ),
    )(shift, speed, level, mark.reshape(1, hh // SR), warm, store, film, bath)
    return pl.pallas_call(
        put_out,
        out_shape=tuple(
            jax.ShapeDtypeStruct(o.shape, d)
            for o, d in ((shift, F32), (speed, F32), (level, jnp.bfloat16), (warm, F32))
        ),
        in_specs=[vmem] * 4,
        out_specs=(hbm,) * 4,
        scratch_shapes=[dma(4)],
    )(*(pltpu.with_memory_space_constraint(o, pltpu.VMEM) for o in outs))


def solution(mesh):
    rows = P(("gx", "gy"), None)
    plate = P(None, "gx", "gy")
    return jax.shard_map(
        functools.partial(per_device, mesh.shape["gx"], mesh.shape["gy"]),
        mesh=mesh,
        in_specs=(plate, plate, plate, P("gx", "gy"), rows, rows, rows, rows),
        out_specs=(plate, plate, plate, rows),
        check_vma=False,
    )
```

```python
import functools
import math

import jax
import jax.numpy as jnp
from jax import lax
from jax.experimental import pallas as pl
from jax.experimental.pallas import tpu as pltpu
from jax.sharding import PartitionSpec as P

SR = 8
SEG = 128
SUBSTEPS = 8
HALO = 8
FIELDS = 7
MESH = pl.DeviceIdType.MESH
F32 = jnp.float32


def lane_iota(shape):
    return lax.broadcasted_iota(jnp.int32, shape, 1)


def row_iota(shape):
    return lax.broadcasted_iota(jnp.int32, shape, 0)


def full_dot(a, b):
    return jnp.dot(a, b, precision=lax.Precision.HIGH, preferred_element_type=F32)


def partner(me, k, n):
    if n & (n - 1):
        return lax.rem(me + k, n)
    t = me
    for b in range(n.bit_length() - 1):
        if k >> b & 1:
            t = t + (1 - 2 * (me // 2**b % 2)) * 2**b
    return t


def far_first(n, hops):
    return sorted(range(1, n), key=lambda k: (-hops(k), -k))


def pick(x, index):
    return jnp.take_along_axis(x, index, axis=1)


def kernel(
    n_gx,
    n_gy,
    shift,
    speed,
    level_h,
    mark_h,
    warm_h,
    store_h,
    film_h,
    bath_h,
    su,
    o_speed,
    o_dam,
    o_warm,
    tsend,
    trecv,
    asend,
    arecv,
    pk,
    rk,
    ck,
    rowsend,
    rowrecv,
    bu,
    bv,
    bs,
    bn,
    past,
    past_n,
    way,
    level,
    warm,
    store,
    film,
    bath,
    sv,
    ss,
    kw,
    kh,
    tx,
    ty,
    fine,
    nx,
    tcx,
    widebuf,
    tab_s,
    gap,
    base_t,
    cpad,
    erow,
    grow_c,
    ecol,
    gcol_c,
    cb4,
    owc,
    own3,
    field,
    zown,
    msend,
    mrecv,
    s_sem,
    r_sem,
    meter,
    mark,
):
    ndev = n_gx * n_gy
    gx = lax.axis_index("gx")
    gy = lax.axis_index("gy")
    me = gx * n_gy + gy
    _, hh, ww = shift.shape
    rpd, _ = warm_h.shape
    cw = ww // 2
    ch = hh // 2
    hb = HALO // rpd
    nsl = n_gy + 2 * hb
    nt = ww // 128
    ntile = nt + 1
    nct = cw // 128
    frows = hh + 2 * HALO
    nstrip = frows // 8
    up = lax.rem(gx + n_gx - 1, n_gx)
    down = lax.rem(gx + 1, n_gx)
    left = lax.rem(gy + n_gy - 1, n_gy)
    right = lax.rem(gy + 1, n_gy)
    has_u, has_d = gx > 0, gx < n_gx - 1
    has_l, has_r = gy > 0, gy < n_gy - 1
    hz = HALO // 2 // rpd
    span = cw * n_gy
    own_r = slice(HALO, HALO + hh)

    n_v = jnp.where(has_u, 1, 0) + jnp.where(has_d, 1, 0)
    n_h = jnp.where(has_l, 1, 0) + jnp.where(has_r, 1, 0)

    def size(ref):
        return math.prod(ref.shape) // 128

    def done(sem, lines):
        part = meter.at[pl.ds(0, lines)]
        pltpu.make_async_copy(part, part, sem).wait()

    def done_if(cond, sem, lines):
        if lines:

            @pl.when(cond)
            def _():
                done(sem, lines)

    barrier = pltpu.get_barrier_semaphore()
    warm_load = pltpu.make_async_copy(warm_h, warm, r_sem.at[9])
    warm_load.start()

    def greet(a, b):
        pl.semaphore_signal(barrier, inc=1, device_id=(a, b), device_id_type=MESH)

    for k in far_first(n_gy, lambda k: k // 2):
        greet(gx, partner(gy, k, n_gy))
    calls = n_gy - 1
    detour = n_gx == 4
    if detour:
        calls = calls + jnp.where((gx == 1) | (gx == 2), 1, 0)

        @pl.when((gx == 0) | (gx == 3))
        def _():
            greet(lax.rem(gx + 2, n_gx), gy)

    for k in range(1, n_gx):
        if k == 1 or k > 3:
            for ok, a in ((gx >= k, gx - k), (gx + k < n_gx, gx + k)):
                sides = ((True, gy), (has_l, left), (has_r, right)) if k == 1 else ((True, gy),)
                for beside, b in sides:
                    calls = calls + jnp.where(ok & beside, 1, 0)

                    @pl.when(ok & beside)
                    def _():
                        greet(a, b)

    loads = [
        pltpu.make_async_copy(src, dst, r_sem.at[i])
        for src, dst, i in (
            (mark_h, mark, 1),
            (level_h, level, 10),
            (store_h, store, 11),
            (film_h, film, 11),
            (bath_h, bath, 11),
        )
    ]
    loads[0].start()
    loads[1].start()
    for src, dst in ((shift, su), (speed, sv)):
        for t in range(nt):
            pltpu.make_async_copy(
                src.at[:, :, 128 * t : 128 * t + 128], dst.at[:, t, own_r, :], r_sem.at[10]
            ).start()
    for copy in loads[2:]:
        copy.start()

    lane_c = lane_iota((rpd, 128))

    def chunk(value, k):
        after = value[:, (cw * (k + 1)) % (cw * n_gy) :][:, 0:128]
        before = value[:, (cw * k - 128) % (cw * n_gy) :][:, 0:128]
        return value[:, cw * k : cw * k + cw], jnp.where(lane_c < 64, after, before)

    def remote(src, dst, ssem, rsem, where):
        return pltpu.make_async_remote_copy(
            src_ref=src, dst_ref=dst, send_sem=ssem, recv_sem=rsem, device_id=where,
            device_id_type=MESH,
        )

    warm_load.wait()
    t_own = warm[...]
    for k in range(n_gy):
        main, edge = chunk(t_own, k)
        tsend[k, :, 0:cw] = main
        tsend[k, :, cw : cw + 128] = edge

    sharp = -4.0 * math.log2(math.e)
    lane = lane_iota((hh, 128))
    loads[0].wait()
    done(r_sem.at[10], 3 * size(level))
    for s in range(hh // SR):
        kw[HALO + SR * s : HALO + SR * s + SR, :] = (
            jnp.full((SR, 128), mark[0, s], jnp.int32).astype(F32) * sharp
        )
    w_own = kw[own_r, :] * (0.125 / sharp)
    grow = gx * hh + row_iota((hh, 128))
    for t in range(nt):
        cols = slice(128 * t, 128 * t + 128)
        gcol = gy * ww + 128 * t + lane
        ss[0, t, own_r, :] = jnp.where(grow >= 1, 1.0 - level[0, :, cols].astype(F32) * w_own, 0.0)
        ss[1, t, own_r, :] = jnp.where(gcol >= 1, 1.0 - level[1, :, cols].astype(F32) * w_own, 0.0)
    for c in range(2):
        for t in range(nt):
            sv[c, t, own_r, :] = 0.4 * sv[c, t, own_r, :]
    lines_of = (8, 8, 7, 7, 8, 7)
    line_at = [nt * sum(lines_of[:f]) for f in range(7)]
    acc_l = jnp.zeros((hh, 128), F32)
    acc_r = jnp.zeros((hh, 128), F32)
    fields = [(ref, c) for ref in (su, sv, ss) for c in range(2)]
    for f in range(FIELDS):
        if f < 6:
            ref, c = fields[f]
            first, last = ref[c, 0, own_r, :], ref[c, nt - 1, own_r, :]
        else:
            first = last = kw[own_r, :]
        here = (lane >= 8 * f) & (lane < 8 * f + 8)
        first = pltpu.roll(first, 8 * f, 1) if f else first
        acc_l = jnp.where(here, first, acc_l)
        acc_r = jnp.where(here, pltpu.roll(last, 8 * f + 8, 1), acc_r)
    pk[0] = acc_l
    pk[1] = acc_r
    side_l = remote(pk.at[0], rk.at[1], s_sem.at[3], r_sem.at[0], (gx, left))
    side_r = remote(pk.at[1], rk.at[0], s_sem.at[4], r_sem.at[0], (gx, right))
    top, end = slice(0, 8), slice(hh - 8, hh)
    corners = [
        (has_u & has_l, remote(pk.at[0, top], ck.at[3], s_sem.at[1], r_sem.at[2], (up, left)), 2),
        (has_u & has_r, remote(pk.at[1, top], ck.at[2], s_sem.at[1], r_sem.at[2], (up, right)), 3),
        (has_d & has_l, remote(pk.at[0, end], ck.at[1], s_sem.at[2], r_sem.at[2], (down, left)), 4),
        (has_d & has_r, remote(pk.at[1, end], ck.at[0], s_sem.at[2], r_sem.at[2], (down, right)), 5),
    ]
    n_lines = rowsend.shape[1]
    turn = 96 if n_gx == 4 else n_lines
    head, rest = pl.ds(0, turn), pl.ds(turn, n_lines - turn)
    row_sends = [
        (has_u, remote(rowsend.at[0, head], rowrecv.at[1, head], s_sem.at[1], r_sem.at[2], (up, gy))),
        (has_d, remote(rowsend.at[1, head], rowrecv.at[0, head], s_sem.at[2], r_sem.at[2], (down, gy))),
    ]
    if detour:
        across = lax.rem(gx + 2, n_gx)
        for straight, around, side, sem, to in (
            (has_u & (gx != 2), gx == 2, 0, 1, up),
            (has_d & (gx != 1), gx == 1, 1, 2, down),
        ):
            src = rowsend.at[side, rest]
            row_sends += [
                (around, remote(src, way, s_sem.at[sem], r_sem.at[13], (across, gy))),
                (straight, remote(src, rowrecv.at[1 - side, rest], s_sem.at[sem], r_sem.at[2], (to, gy))),
            ]
        pass_on = [
            (gx == 0, remote(way, rowrecv.at[1, rest], s_sem.at[5 + 2 * hz], r_sem.at[2], (down, gy))),
            (gx == 3, remote(way, rowrecv.at[0, rest], s_sem.at[5 + 2 * hz], r_sem.at[2], (up, gy))),
        ]
    sends = [(has_l, side_l), (has_r, side_r)] + [(a, b) for a, b, _ in corners]
    sends += row_sends

    def start_if(cond, copy):
        @pl.when(cond)
        def _():
            copy.start()

    def sent_if(cond, copy):
        @pl.when(cond)
        def _():
            copy.wait_send()

    for side, at in ((0, HALO), (1, HALO + hh - 8)):
        for f, (ref, c) in enumerate(fields):
            skip = side if lines_of[f] == 7 else 0
            for t in range(nt):
                to = line_at[f] + lines_of[f] * t
                rowsend[side, to : to + lines_of[f], :] = ref[
                    c, t, at + skip : at + skip + lines_of[f], :
                ]
        rowsend[side, line_at[6] : line_at[6] + 1, :] = kw[at : at + 1, :]
    pl.semaphore_wait(barrier, calls)

    for k in far_first(n_gy, lambda k: k // 2):
        t = partner(gy, k, n_gy)
        remote(tsend.at[t], trecv.at[gy + hb], s_sem.at[0], r_sem.at[3], (gx, t)).start()
    pltpu.make_async_copy(tsend.at[gy], trecv.at[gy + hb], r_sem.at[3]).start()

    for cond, copy in sends[6:]:
        start_if(cond, copy)
    for cond, copy in sends[0:6]:
        start_if(cond, copy)

    k_i, n_i = row_iota((256, 128)), lane_iota((256, 128))
    pos = (k_i % SEG).astype(F32)
    col = (2 * (n_i % 64)).astype(F32)
    tab = jnp.exp(jnp.abs(pos - col) * (-4.0 / SEG)) + jnp.exp(jnp.abs(pos - col - 1.0) * (-4.0 / SEG))
    tab_s[...] = jnp.where(k_i // SEG == n_i // 64, tab * (1.0 / SEG), 0.0)
    done(r_sem.at[11], 3 * size(store))
    base = store[...] + film[...]
    own3[0, hz] = t_own
    own3[1, hz] = base
    own3[2, hz] = store[...] * t_own + film[...] * bath[...]
    for k in range(n_gy):
        asend[k] = base[:, cw * k : cw * k + cw]
    strip = (nstrip - 2) * 8
    nx[:, :, strip : strip + 8, :] = jnp.zeros((2, ntile, 8, 128), F32)
    bn[:, :, :, 32:40, :] = jnp.zeros((2, 2, ntile, 8, 128), F32)

    for h in (1, 2):
        done_if(n_h == h, r_sem.at[0], h * size(pk.at[0]))

    def unpack(got_l, got_r, targets, rows, lines, outside):
        shape = got_l.shape
        lanes = lane_iota(shape)
        gone = outside | (~has_l & (lanes >= 64)) | (~has_r & (lanes < 64))
        for f in range(FIELDS):
            from_r = pltpu.roll(got_r, 128 - 8 * f, 1) if f else got_r
            from_l = pltpu.roll(got_l, 120 - 8 * f, 1)
            side = jnp.where(lanes < 8, from_r, jnp.where(lanes >= 120, from_l, 0.0))
            side = jnp.where(gone, 0.0, side)
            if f < 6:
                ref, c = targets[f]
                ref[c, nt, rows, :] = side
            else:
                kh[lines, :] = side

    unpack(rk[0], rk[1], fields, own_r, own_r, False)
    rims = [
        [(ref.at[side], c) for ref in (bu, bv, bs) for c in range(2)] for side in range(2)
    ]
    for side, (at, to) in enumerate(((8, 8), (frows - 16, 16))):
        for (ref, c), (rim, _) in zip(fields, rims[side]):
            for t in range(ntile):
                rim[c, t, to : to + 8, :] = ref[c, t, at : at + 8, :]

    if detour:
        done_if((gx == 0) | (gx == 3), r_sem.at[13], size(way))
        for cond, copy in pass_on:
            start_if(cond, copy)
    mid = trecv.at[pl.ds(hb, n_gy)]
    pltpu.make_async_copy(mid, mid, r_sem.at[3]).wait()
    far_u = remote(
        trecv.at[pl.ds(hb, hb)], trecv.at[pl.ds(hb + n_gy, hb)], s_sem.at[1], r_sem.at[12], (up, gy)
    )
    far_d = remote(
        trecv.at[pl.ds(n_gy, hb)], trecv.at[pl.ds(0, hb)], s_sem.at[2], r_sem.at[12], (down, gy)
    )
    start_if(has_u, far_u)
    start_if(has_d, far_d)

    for k in range(1, n_gy):
        t = partner(gy, k, n_gy)
        remote(asend.at[t], arecv.at[gy], s_sem.at[0], r_sem.at[4], (gx, t)).start()
    pltpu.make_async_copy(asend.at[gy], arecv.at[gy], r_sem.at[4]).start()
    mine = own3.at[:, hz]
    swaps = []
    for d in range(1, hz + 1):
        for i, to, ok, came in (
            (d - 1, me + d, me + d < ndev, me >= d),
            (hz + d - 1, me - d, me >= d, me + d < ndev),
        ):
            at = hz - d if i < hz else hz + d
            to = lax.rem(to + ndev, ndev)
            copy = remote(mine, own3.at[:, at], s_sem.at[5 + i], r_sem.at[5], (to // n_gy, to % n_gy))
            swaps.append((ok, came, copy))
    for ok, _, copy in swaps:
        start_if(ok, copy)
    lane8 = lane_iota((8, 128))
    first_lane, last_lane = lane8 == 0, lane8 == 127

    def close_edge(rows):
        edge = tcx[nct, rows, :]
        edge = jnp.where(~has_l & last_lane, pltpu.roll(tcx[0, rows, :], 127, 1), edge)
        edge = jnp.where(~has_r & first_lane, pltpu.roll(tcx[nct - 1, rows, :], 1, 1), edge)
        tcx[nct, rows, :] = edge

    for k in range(hb, hb + n_gy):
        for j in range(nct + 1):
            tcx[j, rpd * k : rpd * k + rpd, :] = trecv[k, :, 128 * j : 128 * j + 128]
    for c in range(8, 8 + ch, 8):
        close_edge(slice(c, c + 8))
    half = lane8 // 2
    step = jnp.where(lane8 % 2 == 0, -1, 1)
    lo_g, lo_h = half, jnp.maximum(half + step, 0)
    hi_g, hi_h = half + 64, jnp.minimum(half + 64 + step, 127)
    ed_g = jnp.where(lane8 < 64, half, half + 64)
    ed_h = jnp.minimum(jnp.maximum(ed_g + step, 0), 127)

    def before(tiles):
        turned = [pltpu.roll(x, 1, 1) for x in tiles]
        return [jnp.where(first_lane, turned[t - 1], turned[t]) for t in range(len(tiles))]

    def after(tiles):
        turned = [pltpu.roll(x, 127, 1) for x in tiles]
        n = len(tiles)
        return [jnp.where(last_lane, turned[(t + 1) % n], turned[t]) for t in range(n)]

    def above(ref, s):
        return ref[8 * s - 1 : 8 * s + 7, :] if s else pltpu.roll(ref[0:8, :], 1, 0)

    def heat_x(s):
        rows = slice(8 * s, 8 * s + 8)
        for t in range(ntile):
            tx[t, rows, :] = 0.3 * (fine[t, rows, :] + above(fine.at[t], s))

    def prolong(p):
        c = 8 * p + 4
        for j in range(nct + 1):
            here = 0.75 * tcx[j, c : c + 8, :]
            widebuf[j, pl.ds(16 * p, 8, stride=2), :] = here + 0.25 * tcx[j, c - 1 : c + 7, :]
            widebuf[j, pl.ds(16 * p + 1, 8, stride=2), :] = here + 0.25 * tcx[j, c + 1 : c + 9, :]
        for s in (2 * p, 2 * p + 1):
            rows = slice(8 * s, 8 * s + 8)
            r = [widebuf[j, rows, :] for j in range(nct + 1)]
            fwd = [pltpu.roll(x, 1, 1) for x in r]
            bwd = [pltpu.roll(x, 127, 1) for x in r]
            f = []
            for j in range(nct):
                f.append(
                    0.75 * pick(r[j], lo_g)
                    + 0.25 * jnp.where(first_lane, fwd[j - 1], pick(r[j], lo_h))
                )
                f.append(
                    0.75 * pick(r[j], hi_g)
                    + 0.25 * jnp.where(last_lane, bwd[j + 1], pick(r[j], hi_h))
                )
            e = pick(r[nct], ed_h)
            e = jnp.where(first_lane, fwd[nct - 1], jnp.where(last_lane, bwd[0], e))
            f.append(0.75 * pick(r[nct], ed_g) + 0.25 * e)
            prev = before(f)
            for t in range(ntile):
                fine[t, rows, :] = f[t]
                ty[t, rows, :] = 0.3 * (f[t] + prev[t])

    npair = nstrip // 2
    for p in range(1, npair - 1):
        prolong(p)
    for s in range(2, nstrip - 2):
        heat_x(s)

    def edges(s):
        rows = slice(8 * s, 8 * s + 8)
        u0 = [su[0, t, rows, :] for t in range(ntile)]
        u1 = [su[1, t, rows, :] for t in range(ntile)]
        k_main, k_side = kw[rows, :], kh[rows, :]
        b0, b1 = before(u0), before(u1)
        ay, ny = [], []
        for t in range(ntile):
            k = k_main if t < nt else k_side
            open_x = u0[t] - above(su.at[0, t], s) - tx[t, rows, :]
            st = jnp.maximum(open_x, 0.0)
            sp = jnp.minimum(ss[0, t, rows, :], jnp.exp2(st * st * k))
            ss[0, t, rows, :] = sp
            nx[0, t, rows, :] = sp * open_x
            nx[1, t, rows, :] = sp * (u1[t] - above(su.at[1, t], s))
            open_y = u1[t] - b1[t] - ty[t, rows, :]
            st = jnp.maximum(open_y, 0.0)
            sp = jnp.minimum(ss[1, t, rows, :], jnp.exp2(st * st * k))
            ss[1, t, rows, :] = sp
            ny.append(sp * open_y)
            ay.append(sp * (u0[t] - b0[t]))
        fy0 = [a - b for a, b in zip(after(ay), ay)]
        fy1 = [a - b for a, b in zip(after(ny), ny)]
        return fy0, fy1

    def advance(s, fy):
        rows = slice(8 * s, 8 * s + 8)
        below = slice(8 * s + 1, 8 * s + 9)
        for c in range(2):
            for t in range(ntile):
                force = (nx[c, t, below, :] - nx[c, t, rows, :]) + fy[c][t]
                v = 0.98 * sv[c, t, rows, :] + 0.16 * force
                sv[c, t, rows, :] = v
                su[c, t, rows, :] = su[c, t, rows, :] + v

    def interior(i, carry):
        for f, (ref, c) in enumerate(fields):
            at = frows - 24 + (f == 4)
            for t in range(ntile):
                past[i, 0, f, t] = ref[c, t, 16:24, :]
                past[i, 1, f, t] = ref[c, t, at : at + 8, :]
        old = None
        for s in range(2, nstrip - 2):
            new = edges(s)
            if old:
                advance(s - 1, old)
            old = new
        advance(nstrip - 3, old)
        for c in range(2):
            for t in range(ntile):
                past_n[i, 0, c, t] = nx[c, t, 17:25, :]
                past_n[i, 1, c, t] = nx[c, t, frows - 24 : frows - 16, :]
        return carry

    lax.fori_loop(0, SUBSTEPS, interior, 0)

    far_size = hb * size(trecv.at[0])
    for v in (1, 2):
        for h in (1, 2):
            done_if(
                (n_v == v) & (n_h == h),
                r_sem.at[2],
                v * (size(rowsend.at[0]) + h * size(ck.at[0])),
            )
    for side, (here, at, to) in enumerate(((has_u, 0, 0), (has_d, hh + HALO, 24))):
        rows = slice(to, to + 8)
        lines = slice(at, at + 8)
        for f, (rim, c) in enumerate(rims[side]):
            first = to if side or lines_of[f] == 8 else to + 1
            for t in range(nt):
                line = line_at[f] + lines_of[f] * t
                got = rowrecv[side, line : line + lines_of[f], :]
                rim[c, t, first : first + lines_of[f], :] = jnp.where(here, got, 0.0)
        got = jnp.broadcast_to(rowrecv[side, line_at[6] : line_at[6] + 1, :], (8, 128))
        kw[lines, :] = jnp.where(here, got, 0.0)
        unpack(ck[2 * side], ck[2 * side + 1], rims[side], rows, lines, ~here)
    for v in (1, 2):
        done_if(n_v == v, r_sem.at[12], v * far_size)
    for side, (here, at, slot, line) in enumerate(
        ((has_u, 0, 0, 8), (has_d, ch + 8, hb + n_gy, ch + 7))
    ):

        @pl.when(here)
        def _():
            for k in range(hb):
                for j in range(nct + 1):
                    tcx[j, at + rpd * k : at + rpd * k + rpd, :] = trecv[
                        slot + k, :, 128 * j : 128 * j + 128
                    ]
            close_edge(slice(at, at + 8))

        @pl.when(jnp.logical_not(here))
        def _():
            for j in range(nct + 1):
                tcx[j, at : at + 8, :] = jnp.broadcast_to(tcx[j, line : line + 1, :], (8, 128))

    prolong(0)
    prolong(npair - 1)
    for s in (0, 1, 2, nstrip - 2, nstrip - 1):
        heat_x(s)

    for t in range(ntile):
        bs[1, 0, t, 8:9, :] = ss[0, t, frows - 24 : frows - 23, :]

    def rim_edges(side, x, y):
        shift_by = (frows - 32) * side
        u, spring, flow = bu.at[side], bs.at[side], bn.at[side]
        ex, ex_up, ey = pl.ds(x, 8), pl.ds(x - 1, 8), pl.ds(y, 8)
        gx_rows, gy_rows = pl.ds(x + shift_by, 8), pl.ds(y + shift_by, 8)
        u0 = [u[0, t, ey, :] for t in range(ntile)]
        u1 = [u[1, t, ey, :] for t in range(ntile)]
        b0, b1 = before(u0), before(u1)
        kx = [kw[gx_rows, :], kh[gx_rows, :]]
        ky = [kw[gy_rows, :], kh[gy_rows, :]]
        ay, ny = [], []
        for t in range(ntile):
            open_x = u[0, t, ex, :] - u[0, t, ex_up, :] - tx[t, gx_rows, :]
            st = jnp.maximum(open_x, 0.0)
            sp = jnp.minimum(spring[0, t, ex, :], jnp.exp2(st * st * kx[t // nt]))
            spring[0, t, ex, :] = sp
            flow[0, t, ex, :] = sp * open_x
            flow[1, t, ex, :] = sp * (u[1, t, ex, :] - u[1, t, ex_up, :])
            open_y = u1[t] - b1[t] - ty[t, gy_rows, :]
            st = jnp.maximum(open_y, 0.0)
            sp = jnp.minimum(spring[1, t, ey, :], jnp.exp2(st * st * ky[t // nt]))
            spring[1, t, ey, :] = sp
            ny.append(sp * open_y)
            ay.append(sp * (u0[t] - b0[t]))
        fy0 = [a - b for a, b in zip(after(ay), ay)]
        fy1 = [a - b for a, b in zip(after(ny), ny)]
        return fy0, fy1

    def rim_advance(side, y, fy):
        rows, below = pl.ds(y, 8), pl.ds(y + 1, 8)
        for c in range(2):
            for t in range(ntile):
                force = (bn[side, c, t, below, :] - bn[side, c, t, rows, :]) + fy[c][t]
                v = 0.98 * bv[side, c, t, rows, :] + 0.16 * force
                bv[side, c, t, rows, :] = v
                bu[side, c, t, rows, :] = bu[side, c, t, rows, :] + v

    for i in range(SUBSTEPS):
        for t in range(ntile):
            for f in range(6):
                rim, c = rims[0][f]
                rim[c, t, 16 + i : 17 + i, :] = past[i, 0, f, t, i : i + 1, :]
                rim, c = rims[1][f]
                to = 15 - i + (f == 4)
                rim[c, t, to : to + 1, :] = past[i, 1, f, t, 7 - i : 8 - i, :]
            for c in range(2):
                bn[0, c, t, 17 + i : 18 + i, :] = past_n[i, 0, c, t, i : i + 1, :]
                bn[1, c, t, 15 - i : 16 - i, :] = past_n[i, 1, c, t, 7 - i : 8 - i, :]
        for side, x, y in ((0, i + 1, i + 1), (1, 16 - i, 15 - i)):
            first = rim_edges(side, x, y)
            second = rim_edges(side, x + 8, y + 8)
            rim_advance(side, y, first)
            rim_advance(side, y + 8, second)
    def settle(some):
        for side, at in ((0, 8), (1, frows - 24)):
            for (ref, c), (rim, _) in zip(some(fields), some(rims[side])):
                for t in range(nt):
                    ref[c, t, at : at + 16, :] = rim[c, t, 8:24, :]

    settle(lambda x: x[4:6])
    for t in range(nt):
        gcol = gy * ww + 128 * t + lane
        dam_x = jnp.where(grow >= 1, 1.0 - ss[0, t, own_r, :], 0.0)
        dam_y = jnp.where(gcol >= 1, 1.0 - ss[1, t, own_r, :], 0.0)
        gap[t] = dam_x + dam_y
    rows2 = jnp.concatenate(
        [
            gap[t, pl.ds(0, ch, stride=2), :] + gap[t, pl.ds(1, ch, stride=2), :]
            for t in range(ww // 128)
        ],
        axis=1,
    )
    pairs = ww // 256
    glow = full_dot(
        jnp.concatenate([rows2[:, 256 * t : 256 * t + 256] for t in range(pairs)], axis=0), tab_s[...]
    )
    resist = jnp.concatenate([glow[ch * t : ch * t + ch] for t in range(pairs)], axis=1)
    t_tile = jnp.concatenate([tcx[j, 8 : 8 + ch, :] for j in range(nct)], axis=1)
    cond = (1.0 + 0.5 * t_tile) / (1.0 + resist)
    for j in range(nct):
        cpad[j, 8 : 8 + ch, :] = cond[:, 128 * j : 128 * j + 128]
    erow[0] = cond[0:1, :]
    erow[1] = cond[ch - 1 : ch, :]
    first_col, last_col = cond[0:8, 0:128], pltpu.roll(cond[0:8, cw - 128 : cw], 1, 1)
    for i in range(1, ch // 8):
        rows = slice(8 * i, 8 * i + 8)
        here = lane8 == i
        first_col = jnp.where(here, pltpu.roll(cond[rows, 0:128], i, 1), first_col)
        last_col = jnp.where(here, pltpu.roll(cond[rows, cw - 128 : cw], i + 1, 1), last_col)
    ecol[0] = first_col
    ecol[1] = last_col
    beside = [
        (has_u, has_d, remote(erow.at[0], grow_c.at[1], s_sem.at[1], r_sem.at[6], (up, gy))),
        (has_d, has_u, remote(erow.at[1], grow_c.at[0], s_sem.at[2], r_sem.at[6], (down, gy))),
        (has_l, has_r, remote(ecol.at[0], gcol_c.at[1], s_sem.at[3], r_sem.at[6], (gx, left))),
        (has_r, has_l, remote(ecol.at[1], gcol_c.at[0], s_sem.at[4], r_sem.at[6], (gx, right))),
    ]
    for ok, _, copy in beside:
        start_if(ok, copy)
    for b in range(n_gy):
        cb4[b] = cond[rpd * b : rpd * b + rpd, :]
    my_cols = pl.ds(pl.multiple_of(gy * cw, 128), cw)
    to_owner = []
    for t in range(n_gy):
        lo, hi = max(0, t - hz), min(n_gy, t + hz + 1)
        src = cb4.at[pl.ds(lo, hi - lo)]
        dst = owc.at[pl.ds(lo - t + hz, hi - lo), :, my_cols]
        to_owner.append((gy != t, remote(src, dst, s_sem.at[0], r_sem.at[7], (gx, t))))
        here = pltpu.make_async_copy(src, dst, r_sem.at[7])

        @pl.when(gy == t)
        def _():
            here.start()

    for t in range(hz):
        n = hz - t
        src, dst = cb4.at[pl.ds(n_gy - n, n)], owc.at[pl.ds(0, n), :, my_cols]
        to_owner.append((has_d, remote(src, dst, s_sem.at[2], r_sem.at[7], (down, t))))
        src, dst = cb4.at[pl.ds(0, n)], owc.at[pl.ds(2 * hz + 1 - n, n), :, my_cols]
        to_owner.append((has_u, remote(src, dst, s_sem.at[1], r_sem.at[7], (up, n_gy - 1 - t))))
    for ok, copy in to_owner:
        start_if(ok, copy)

    settle(lambda x: x[0:4])
    for c in range(2):
        for t in range(nt):
            o_speed[c, t] = 2.5 * sv[c, t, own_r, :]
    for t in range(nt):
        gcol = gy * ww + 128 * t + lane
        dam_x = jnp.where(grow >= 1, 1.0 - ss[0, t, own_r, :], 0.0)
        dam_y = jnp.where(gcol >= 1, 1.0 - ss[1, t, own_r, :], 0.0)
        o_dam[0, t] = dam_x.astype(jnp.bfloat16)
        o_dam[1, t] = dam_y.astype(jnp.bfloat16)

    pltpu.make_async_copy(arecv, arecv, r_sem.at[4]).wait()
    for k in range(n_gy):
        for j in range(nct):
            base_t[j, rpd * k : rpd * k + rpd, :] = arecv[k, :, 128 * j : 128 * j + 128]
    for v in (1, 2):
        for h in (1, 2):
            done_if(
                (n_v == v) & (n_h == h),
                r_sem.at[6],
                v * size(erow.at[0]) + h * size(ecol.at[0]),
            )
    for j in range(nct):
        cols = slice(128 * j, 128 * j + 128)
        cpad[j, 7:8, :] = jnp.where(has_u, grow_c[0, :, cols], 0.0)
        cpad[j, 8 + ch : 9 + ch, :] = jnp.where(has_d, grow_c[1, :, cols], 0.0)
    from_l, from_r = gcol_c[0], gcol_c[1]
    sub8 = row_iota((8, 128))
    peak = None
    for i in range(ch // 8):
        r0 = 8 + 8 * i
        mid = [cpad[j, r0 : r0 + 8, :] for j in range(nct)]
        fwd = [pltpu.roll(x, 1, 1) for x in mid]
        bwd = [pltpu.roll(x, 127, 1) for x in mid]
        fwd_in = [pltpu.roll(from_l, 128 - i, 1) if i else from_l] + fwd[:-1]
        bwd_in = bwd[1:] + [pltpu.roll(from_r, 127 - i, 1)]
        for j in range(nct):
            c = mid[j]
            f_u = c + cpad[j, r0 - 1 : r0 + 7, :]
            f_d = c + cpad[j, r0 + 1 : r0 + 9, :]
            f_l = c + jnp.where(first_lane, fwd_in[j], fwd[j])
            f_r = c + jnp.where(last_lane, bwd_in[j], bwd[j])
            if i == 0:
                f_u = jnp.where(~has_u & (sub8 == 0), 0.0, f_u)
            if i == ch // 8 - 1:
                f_d = jnp.where(~has_d & (sub8 == 7), 0.0, f_d)
            if j == 0:
                f_l = jnp.where(~has_l & first_lane, 0.0, f_l)
            if j == nct - 1:
                f_r = jnp.where(~has_r & last_lane, 0.0, f_r)
            off = 0.5 * ((f_u + f_d) + (f_l + f_r))
            ratio = off / (base_t[j, 8 * i : 8 * i + 8, :] + off)
            peak = ratio if peak is None else jnp.maximum(peak, ratio)
    msend[...] = jnp.full((1, 128), jnp.max(peak), F32)

    for k in far_first(ndev, lambda k: k % n_gy // 2 + (k // n_gy).bit_count()):
        t = partner(me, k, ndev)
        remote(
            msend, mrecv.at[k - 1], s_sem.at[0], r_sem.at[8], (t // n_gy, t % n_gy)
        ).start()

    orows = 16
    n_swap = sum(jnp.where(came, 1, 0) for _, came, _ in swaps)
    for n in range(1, 2 * hz + 1):
        done_if(n_swap == n, r_sem.at[5], n * size(mine))
    reach = hz * rpd

    def gather(q, ref, fill):
        for b in range(2 * hz + 1):
            value = ref[b]
            if b != hz:
                there = me >= hz - b if b < hz else me + (b - hz) < ndev
                value = jnp.where(there, value, fill)
            field[q, rpd * b : rpd * b + rpd, :] = value

    for q in range(3):
        gather(q, own3.at[q], 1.0)
    rest = (2 * hz + 1) * rpd
    for q in range(4):
        field[q, rest:orows, :] = jnp.full((orows - rest, span), 0.0 if q == 3 else 1.0, F32)

    short_t = jnp.where(gx == 0, jnp.maximum(hz - gy, 0), 0)
    short_b = jnp.where(gx == n_gx - 1, jnp.maximum(hz - (n_gy - 1 - gy), 0), 0)
    for a in range(hz + 1):
        for b in range(hz + 1):
            got = owc.at[pl.ds(a, 2 * hz + 1 - a - b)]

            @pl.when((short_t == a) & (short_b == b))
            def _():
                pltpu.make_async_copy(got, got, r_sem.at[7]).wait()

    gather(3, owc, 0.0)
    oshape = (orows, span)
    row_g = me * rpd - reach + row_iota(oshape)
    col_g = lane_iota(oshape)
    total_rows = ndev * rpd

    def four(x):
        return (
            pltpu.roll(x, 1, 0),
            pltpu.roll(x, orows - 1, 0),
            pltpu.roll(x, 1, 1),
            pltpu.roll(x, span - 1, 1),
        )

    inside = (row_g >= 0) & (row_g < total_rows)
    masks = (
        inside & (row_g >= 1),
        inside & (row_g <= total_rows - 2),
        col_g >= 1,
        col_g <= span - 2,
    )
    cond = field[3]
    faces = [jnp.where(m, 0.5 * (cond + nb), 0.0) for m, nb in zip(masks, four(cond))]
    diagonal = field[1] + (faces[0] + faces[1] + faces[2] + faces[3])
    inv = 1.0 / diagonal
    t_all = field[0]
    near = sum(f * nb for f, nb in zip(faces, four(t_all)))
    z = (field[2] - (diagonal * t_all - near)) * inv
    faces = [f * inv for f in faces]
    for j in range(4):
        if j:
            z = z - sum(f * nb for f, nb in zip(faces, four(z)))
        zown[j] = z[reach : reach + rpd, :]

    pltpu.make_async_copy(mrecv, mrecv, r_sem.at[8]).wait()
    peak = jnp.maximum(jnp.max(mrecv[...], axis=0), msend[...])[0:1, :]
    low, high = 1.0 - peak, 1.0 + peak
    center = 0.5 * (high + low)
    spread = 0.5 * (high - low)
    sigma = center / spread
    rho = 1.0 / sigma
    zero = jnp.zeros_like(center)
    e = [zero + 1.0, zero, zero, zero]
    d = [1.0 / center, zero, zero, zero]
    total = list(d)
    for _ in range(3):
        e = [e[0]] + [e[i] - d[i - 1] for i in range(1, 4)]
        rho_next = 1.0 / (2.0 * sigma - rho)
        d = [rho_next * rho * d[i] + (2.0 * rho_next / spread) * e[i] for i in range(4)]
        total = [a + b for a, b in zip(total, d)]
        rho = rho_next
    for t in range(span // 128):
        cols = slice(128 * t, 128 * t + 128)
        x = warm[:, cols]
        for j in range(4):
            x = x + total[j] * zown[j, :, cols]
        o_warm[:, cols] = x

    for ok, _, copy in swaps:
        sent_if(ok, copy)
    always = (n_gy - 1) * (size(tsend.at[0]) + size(asend.at[0])) + (ndev - 1)
    blocks = [min(n_gy, t + hz + 1) - max(0, t - hz) for t in range(n_gy)]
    one = size(cb4.at[0])
    for t in range(n_gy):
        done_if(gy == t, s_sem.at[0], always + one * (sum(blocks) - blocks[t]))
    tall = size(rowsend.at[0]) + far_size + size(erow.at[0]) + one * (hz * (hz + 1) // 2)
    for i, ok in ((1, has_u), (2, has_d)):
        for h in (1, 2):
            done_if(ok & (n_h == h), s_sem.at[i], tall + h * size(ck.at[0]))
    if detour:
        done_if((gx == 0) | (gx == 3), s_sem.at[5 + 2 * hz], size(way))
    for i, ok in ((3, has_l), (4, has_r)):
        done_if(ok, s_sem.at[i], size(pk.at[0]) + size(ecol.at[0]))


def put_out(su, speed, dam, warm, o_shift, o_speed, o_dam, o_warm, sem):
    nt, hh = dam.shape[1:3]
    for t in range(nt):
        cols = slice(128 * t, 128 * t + 128)
        for i, (src, dst) in enumerate(
            (
                (su.at[:, t, HALO : HALO + hh, :], o_shift.at[:, :, cols]),
                (speed.at[:, t], o_speed.at[:, :, cols]),
                (dam.at[:, t], o_dam.at[:, :, cols]),
            )
        ):
            pltpu.make_async_copy(src, dst, sem.at[i]).start()
    last = pltpu.make_async_copy(warm, o_warm, sem.at[3])
    last.start()
    for i, dst in enumerate((o_shift, o_speed, o_dam)):
        pltpu.make_async_copy(dst, dst, sem.at[i]).wait()
    last.wait()


def per_device(n_gx, n_gy, shift, speed, level, mark, warm, store, film, bath):
    _, hh, ww = shift.shape
    rpd, _ = warm.shape
    cw, ch = ww // 2, hh // 2
    wide = cw + 128
    nt, nct = ww // 128, cw // 128
    ntile = nt + 1
    crows, frows = ch + 16, hh + 2 * HALO
    nsl = n_gy + 2 * (HALO // rpd)
    hz = HALO // 2 // rpd
    vm = lambda *s: pltpu.VMEM(s, F32)
    dma = lambda n: pltpu.SemaphoreType.DMA((n,))
    hbm = pl.BlockSpec(memory_space=pltpu.HBM)
    vmem = pl.BlockSpec(memory_space=pltpu.VMEM)
    outs = pl.pallas_call(
        functools.partial(kernel, n_gx, n_gy),
        out_shape=(
            vm(2, ntile, frows, 128),
            vm(2, nt, hh, 128),
            pltpu.VMEM((2, nt, hh, 128), jnp.bfloat16),
            vm(*warm.shape),
        ),
        in_specs=[hbm] * 8,
        out_specs=(vmem,) * 4,
        scratch_shapes=[
            vm(n_gy, rpd, wide),
            vm(nsl, rpd, wide),
            vm(n_gy, rpd, cw),
            vm(n_gy, rpd, cw),
            vm(2, hh, 128),
            vm(2, hh, 128),
            vm(4, 8, 128),
            vm(2, 45 * nt + 1, 128),
            vm(2, 45 * nt + 1, 128),
            vm(2, 2, ntile, 32, 128),
            vm(2, 2, ntile, 32, 128),
            vm(2, 2, ntile, 32, 128),
            vm(2, 2, ntile, 40, 128),
            vm(SUBSTEPS, 2, 6, ntile, 8, 128),
            vm(SUBSTEPS, 2, 2, ntile, 8, 128),
            vm(45 * nt + 1 - 96, 128),
            pltpu.VMEM(level.shape, level.dtype),
            vm(*warm.shape),
            vm(*warm.shape),
            vm(*warm.shape),
            vm(*warm.shape),
            vm(2, ntile, frows, 128),
            vm(2, ntile, frows, 128),
            vm(frows, 128),
            vm(frows, 128),
            vm(ntile, frows, 128),
            vm(ntile, frows, 128),
            vm(ntile, frows, 128),
            vm(2, ntile, frows + 8, 128),
            vm(nct + 1, crows, 128),
            vm(nct + 1, frows, 128),
            vm(256, 128),
            vm(nt, hh, 128),
            vm(nct, ch, 128),
            vm(nct, crows, 128),
            vm(2, 1, cw),
            vm(2, 1, cw),
            vm(2, 8, 128),
            vm(2, 8, 128),
            vm(n_gy, rpd, cw),
            vm(2 * hz + 1, rpd, cw * n_gy),
            vm(3, 2 * hz + 1, rpd, cw * n_gy),
            vm(4, 16, cw * n_gy),
            vm(4, rpd, cw * n_gy),
            vm(1, 128),
            vm(n_gx * n_gy - 1, 1, 128),
            dma(6 + 2 * hz),
            dma(14),
            vm(3 * level.size // 128, 1, 128),
            pltpu.SMEM((1, hh // SR), mark.dtype),
        ],
        compiler_params=pltpu.CompilerParams(
            collective_id=0, has_side_effects=True
        ),
    )(shift, speed, level, mark.reshape(1, hh // SR), warm, store, film, bath)
    return pl.pallas_call(
        put_out,
        out_shape=tuple(
            jax.ShapeDtypeStruct(o.shape, d)
            for o, d in ((shift, F32), (speed, F32), (level, jnp.bfloat16), (warm, F32))
        ),
        in_specs=[vmem] * 4,
        out_specs=(hbm,) * 4,
        scratch_shapes=[dma(4)],
    )(*(pltpu.with_memory_space_constraint(o, pltpu.VMEM) for o in outs))


def solution(mesh):
    rows = P(("gx", "gy"), None)
    plate = P(None, "gx", "gy")
    return jax.shard_map(
        functools.partial(per_device, mesh.shape["gx"], mesh.shape["gy"]),
        mesh=mesh,
        in_specs=(plate, plate, plate, P("gx", "gy"), rows, rows, rows, rows),
        out_specs=(plate, plate, plate, rows),
        check_vma=False,
    )
```

```python
import functools
import math

import jax
import jax.numpy as jnp
from jax import lax
from jax.experimental import pallas as pl
from jax.experimental.pallas import tpu as pltpu
from jax.sharding import PartitionSpec as P

SR = 8
SEG = 128
SUBSTEPS = 8
HALO = 8
FIELDS = 7
MESH = pl.DeviceIdType.MESH
F32 = jnp.float32


def lane_iota(shape):
    return lax.broadcasted_iota(jnp.int32, shape, 1)


def row_iota(shape):
    return lax.broadcasted_iota(jnp.int32, shape, 0)


def full_dot(a, b):
    return jnp.dot(a, b, precision=lax.Precision.HIGH, preferred_element_type=F32)


def partner(me, k, n):
    if n & (n - 1):
        return lax.rem(me + k, n)
    t = me
    for b in range(n.bit_length() - 1):
        if k >> b & 1:
            t = t + (1 - 2 * (me // 2**b % 2)) * 2**b
    return t


def far_first(n, hops):
    return sorted(range(1, n), key=lambda k: (-hops(k), -k))


def pick(x, index):
    return jnp.take_along_axis(x, index, axis=1)


def kernel(
    n_gx,
    n_gy,
    shift,
    speed,
    level_h,
    mark_h,
    warm_h,
    store_h,
    film_h,
    bath_h,
    su,
    o_speed,
    o_dam,
    o_warm,
    tsend,
    trecv,
    asend,
    arecv,
    pk,
    rk,
    ck,
    rowsend,
    rowrecv,
    bu,
    bv,
    bs,
    bn,
    past,
    past_n,
    level,
    warm,
    store,
    film,
    bath,
    sv,
    ss,
    kw,
    kh,
    tx,
    ty,
    fine,
    nx,
    tcx,
    widebuf,
    tab_s,
    gap,
    base_t,
    cpad,
    erow,
    grow_c,
    ecol,
    gcol_c,
    cb4,
    owc,
    own3,
    field,
    zown,
    msend,
    mrecv,
    s_sem,
    r_sem,
    meter,
    mark,
):
    ndev = n_gx * n_gy
    gx = lax.axis_index("gx")
    gy = lax.axis_index("gy")
    me = gx * n_gy + gy
    _, hh, ww = shift.shape
    rpd, _ = warm_h.shape
    cw = ww // 2
    ch = hh // 2
    hb = HALO // rpd
    nsl = n_gy + 2 * hb
    nt = ww // 128
    ntile = nt + 1
    nct = cw // 128
    frows = hh + 2 * HALO
    nstrip = frows // 8
    up = lax.rem(gx + n_gx - 1, n_gx)
    down = lax.rem(gx + 1, n_gx)
    left = lax.rem(gy + n_gy - 1, n_gy)
    right = lax.rem(gy + 1, n_gy)
    has_u, has_d = gx > 0, gx < n_gx - 1
    has_l, has_r = gy > 0, gy < n_gy - 1
    hz = HALO // 2 // rpd
    span = cw * n_gy
    own_r = slice(HALO, HALO + hh)

    n_v = jnp.where(has_u, 1, 0) + jnp.where(has_d, 1, 0)
    n_h = jnp.where(has_l, 1, 0) + jnp.where(has_r, 1, 0)

    def size(ref):
        return math.prod(ref.shape) // 128

    def done(sem, lines):
        part = meter.at[pl.ds(0, lines)]
        pltpu.make_async_copy(part, part, sem).wait()

    def done_if(cond, sem, lines):
        if lines:

            @pl.when(cond)
            def _():
                done(sem, lines)

    barrier = pltpu.get_barrier_semaphore()
    warm_load = pltpu.make_async_copy(warm_h, warm, r_sem.at[9])
    warm_load.start()

    def greet(a, b):
        pl.semaphore_signal(barrier, inc=1, device_id=(a, b), device_id_type=MESH)

    for k in far_first(n_gy, lambda k: k // 2):
        greet(gx, partner(gy, k, n_gy))
    calls = n_gy - 1
    for k in range(1, n_gx):
        if k == 1 or k > 3:
            for ok, a in ((gx >= k, gx - k), (gx + k < n_gx, gx + k)):
                sides = ((True, gy), (has_l, left), (has_r, right)) if k == 1 else ((True, gy),)
                for beside, b in sides:
                    calls = calls + jnp.where(ok & beside, 1, 0)

                    @pl.when(ok & beside)
                    def _():
                        greet(a, b)

    loads = [
        pltpu.make_async_copy(src, dst, r_sem.at[i])
        for src, dst, i in (
            (mark_h, mark, 1),
            (level_h, level, 10),
            (store_h, store, 11),
            (film_h, film, 11),
            (bath_h, bath, 11),
        )
    ]
    loads[0].start()
    loads[1].start()
    for src, dst in ((shift, su), (speed, sv)):
        for t in range(nt):
            pltpu.make_async_copy(
                src.at[:, :, 128 * t : 128 * t + 128], dst.at[:, t, own_r, :], r_sem.at[10]
            ).start()
    for copy in loads[2:]:
        copy.start()

    lane_c = lane_iota((rpd, 128))

    def chunk(value, k):
        after = value[:, (cw * (k + 1)) % (cw * n_gy) :][:, 0:128]
        before = value[:, (cw * k - 128) % (cw * n_gy) :][:, 0:128]
        return value[:, cw * k : cw * k + cw], jnp.where(lane_c < 64, after, before)

    def remote(src, dst, ssem, rsem, where):
        return pltpu.make_async_remote_copy(
            src_ref=src, dst_ref=dst, send_sem=ssem, recv_sem=rsem, device_id=where,
            device_id_type=MESH,
        )

    warm_load.wait()
    t_own = warm[...]
    for k in range(n_gy):
        main, edge = chunk(t_own, k)
        tsend[k, :, 0:cw] = main
        tsend[k, :, cw : cw + 128] = edge

    sharp = -4.0 * math.log2(math.e)
    lane = lane_iota((hh, 128))
    loads[0].wait()
    done(r_sem.at[10], 3 * size(level))
    for s in range(hh // SR):
        kw[HALO + SR * s : HALO + SR * s + SR, :] = (
            jnp.full((SR, 128), mark[0, s], jnp.int32).astype(F32) * sharp
        )
    w_own = kw[own_r, :] * (0.125 / sharp)
    grow = gx * hh + row_iota((hh, 128))
    for t in range(nt):
        cols = slice(128 * t, 128 * t + 128)
        gcol = gy * ww + 128 * t + lane
        ss[0, t, own_r, :] = jnp.where(grow >= 1, 1.0 - level[0, :, cols].astype(F32) * w_own, 0.0)
        ss[1, t, own_r, :] = jnp.where(gcol >= 1, 1.0 - level[1, :, cols].astype(F32) * w_own, 0.0)
    for c in range(2):
        for t in range(nt):
            sv[c, t, own_r, :] = 0.4 * sv[c, t, own_r, :]
    lines_of = (8, 8, 7, 7, 8, 7)
    line_at = [nt * sum(lines_of[:f]) for f in range(7)]
    acc_l = jnp.zeros((hh, 128), F32)
    acc_r = jnp.zeros((hh, 128), F32)
    fields = [(ref, c) for ref in (su, sv, ss) for c in range(2)]
    for f in range(FIELDS):
        if f < 6:
            ref, c = fields[f]
            first, last = ref[c, 0, own_r, :], ref[c, nt - 1, own_r, :]
        else:
            first = last = kw[own_r, :]
        here = (lane >= 8 * f) & (lane < 8 * f + 8)
        first = pltpu.roll(first, 8 * f, 1) if f else first
        acc_l = jnp.where(here, first, acc_l)
        acc_r = jnp.where(here, pltpu.roll(last, 8 * f + 8, 1), acc_r)
    pk[0] = acc_l
    pk[1] = acc_r
    side_l = remote(pk.at[0], rk.at[1], s_sem.at[3], r_sem.at[0], (gx, left))
    side_r = remote(pk.at[1], rk.at[0], s_sem.at[4], r_sem.at[0], (gx, right))
    top, end = slice(0, 8), slice(hh - 8, hh)
    corners = [
        (has_u & has_l, remote(pk.at[0, top], ck.at[3], s_sem.at[1], r_sem.at[2], (up, left)), 2),
        (has_u & has_r, remote(pk.at[1, top], ck.at[2], s_sem.at[1], r_sem.at[2], (up, right)), 3),
        (has_d & has_l, remote(pk.at[0, end], ck.at[1], s_sem.at[2], r_sem.at[2], (down, left)), 4),
        (has_d & has_r, remote(pk.at[1, end], ck.at[0], s_sem.at[2], r_sem.at[2], (down, right)), 5),
    ]
    rows_u = remote(rowsend.at[0], rowrecv.at[1], s_sem.at[1], r_sem.at[2], (up, gy))
    rows_d = remote(rowsend.at[1], rowrecv.at[0], s_sem.at[2], r_sem.at[2], (down, gy))
    sends = [(has_l, side_l), (has_r, side_r)] + [(a, b) for a, b, _ in corners]
    sends += [(has_u, rows_u), (has_d, rows_d)]

    def start_if(cond, copy):
        @pl.when(cond)
        def _():
            copy.start()

    def sent_if(cond, copy):
        @pl.when(cond)
        def _():
            copy.wait_send()

    for side, at in ((0, HALO), (1, HALO + hh - 8)):
        for f, (ref, c) in enumerate(fields):
            skip = side if lines_of[f] == 7 else 0
            for t in range(nt):
                to = line_at[f] + lines_of[f] * t
                rowsend[side, to : to + lines_of[f], :] = ref[
                    c, t, at + skip : at + skip + lines_of[f], :
                ]
        rowsend[side, line_at[6] : line_at[6] + 1, :] = kw[at : at + 1, :]
    pl.semaphore_wait(barrier, calls)

    for k in far_first(n_gy, lambda k: k // 2):
        t = partner(gy, k, n_gy)
        remote(tsend.at[t], trecv.at[gy + hb], s_sem.at[0], r_sem.at[3], (gx, t)).start()
    pltpu.make_async_copy(tsend.at[gy], trecv.at[gy + hb], r_sem.at[3]).start()

    for cond, copy in sends[6:8]:
        start_if(cond, copy)
    for cond, copy in sends[0:6]:
        start_if(cond, copy)

    k_i, n_i = row_iota((256, 128)), lane_iota((256, 128))
    pos = (k_i % SEG).astype(F32)
    col = (2 * (n_i % 64)).astype(F32)
    tab = jnp.exp(jnp.abs(pos - col) * (-4.0 / SEG)) + jnp.exp(jnp.abs(pos - col - 1.0) * (-4.0 / SEG))
    tab_s[...] = jnp.where(k_i // SEG == n_i // 64, tab * (1.0 / SEG), 0.0)
    done(r_sem.at[11], 3 * size(store))
    base = store[...] + film[...]
    own3[0, hz] = t_own
    own3[1, hz] = base
    own3[2, hz] = store[...] * t_own + film[...] * bath[...]
    for k in range(n_gy):
        asend[k] = base[:, cw * k : cw * k + cw]
    strip = (nstrip - 2) * 8
    nx[:, :, strip : strip + 8, :] = jnp.zeros((2, ntile, 8, 128), F32)
    bn[:, :, :, 32:40, :] = jnp.zeros((2, 2, ntile, 8, 128), F32)

    for h in (1, 2):
        done_if(n_h == h, r_sem.at[0], h * size(pk.at[0]))

    def unpack(got_l, got_r, targets, rows, lines, outside):
        shape = got_l.shape
        lanes = lane_iota(shape)
        gone = outside | (~has_l & (lanes >= 64)) | (~has_r & (lanes < 64))
        for f in range(FIELDS):
            from_r = pltpu.roll(got_r, 128 - 8 * f, 1) if f else got_r
            from_l = pltpu.roll(got_l, 120 - 8 * f, 1)
            side = jnp.where(lanes < 8, from_r, jnp.where(lanes >= 120, from_l, 0.0))
            side = jnp.where(gone, 0.0, side)
            if f < 6:
                ref, c = targets[f]
                ref[c, nt, rows, :] = side
            else:
                kh[lines, :] = side

    unpack(rk[0], rk[1], fields, own_r, own_r, False)
    rims = [
        [(ref.at[side], c) for ref in (bu, bv, bs) for c in range(2)] for side in range(2)
    ]
    for side, (at, to) in enumerate(((8, 8), (frows - 16, 16))):
        for (ref, c), (rim, _) in zip(fields, rims[side]):
            for t in range(ntile):
                rim[c, t, to : to + 8, :] = ref[c, t, at : at + 8, :]

    mid = trecv.at[pl.ds(hb, n_gy)]
    pltpu.make_async_copy(mid, mid, r_sem.at[3]).wait()
    far_u = remote(
        trecv.at[pl.ds(hb, hb)], trecv.at[pl.ds(hb + n_gy, hb)], s_sem.at[1], r_sem.at[12], (up, gy)
    )
    far_d = remote(
        trecv.at[pl.ds(n_gy, hb)], trecv.at[pl.ds(0, hb)], s_sem.at[2], r_sem.at[12], (down, gy)
    )
    start_if(has_u, far_u)
    start_if(has_d, far_d)

    for k in range(1, n_gy):
        t = partner(gy, k, n_gy)
        remote(asend.at[t], arecv.at[gy], s_sem.at[0], r_sem.at[4], (gx, t)).start()
    pltpu.make_async_copy(asend.at[gy], arecv.at[gy], r_sem.at[4]).start()
    mine = own3.at[:, hz]
    swaps = []
    for d in range(1, hz + 1):
        for i, to, ok, came in (
            (d - 1, me + d, me + d < ndev, me >= d),
            (hz + d - 1, me - d, me >= d, me + d < ndev),
        ):
            at = hz - d if i < hz else hz + d
            to = lax.rem(to + ndev, ndev)
            copy = remote(mine, own3.at[:, at], s_sem.at[5 + i], r_sem.at[5], (to // n_gy, to % n_gy))
            swaps.append((ok, came, copy))
    for ok, _, copy in swaps:
        start_if(ok, copy)
    lane8 = lane_iota((8, 128))
    first_lane, last_lane = lane8 == 0, lane8 == 127

    def close_edge(rows):
        edge = tcx[nct, rows, :]
        edge = jnp.where(~has_l & last_lane, pltpu.roll(tcx[0, rows, :], 127, 1), edge)
        edge = jnp.where(~has_r & first_lane, pltpu.roll(tcx[nct - 1, rows, :], 1, 1), edge)
        tcx[nct, rows, :] = edge

    for k in range(hb, hb + n_gy):
        for j in range(nct + 1):
            tcx[j, rpd * k : rpd * k + rpd, :] = trecv[k, :, 128 * j : 128 * j + 128]
    for c in range(8, 8 + ch, 8):
        close_edge(slice(c, c + 8))
    half = lane8 // 2
    step = jnp.where(lane8 % 2 == 0, -1, 1)
    lo_g, lo_h = half, jnp.maximum(half + step, 0)
    hi_g, hi_h = half + 64, jnp.minimum(half + 64 + step, 127)
    ed_g = jnp.where(lane8 < 64, half, half + 64)
    ed_h = jnp.minimum(jnp.maximum(ed_g + step, 0), 127)

    def before(tiles):
        turned = [pltpu.roll(x, 1, 1) for x in tiles]
        return [jnp.where(first_lane, turned[t - 1], turned[t]) for t in range(len(tiles))]

    def after(tiles):
        turned = [pltpu.roll(x, 127, 1) for x in tiles]
        n = len(tiles)
        return [jnp.where(last_lane, turned[(t + 1) % n], turned[t]) for t in range(n)]

    def above(ref, s):
        return ref[8 * s - 1 : 8 * s + 7, :] if s else pltpu.roll(ref[0:8, :], 1, 0)

    def heat_x(s):
        rows = slice(8 * s, 8 * s + 8)
        for t in range(ntile):
            tx[t, rows, :] = 0.3 * (fine[t, rows, :] + above(fine.at[t], s))

    def prolong(p):
        c = 8 * p + 4
        for j in range(nct + 1):
            here = 0.75 * tcx[j, c : c + 8, :]
            widebuf[j, pl.ds(16 * p, 8, stride=2), :] = here + 0.25 * tcx[j, c - 1 : c + 7, :]
            widebuf[j, pl.ds(16 * p + 1, 8, stride=2), :] = here + 0.25 * tcx[j, c + 1 : c + 9, :]
        for s in (2 * p, 2 * p + 1):
            rows = slice(8 * s, 8 * s + 8)
            r = [widebuf[j, rows, :] for j in range(nct + 1)]
            fwd = [pltpu.roll(x, 1, 1) for x in r]
            bwd = [pltpu.roll(x, 127, 1) for x in r]
            f = []
            for j in range(nct):
                f.append(
                    0.75 * pick(r[j], lo_g)
                    + 0.25 * jnp.where(first_lane, fwd[j - 1], pick(r[j], lo_h))
                )
                f.append(
                    0.75 * pick(r[j], hi_g)
                    + 0.25 * jnp.where(last_lane, bwd[j + 1], pick(r[j], hi_h))
                )
            e = pick(r[nct], ed_h)
            e = jnp.where(first_lane, fwd[nct - 1], jnp.where(last_lane, bwd[0], e))
            f.append(0.75 * pick(r[nct], ed_g) + 0.25 * e)
            prev = before(f)
            for t in range(ntile):
                fine[t, rows, :] = f[t]
                ty[t, rows, :] = 0.3 * (f[t] + prev[t])

    npair = nstrip // 2
    for p in range(1, npair - 1):
        prolong(p)
    for s in range(2, nstrip - 2):
        heat_x(s)

    def edges(s):
        rows = slice(8 * s, 8 * s + 8)
        u0 = [su[0, t, rows, :] for t in range(ntile)]
        u1 = [su[1, t, rows, :] for t in range(ntile)]
        k_main, k_side = kw[rows, :], kh[rows, :]
        b0, b1 = before(u0), before(u1)
        ay, ny = [], []
        for t in range(ntile):
            k = k_main if t < nt else k_side
            open_x = u0[t] - above(su.at[0, t], s) - tx[t, rows, :]
            st = jnp.maximum(open_x, 0.0)
            sp = jnp.minimum(ss[0, t, rows, :], jnp.exp2(st * st * k))
            ss[0, t, rows, :] = sp
            nx[0, t, rows, :] = sp * open_x
            nx[1, t, rows, :] = sp * (u1[t] - above(su.at[1, t], s))
            open_y = u1[t] - b1[t] - ty[t, rows, :]
            st = jnp.maximum(open_y, 0.0)
            sp = jnp.minimum(ss[1, t, rows, :], jnp.exp2(st * st * k))
            ss[1, t, rows, :] = sp
            ny.append(sp * open_y)
            ay.append(sp * (u0[t] - b0[t]))
        fy0 = [a - b for a, b in zip(after(ay), ay)]
        fy1 = [a - b for a, b in zip(after(ny), ny)]
        return fy0, fy1

    def advance(s, fy):
        rows = slice(8 * s, 8 * s + 8)
        below = slice(8 * s + 1, 8 * s + 9)
        for c in range(2):
            for t in range(ntile):
                force = (nx[c, t, below, :] - nx[c, t, rows, :]) + fy[c][t]
                v = 0.98 * sv[c, t, rows, :] + 0.16 * force
                sv[c, t, rows, :] = v
                su[c, t, rows, :] = su[c, t, rows, :] + v

    def interior(i, carry):
        for f, (ref, c) in enumerate(fields):
            at = frows - 24 + (f == 4)
            for t in range(ntile):
                past[i, 0, f, t] = ref[c, t, 16:24, :]
                past[i, 1, f, t] = ref[c, t, at : at + 8, :]
        old = None
        for s in range(2, nstrip - 2):
            new = edges(s)
            if old:
                advance(s - 1, old)
            old = new
        advance(nstrip - 3, old)
        for c in range(2):
            for t in range(ntile):
                past_n[i, 0, c, t] = nx[c, t, 17:25, :]
                past_n[i, 1, c, t] = nx[c, t, frows - 24 : frows - 16, :]
        return carry

    lax.fori_loop(0, SUBSTEPS, interior, 0)

    far_size = hb * size(trecv.at[0])
    for v in (1, 2):
        for h in (1, 2):
            done_if(
                (n_v == v) & (n_h == h),
                r_sem.at[2],
                v * (size(rowsend.at[0]) + h * size(ck.at[0])),
            )
    for side, (here, at, to) in enumerate(((has_u, 0, 0), (has_d, hh + HALO, 24))):
        rows = slice(to, to + 8)
        lines = slice(at, at + 8)
        for f, (rim, c) in enumerate(rims[side]):
            first = to if side or lines_of[f] == 8 else to + 1
            for t in range(nt):
                line = line_at[f] + lines_of[f] * t
                got = rowrecv[side, line : line + lines_of[f], :]
                rim[c, t, first : first + lines_of[f], :] = jnp.where(here, got, 0.0)
        got = jnp.broadcast_to(rowrecv[side, line_at[6] : line_at[6] + 1, :], (8, 128))
        kw[lines, :] = jnp.where(here, got, 0.0)
        unpack(ck[2 * side], ck[2 * side + 1], rims[side], rows, lines, ~here)
    for v in (1, 2):
        done_if(n_v == v, r_sem.at[12], v * far_size)
    for side, (here, at, slot, line) in enumerate(
        ((has_u, 0, 0, 8), (has_d, ch + 8, hb + n_gy, ch + 7))
    ):

        @pl.when(here)
        def _():
            for k in range(hb):
                for j in range(nct + 1):
                    tcx[j, at + rpd * k : at + rpd * k + rpd, :] = trecv[
                        slot + k, :, 128 * j : 128 * j + 128
                    ]
            close_edge(slice(at, at + 8))

        @pl.when(jnp.logical_not(here))
        def _():
            for j in range(nct + 1):
                tcx[j, at : at + 8, :] = jnp.broadcast_to(tcx[j, line : line + 1, :], (8, 128))

    prolong(0)
    prolong(npair - 1)
    for s in (0, 1, 2, nstrip - 2, nstrip - 1):
        heat_x(s)

    for t in range(ntile):
        bs[1, 0, t, 8:9, :] = ss[0, t, frows - 24 : frows - 23, :]

    def rim_edges(side, x, y):
        shift_by = (frows - 32) * side
        u, spring, flow = bu.at[side], bs.at[side], bn.at[side]
        ex, ex_up, ey = pl.ds(x, 8), pl.ds(x - 1, 8), pl.ds(y, 8)
        gx_rows, gy_rows = pl.ds(x + shift_by, 8), pl.ds(y + shift_by, 8)
        u0 = [u[0, t, ey, :] for t in range(ntile)]
        u1 = [u[1, t, ey, :] for t in range(ntile)]
        b0, b1 = before(u0), before(u1)
        kx = [kw[gx_rows, :], kh[gx_rows, :]]
        ky = [kw[gy_rows, :], kh[gy_rows, :]]
        ay, ny = [], []
        for t in range(ntile):
            open_x = u[0, t, ex, :] - u[0, t, ex_up, :] - tx[t, gx_rows, :]
            st = jnp.maximum(open_x, 0.0)
            sp = jnp.minimum(spring[0, t, ex, :], jnp.exp2(st * st * kx[t // nt]))
            spring[0, t, ex, :] = sp
            flow[0, t, ex, :] = sp * open_x
            flow[1, t, ex, :] = sp * (u[1, t, ex, :] - u[1, t, ex_up, :])
            open_y = u1[t] - b1[t] - ty[t, gy_rows, :]
            st = jnp.maximum(open_y, 0.0)
            sp = jnp.minimum(spring[1, t, ey, :], jnp.exp2(st * st * ky[t // nt]))
            spring[1, t, ey, :] = sp
            ny.append(sp * open_y)
            ay.append(sp * (u0[t] - b0[t]))
        fy0 = [a - b for a, b in zip(after(ay), ay)]
        fy1 = [a - b for a, b in zip(after(ny), ny)]
        return fy0, fy1

    def rim_advance(side, y, fy):
        rows, below = pl.ds(y, 8), pl.ds(y + 1, 8)
        for c in range(2):
            for t in range(ntile):
                force = (bn[side, c, t, below, :] - bn[side, c, t, rows, :]) + fy[c][t]
                v = 0.98 * bv[side, c, t, rows, :] + 0.16 * force
                bv[side, c, t, rows, :] = v
                bu[side, c, t, rows, :] = bu[side, c, t, rows, :] + v

    for i in range(SUBSTEPS):
        for t in range(ntile):
            for f in range(6):
                rim, c = rims[0][f]
                rim[c, t, 16 + i : 17 + i, :] = past[i, 0, f, t, i : i + 1, :]
                rim, c = rims[1][f]
                to = 15 - i + (f == 4)
                rim[c, t, to : to + 1, :] = past[i, 1, f, t, 7 - i : 8 - i, :]
            for c in range(2):
                bn[0, c, t, 17 + i : 18 + i, :] = past_n[i, 0, c, t, i : i + 1, :]
                bn[1, c, t, 15 - i : 16 - i, :] = past_n[i, 1, c, t, 7 - i : 8 - i, :]
        for side, x, y in ((0, i + 1, i + 1), (1, 16 - i, 15 - i)):
            first = rim_edges(side, x, y)
            second = rim_edges(side, x + 8, y + 8)
            rim_advance(side, y, first)
            rim_advance(side, y + 8, second)
    def settle(some):
        for side, at in ((0, 8), (1, frows - 24)):
            for (ref, c), (rim, _) in zip(some(fields), some(rims[side])):
                for t in range(nt):
                    ref[c, t, at : at + 16, :] = rim[c, t, 8:24, :]

    settle(lambda x: x[4:6])
    for t in range(nt):
        gcol = gy * ww + 128 * t + lane
        dam_x = jnp.where(grow >= 1, 1.0 - ss[0, t, own_r, :], 0.0)
        dam_y = jnp.where(gcol >= 1, 1.0 - ss[1, t, own_r, :], 0.0)
        gap[t] = dam_x + dam_y
    rows2 = jnp.concatenate(
        [
            gap[t, pl.ds(0, ch, stride=2), :] + gap[t, pl.ds(1, ch, stride=2), :]
            for t in range(ww // 128)
        ],
        axis=1,
    )
    pairs = ww // 256
    glow = full_dot(
        jnp.concatenate([rows2[:, 256 * t : 256 * t + 256] for t in range(pairs)], axis=0), tab_s[...]
    )
    resist = jnp.concatenate([glow[ch * t : ch * t + ch] for t in range(pairs)], axis=1)
    t_tile = jnp.concatenate([tcx[j, 8 : 8 + ch, :] for j in range(nct)], axis=1)
    cond = (1.0 + 0.5 * t_tile) / (1.0 + resist)
    for j in range(nct):
        cpad[j, 8 : 8 + ch, :] = cond[:, 128 * j : 128 * j + 128]
    erow[0] = cond[0:1, :]
    erow[1] = cond[ch - 1 : ch, :]
    first_col, last_col = cond[0:8, 0:128], pltpu.roll(cond[0:8, cw - 128 : cw], 1, 1)
    for i in range(1, ch // 8):
        rows = slice(8 * i, 8 * i + 8)
        here = lane8 == i
        first_col = jnp.where(here, pltpu.roll(cond[rows, 0:128], i, 1), first_col)
        last_col = jnp.where(here, pltpu.roll(cond[rows, cw - 128 : cw], i + 1, 1), last_col)
    ecol[0] = first_col
    ecol[1] = last_col
    beside = [
        (has_u, has_d, remote(erow.at[0], grow_c.at[1], s_sem.at[1], r_sem.at[6], (up, gy))),
        (has_d, has_u, remote(erow.at[1], grow_c.at[0], s_sem.at[2], r_sem.at[6], (down, gy))),
        (has_l, has_r, remote(ecol.at[0], gcol_c.at[1], s_sem.at[3], r_sem.at[6], (gx, left))),
        (has_r, has_l, remote(ecol.at[1], gcol_c.at[0], s_sem.at[4], r_sem.at[6], (gx, right))),
    ]
    for ok, _, copy in beside:
        start_if(ok, copy)
    for b in range(n_gy):
        cb4[b] = cond[rpd * b : rpd * b + rpd, :]
    my_cols = pl.ds(pl.multiple_of(gy * cw, 128), cw)
    to_owner = []
    for t in range(n_gy):
        lo, hi = max(0, t - hz), min(n_gy, t + hz + 1)
        src = cb4.at[pl.ds(lo, hi - lo)]
        dst = owc.at[pl.ds(lo - t + hz, hi - lo), :, my_cols]
        to_owner.append((gy != t, remote(src, dst, s_sem.at[0], r_sem.at[7], (gx, t))))
        here = pltpu.make_async_copy(src, dst, r_sem.at[7])

        @pl.when(gy == t)
        def _():
            here.start()

    for t in range(hz):
        n = hz - t
        src, dst = cb4.at[pl.ds(n_gy - n, n)], owc.at[pl.ds(0, n), :, my_cols]
        to_owner.append((has_d, remote(src, dst, s_sem.at[2], r_sem.at[7], (down, t))))
        src, dst = cb4.at[pl.ds(0, n)], owc.at[pl.ds(2 * hz + 1 - n, n), :, my_cols]
        to_owner.append((has_u, remote(src, dst, s_sem.at[1], r_sem.at[7], (up, n_gy - 1 - t))))
    for ok, copy in to_owner:
        start_if(ok, copy)

    settle(lambda x: x[0:4])
    for c in range(2):
        for t in range(nt):
            o_speed[c, t] = 2.5 * sv[c, t, own_r, :]
    for t in range(nt):
        gcol = gy * ww + 128 * t + lane
        dam_x = jnp.where(grow >= 1, 1.0 - ss[0, t, own_r, :], 0.0)
        dam_y = jnp.where(gcol >= 1, 1.0 - ss[1, t, own_r, :], 0.0)
        o_dam[0, t] = dam_x.astype(jnp.bfloat16)
        o_dam[1, t] = dam_y.astype(jnp.bfloat16)

    pltpu.make_async_copy(arecv, arecv, r_sem.at[4]).wait()
    for k in range(n_gy):
        for j in range(nct):
            base_t[j, rpd * k : rpd * k + rpd, :] = arecv[k, :, 128 * j : 128 * j + 128]
    for v in (1, 2):
        for h in (1, 2):
            done_if(
                (n_v == v) & (n_h == h),
                r_sem.at[6],
                v * size(erow.at[0]) + h * size(ecol.at[0]),
            )
    for j in range(nct):
        cols = slice(128 * j, 128 * j + 128)
        cpad[j, 7:8, :] = jnp.where(has_u, grow_c[0, :, cols], 0.0)
        cpad[j, 8 + ch : 9 + ch, :] = jnp.where(has_d, grow_c[1, :, cols], 0.0)
    from_l, from_r = gcol_c[0], gcol_c[1]
    sub8 = row_iota((8, 128))
    peak = None
    for i in range(ch // 8):
        r0 = 8 + 8 * i
        mid = [cpad[j, r0 : r0 + 8, :] for j in range(nct)]
        fwd = [pltpu.roll(x, 1, 1) for x in mid]
        bwd = [pltpu.roll(x, 127, 1) for x in mid]
        fwd_in = [pltpu.roll(from_l, 128 - i, 1) if i else from_l] + fwd[:-1]
        bwd_in = bwd[1:] + [pltpu.roll(from_r, 127 - i, 1)]
        for j in range(nct):
            c = mid[j]
            f_u = c + cpad[j, r0 - 1 : r0 + 7, :]
            f_d = c + cpad[j, r0 + 1 : r0 + 9, :]
            f_l = c + jnp.where(first_lane, fwd_in[j], fwd[j])
            f_r = c + jnp.where(last_lane, bwd_in[j], bwd[j])
            if i == 0:
                f_u = jnp.where(~has_u & (sub8 == 0), 0.0, f_u)
            if i == ch // 8 - 1:
                f_d = jnp.where(~has_d & (sub8 == 7), 0.0, f_d)
            if j == 0:
                f_l = jnp.where(~has_l & first_lane, 0.0, f_l)
            if j == nct - 1:
                f_r = jnp.where(~has_r & last_lane, 0.0, f_r)
            off = 0.5 * ((f_u + f_d) + (f_l + f_r))
            ratio = off / (base_t[j, 8 * i : 8 * i + 8, :] + off)
            peak = ratio if peak is None else jnp.maximum(peak, ratio)
    msend[...] = jnp.full((1, 128), jnp.max(peak), F32)

    for k in far_first(ndev, lambda k: k % n_gy // 2 + (k // n_gy).bit_count()):
        t = partner(me, k, ndev)
        remote(
            msend, mrecv.at[k - 1], s_sem.at[0], r_sem.at[8], (t // n_gy, t % n_gy)
        ).start()

    orows = 16
    n_swap = sum(jnp.where(came, 1, 0) for _, came, _ in swaps)
    for n in range(1, 2 * hz + 1):
        done_if(n_swap == n, r_sem.at[5], n * size(mine))
    reach = hz * rpd

    def gather(q, ref, fill):
        for b in range(2 * hz + 1):
            value = ref[b]
            if b != hz:
                there = me >= hz - b if b < hz else me + (b - hz) < ndev
                value = jnp.where(there, value, fill)
            field[q, rpd * b : rpd * b + rpd, :] = value

    for q in range(3):
        gather(q, own3.at[q], 1.0)
    rest = (2 * hz + 1) * rpd
    for q in range(4):
        field[q, rest:orows, :] = jnp.full((orows - rest, span), 0.0 if q == 3 else 1.0, F32)

    short_t = jnp.where(gx == 0, jnp.maximum(hz - gy, 0), 0)
    short_b = jnp.where(gx == n_gx - 1, jnp.maximum(hz - (n_gy - 1 - gy), 0), 0)
    for a in range(hz + 1):
        for b in range(hz + 1):
            got = owc.at[pl.ds(a, 2 * hz + 1 - a - b)]

            @pl.when((short_t == a) & (short_b == b))
            def _():
                pltpu.make_async_copy(got, got, r_sem.at[7]).wait()

    gather(3, owc, 0.0)
    oshape = (orows, span)
    row_g = me * rpd - reach + row_iota(oshape)
    col_g = lane_iota(oshape)
    total_rows = ndev * rpd

    def four(x):
        return (
            pltpu.roll(x, 1, 0),
            pltpu.roll(x, orows - 1, 0),
            pltpu.roll(x, 1, 1),
            pltpu.roll(x, span - 1, 1),
        )

    inside = (row_g >= 0) & (row_g < total_rows)
    masks = (
        inside & (row_g >= 1),
        inside & (row_g <= total_rows - 2),
        col_g >= 1,
        col_g <= span - 2,
    )
    cond = field[3]
    faces = [jnp.where(m, 0.5 * (cond + nb), 0.0) for m, nb in zip(masks, four(cond))]
    diagonal = field[1] + (faces[0] + faces[1] + faces[2] + faces[3])
    inv = 1.0 / diagonal
    t_all = field[0]
    near = sum(f * nb for f, nb in zip(faces, four(t_all)))
    z = (field[2] - (diagonal * t_all - near)) * inv
    faces = [f * inv for f in faces]
    for j in range(4):
        if j:
            z = z - sum(f * nb for f, nb in zip(faces, four(z)))
        zown[j] = z[reach : reach + rpd, :]

    pltpu.make_async_copy(mrecv, mrecv, r_sem.at[8]).wait()
    peak = jnp.maximum(jnp.max(mrecv[...], axis=0), msend[...])[0:1, :]
    low, high = 1.0 - peak, 1.0 + peak
    center = 0.5 * (high + low)
    spread = 0.5 * (high - low)
    sigma = center / spread
    rho = 1.0 / sigma
    zero = jnp.zeros_like(center)
    e = [zero + 1.0, zero, zero, zero]
    d = [1.0 / center, zero, zero, zero]
    total = list(d)
    for _ in range(3):
        e = [e[0]] + [e[i] - d[i - 1] for i in range(1, 4)]
        rho_next = 1.0 / (2.0 * sigma - rho)
        d = [rho_next * rho * d[i] + (2.0 * rho_next / spread) * e[i] for i in range(4)]
        total = [a + b for a, b in zip(total, d)]
        rho = rho_next
    for t in range(span // 128):
        cols = slice(128 * t, 128 * t + 128)
        x = warm[:, cols]
        for j in range(4):
            x = x + total[j] * zown[j, :, cols]
        o_warm[:, cols] = x

    for ok, _, copy in swaps:
        sent_if(ok, copy)
    always = (n_gy - 1) * (size(tsend.at[0]) + size(asend.at[0])) + (ndev - 1)
    blocks = [min(n_gy, t + hz + 1) - max(0, t - hz) for t in range(n_gy)]
    one = size(cb4.at[0])
    for t in range(n_gy):
        done_if(gy == t, s_sem.at[0], always + one * (sum(blocks) - blocks[t]))
    tall = size(rowsend.at[0]) + far_size + size(erow.at[0]) + one * (hz * (hz + 1) // 2)
    for i, ok in ((1, has_u), (2, has_d)):
        for h in (1, 2):
            done_if(ok & (n_h == h), s_sem.at[i], tall + h * size(ck.at[0]))
    for i, ok in ((3, has_l), (4, has_r)):
        done_if(ok, s_sem.at[i], size(pk.at[0]) + size(ecol.at[0]))


def put_out(su, speed, dam, warm, o_shift, o_speed, o_dam, o_warm, sem):
    nt, hh = dam.shape[1:3]
    for t in range(nt):
        cols = slice(128 * t, 128 * t + 128)
        for i, (src, dst) in enumerate(
            (
                (su.at[:, t, HALO : HALO + hh, :], o_shift.at[:, :, cols]),
                (speed.at[:, t], o_speed.at[:, :, cols]),
                (dam.at[:, t], o_dam.at[:, :, cols]),
            )
        ):
            pltpu.make_async_copy(src, dst, sem.at[i]).start()
    last = pltpu.make_async_copy(warm, o_warm, sem.at[3])
    last.start()
    for i, dst in enumerate((o_shift, o_speed, o_dam)):
        pltpu.make_async_copy(dst, dst, sem.at[i]).wait()
    last.wait()


def per_device(n_gx, n_gy, shift, speed, level, mark, warm, store, film, bath):
    _, hh, ww = shift.shape
    rpd, _ = warm.shape
    cw, ch = ww // 2, hh // 2
    wide = cw + 128
    nt, nct = ww // 128, cw // 128
    ntile = nt + 1
    crows, frows = ch + 16, hh + 2 * HALO
    nsl = n_gy + 2 * (HALO // rpd)
    hz = HALO // 2 // rpd
    vm = lambda *s: pltpu.VMEM(s, F32)
    dma = lambda n: pltpu.SemaphoreType.DMA((n,))
    hbm = pl.BlockSpec(memory_space=pltpu.HBM)
    vmem = pl.BlockSpec(memory_space=pltpu.VMEM)
    outs = pl.pallas_call(
        functools.partial(kernel, n_gx, n_gy),
        out_shape=(
            vm(2, ntile, frows, 128),
            vm(2, nt, hh, 128),
            pltpu.VMEM((2, nt, hh, 128), jnp.bfloat16),
            vm(*warm.shape),
        ),
        in_specs=[hbm] * 8,
        out_specs=(vmem,) * 4,
        scratch_shapes=[
            vm(n_gy, rpd, wide),
            vm(nsl, rpd, wide),
            vm(n_gy, rpd, cw),
            vm(n_gy, rpd, cw),
            vm(2, hh, 128),
            vm(2, hh, 128),
            vm(4, 8, 128),
            vm(2, 45 * nt + 1, 128),
            vm(2, 45 * nt + 1, 128),
            vm(2, 2, ntile, 32, 128),
            vm(2, 2, ntile, 32, 128),
            vm(2, 2, ntile, 32, 128),
            vm(2, 2, ntile, 40, 128),
            vm(SUBSTEPS, 2, 6, ntile, 8, 128),
            vm(SUBSTEPS, 2, 2, ntile, 8, 128),
            pltpu.VMEM(level.shape, level.dtype),
            vm(*warm.shape),
            vm(*warm.shape),
            vm(*warm.shape),
            vm(*warm.shape),
            vm(2, ntile, frows, 128),
            vm(2, ntile, frows, 128),
            vm(frows, 128),
            vm(frows, 128),
            vm(ntile, frows, 128),
            vm(ntile, frows, 128),
            vm(ntile, frows, 128),
            vm(2, ntile, frows + 8, 128),
            vm(nct + 1, crows, 128),
            vm(nct + 1, frows, 128),
            vm(256, 128),
            vm(nt, hh, 128),
            vm(nct, ch, 128),
            vm(nct, crows, 128),
            vm(2, 1, cw),
            vm(2, 1, cw),
            vm(2, 8, 128),
            vm(2, 8, 128),
            vm(n_gy, rpd, cw),
            vm(2 * hz + 1, rpd, cw * n_gy),
            vm(3, 2 * hz + 1, rpd, cw * n_gy),
            vm(4, 16, cw * n_gy),
            vm(4, rpd, cw * n_gy),
            vm(1, 128),
            vm(n_gx * n_gy - 1, 1, 128),
            dma(5 + 2 * hz),
            dma(13),
            vm(3 * level.size // 128, 1, 128),
            pltpu.SMEM((1, hh // SR), mark.dtype),
        ],
        compiler_params=pltpu.CompilerParams(
            collective_id=0, has_side_effects=True
        ),
    )(shift, speed, level, mark.reshape(1, hh // SR), warm, store, film, bath)
    return pl.pallas_call(
        put_out,
        out_shape=tuple(
            jax.ShapeDtypeStruct(o.shape, d)
            for o, d in ((shift, F32), (speed, F32), (level, jnp.bfloat16), (warm, F32))
        ),
        in_specs=[vmem] * 4,
        out_specs=(hbm,) * 4,
        scratch_shapes=[dma(4)],
    )(*(pltpu.with_memory_space_constraint(o, pltpu.VMEM) for o in outs))


def solution(mesh):
    rows = P(("gx", "gy"), None)
    plate = P(None, "gx", "gy")
    return jax.shard_map(
        functools.partial(per_device, mesh.shape["gx"], mesh.shape["gy"]),
        mesh=mesh,
        in_specs=(plate, plate, plate, P("gx", "gy"), rows, rows, rows, rows),
        out_specs=(plate, plate, plate, rows),
        check_vma=False,
    )
```
